128 devices in a mesh: chan: 8 (over y_lo, x), pos: 16 (over y_hi, z, core).
Axes of the slice: x: 4, y: 4 (y_hi: 2, y_lo: 2; y = y_hi * 2 + y_lo), z: 4, core: 2. Of those that a mesh axis runs over, the one named last changes fastest.
Arguments:
- state: float32 [8, 8, 50, 16384], P('chan', None, None, 'pos'), may hold values from -6 to 6
- courant: float32 [8, 50, 16384], P('chan', None, 'pos'), may hold values from 0.6 to 0.95
- level_mix: float32 [50, 50], replicated, may hold values from -0.875 to 0.875
- field_mix: float32 [8, 8], replicated, may hold values from -2 to 2
- send_list: int32 [2, 8, 16, 4], P(None, 'chan', 'pos'), may hold values from 0 to 7, as said below
- send_count: int32 [2, 8, 16], P(None, 'chan', 'pos'), may hold values from 0 to 4, as said below
Outputs:
- advanced: float32 [8, 8, 50, 16384], P('chan', None, None, 'pos')
The draws below stay inside these ranges and needn't reach their ends.
Inputs may be any that keep to these rules, and one draw needn't show every extreme that they name: `send_list`: each device's row of a cycle holds 4 distinct local segment numbers; only the first send_count of them are used. `send_count`: in each cycle the counts of two devices at the same pos whose chan indices differ by half the chan axis sum to at most 4; in every cycle some device has 4.
All inputs are finite; a program needn't handle non-finite values.
Results may differ from the reference program's by a relative error of at most 0.0003.
Values sent between devices are 32-bit elements; how exact they have to be, the bound alone decides.
No kernel may reach another device: no remote copies, remote signals or barrier semaphores. Data moves between devices by JAX's collectives and lax.ppermute only.
A program may use at most 128 MiB of HBM per device.

```python
import jax
import jax.numpy as jnp
from jax import lax

FIELDS = 8
LEVELS = 50
CELLS = 128
CH_DEV = 1
SEG_DEV = 8
SECTIONS = 12
SWEEPS = 4
CYCLES = 2
CAP = 4
CHANNELS = 8
POSITIONS = 16384
N_CHAN = 8
N_POS = 16


def draw_send_count(key, part):
    base = jax.random.fold_in(key, 7)
    keys = jax.random.split(base, 4)
    half_chan = N_CHAN // 2
    pairs = half_chan * N_POS
    totals = jax.random.randint(keys[0], (CYCLES, pairs), 0, CAP + 1)
    shares = jax.random.randint(keys[1], (CYCLES, pairs), 0, totals + 1)
    force_low = jax.random.randint(keys[2], (CYCLES, 1), 0, pairs)
    force_high = (force_low + 1 + jax.random.randint(keys[3], (CYCLES, 1), 0, pairs - 1)) % pairs
    indices = jnp.arange(pairs)[None, :]
    forced = (indices == force_low) | (indices == force_high)
    totals = jnp.where(forced, CAP, totals)
    shares = jnp.where(indices == force_low, CAP, jnp.where(indices == force_high, 0, shares))
    lower_counts = shares.reshape(CYCLES, half_chan, N_POS)
    upper_counts = (totals - shares).reshape(CYCLES, half_chan, N_POS)
    return jnp.concatenate([lower_counts, upper_counts], axis=1).astype(jnp.int32)


def draw_send_list(key, part):
    base = jax.random.fold_in(key, 11)
    keys = jax.random.split(base, CYCLES * N_CHAN * N_POS)
    rows = jax.vmap(lambda single_key: jax.random.permutation(single_key, CH_DEV * SEG_DEV)[:CAP])(keys)
    return rows.reshape(CYCLES, N_CHAN, N_POS, CAP).astype(jnp.int32)


def levels(key, shape, shards, low, top_value):
    def one(position, shards_of):
        draws = jax.random.uniform(jax.random.fold_in(jax.random.fold_in(key, 6), position), (shards_of,), jnp.float32, low / len(shards), top_value / len(shards))
        return jnp.repeat(jnp.exp(draws), shape[position] // shards_of).reshape((-1,) + (1,) * (len(shape) - position - 1))

    gain = one(*shards[0])
    for cut in shards[1:]:
        gain = gain * one(*cut)
    return gain


def noise(key, extent, spread, limit, cuts=(), kind=jnp.bfloat16):
    drawn = jax.random.normal(key, extent, jnp.float32) * spread
    if len(cuts) > 0:
        drawn = levels(key, extent, cuts, -0.22, 0.18) * drawn
    return jnp.clip(drawn, min=-limit, max=limit).astype(kind)


def setup_inputs(seed: int = 0) -> dict:
    streams_of = jax.random.split(jax.random.key(seed), 7)
    state = noise(streams_of[0], (CHANNELS, FIELDS, LEVELS, POSITIONS), 1.0, 6.0, ((0, 8), (3, 16)), jnp.float32)
    courant = jnp.clip(0.6 + 0.34999996 * jax.random.uniform(streams_of[1], (CHANNELS, LEVELS, POSITIONS), jnp.float32) ** levels(streams_of[1], (CHANNELS, LEVELS, POSITIONS), ((0, 8), (2, 16)), -0.2, 0.2), 0.6, 0.95)
    level_mix = noise(streams_of[2], (LEVELS, LEVELS), LEVELS ** -0.5, 0.875, (), jnp.float32)
    field_mix = noise(streams_of[3], (FIELDS, FIELDS), FIELDS ** -0.5, 2.0, (), jnp.float32)
    send_list = draw_send_list(jax.random.fold_in(streams_of[6], 71), 0)
    send_count = draw_send_count(jax.random.fold_in(streams_of[6], 71), 0)
    return {"state": state, "courant": courant, "level_mix": level_mix, "field_mix": field_mix, "send_list": send_list, "send_count": send_count}


buoyancy = 0.4


def column_physics(segments, level_mix, field_mix):
    for sweep_index in range(SWEEPS):
        bent_values = jnp.tanh(segments)
        vertical = jnp.einsum('lm,...fmx->...flx', level_mix, bent_values, precision=lax.Precision.HIGHEST)
        across = jnp.einsum('fg,...glx->...flx', field_mix, bent_values, precision=lax.Precision.HIGHEST)
        segments = segments + vertical + across
    return segments


def advance(fields, drifts):
    parity = (jnp.arange(fields.shape[1]) % 2 == 0)[None, :, None, None]
    speeds = drifts[:, None]
    rightward = jnp.roll(speeds, 1, -1) * jnp.roll(fields, 1, -1)
    leftward = jnp.roll(speeds, -1, -1) * jnp.roll(fields, -1, -1)
    shifted = (1.0 - speeds) * fields + jnp.where(parity, rightward, leftward)
    lifted = shifted[:, 1] + buoyancy * shifted[:, 2]
    heated = shifted[:, 2] - buoyancy * lifted
    return jnp.concatenate([shifted[:, :1], lifted[:, None], heated[:, None], shifted[:, 3:]], axis=1)


def reference(state, courant, level_mix, field_mix, send_list, send_count):
    fields_now = state
    chan_grid = jnp.arange(N_CHAN, dtype=jnp.int32)[:, None, None]
    pos_grid = jnp.arange(N_POS, dtype=jnp.int32)[None, :, None]
    slot_grid = jnp.arange(CAP, dtype=jnp.int32)[None, None, :]
    for cycle_index in range(CYCLES):
        chosen = send_list[cycle_index]
        chan_of = (chan_grid * CH_DEV + chosen // SEG_DEV).reshape(-1).astype(jnp.int32)
        seg_of = (pos_grid * SEG_DEV + chosen % SEG_DEV).reshape(-1).astype(jnp.int32)
        usable = (slot_grid < send_count[cycle_index][:, :, None]).reshape(-1)

        def apply_one(slot_index, current):
            starts = (chan_of[slot_index], jnp.int32(0), jnp.int32(0), seg_of[slot_index] * CELLS)
            before = lax.dynamic_slice(current, starts, (1, FIELDS, LEVELS, CELLS))
            after = lax.cond(usable[slot_index], lambda segment_block: column_physics(segment_block, level_mix, field_mix), lambda segment_block: segment_block, before)
            return lax.dynamic_update_slice(current, after, starts)

        fields_now = lax.fori_loop(0, chan_of.shape[0], apply_one, fields_now)
        for section_index in range(SECTIONS):
            fields_now = advance(fields_now, courant)
    return fields_now
```

```python
import functools

import jax
import jax.numpy as jnp
from jax import lax
from jax.experimental import pallas as pl
from jax.experimental.pallas import tpu as pltpu
from jax.sharding import PartitionSpec as P

LEVELS = 50
FIELDS = 8
CELLS = 128
SECTIONS = 12
SWEEPS = 4
CYCLES = 2
TILES = 8
ROWS = LEVELS * FIELDS
CROWS = 56
NET = CELLS - 2 * SECTIONS
WINDOWS = 11
FIRST = CELLS - 2 * SECTIONS
BUOYANCY = 0.4
FULL = 6
PAY = 464

F32 = jnp.float32
BF16 = jnp.bfloat16


def iota(shape, dim):
    return lax.broadcasted_iota(jnp.int32, shape, dim)


def level_field(u):
    tail = u - 64 * FULL
    half = tail // 8
    rest = tail % 8
    level = jnp.where(tail < 0, 8 * (u // 64) + u % 8, 8 * FULL + rest // 4)
    field = jnp.where(tail < 0, (u // 8) % 8, 2 * (rest % 4) + half)
    return level, field


def natural_rows(base, level_stride):
    out = []
    for g in range(FULL):
        for f in range(FIELDS):
            out.append(pl.ds(base + 8 * g * level_stride + f, 8, stride=level_stride))
    return out


def build_weights(lm, fm, w_ref):
    split = lambda v: (v.astype(BF16).astype(F32), v - v.astype(BF16).astype(F32))
    dot = functools.partial(jnp.dot, preferred_element_type=F32)
    lv, fv = level_field(iota((ROWS, LEVELS), 0))
    el = (lv == iota((ROWS, LEVELS), 1)).astype(F32).astype(BF16)
    lv, fv = level_field(iota((ROWS, FIELDS), 0))
    ef = (fv == iota((ROWS, FIELDS), 1)).astype(F32).astype(BF16)
    lt, ft = level_field(iota((LEVELS, ROWS), 1))
    elt = (lt == iota((LEVELS, ROWS), 0)).astype(F32).astype(BF16)
    lt, ft = level_field(iota((FIELDS, ROWS), 1))
    eft = (ft == iota((FIELDS, ROWS), 0)).astype(F32).astype(BF16)
    lhi, llo = split(lm)
    fhi, flo = split(fm)
    wl = dot(dot(el, lhi.astype(BF16)).astype(BF16), elt) + dot(
        dot(el, llo.astype(BF16)).astype(BF16), elt
    )
    wf = dot(dot(ef, fhi.astype(BF16)).astype(BF16), eft) + dot(
        dot(ef, flo.astype(BF16)).astype(BF16), eft
    )
    lr, fr = level_field(iota((ROWS, ROWS), 0))
    lc, fc = level_field(iota((ROWS, ROWS), 1))
    w = jnp.where(fr == fc, wl, 0.0) + jnp.where(lr == lc, wf, 0.0)
    whi, wlo = split(w)
    w_ref[...] = jnp.concatenate([whi, whi, wlo], axis=1).astype(BF16)


def physics_pair(s_ref, ja, jb, w_ref, v_ref, r_ref):
    v_ref[:, :CELLS] = s_ref[ja]
    v_ref[:, CELLS:] = s_ref[jb]

    def sweep(_, carry):
        for r in range(0, ROWS, 16):
            t = jnp.tanh(v_ref[r : r + 16, :])
            hi = t.astype(BF16)
            r_ref[r : r + 16, :] = hi
            r_ref[ROWS + r : ROWS + r + 16, :] = (t - hi.astype(F32)).astype(BF16)
            r_ref[2 * ROWS + r : 2 * ROWS + r + 16, :] = hi
        v_ref[...] += jnp.dot(w_ref[...], r_ref[...], preferred_element_type=F32)
        return carry

    lax.fori_loop(0, SWEEPS, sweep, 0)
    s_ref[ja] = v_ref[:, :CELLS]
    s_ref[jb] = v_ref[:, CELLS:]


def coefficients(ct_ref, ja, jb, off, coef_ref, k):
    lane = iota((8, CELLS), 1)
    sub = iota((8, CELLS), 0)
    for g in range(FULL + 1):
        rows = pl.ds(8 * g, 8)
        c = pltpu.roll(
            jnp.where(lane >= off, ct_ref[ja, rows, :], ct_ref[jb, rows, :]), CELLS - off, 1
        )
        p = c
        for sh in (1, 2, 4, 8, 16, 32, 64):
            p = p * jnp.where(lane >= sh, pltpu.roll(p, sh, 1), 1.0)
        mid = jnp.sum(jnp.where(lane == CELLS // 2 - 1, p, 0.0), axis=1, keepdims=True)
        scale = jnp.broadcast_to(1.0 / mid, (8, CELLS))
        ei = p * scale
        d = jnp.where(lane >= 1, pltpu.roll(ei, 1, 1), scale)
        e = 1.0 / ei
        di = 1.0 / d
        k1 = BUOYANCY * (d * ei)
        k2 = BUOYANCY * (e * di)
        if g == FULL:
            k1 = jnp.where(sub % 4 == 0, k1, 0.0)
            k2 = jnp.where(sub % 4 == 1, k2, 0.0)
        for i, value in enumerate((1.0 - c, d, di, ei, e, k1, k2)):
            coef_ref[i, k, rows, :] = value


def window(src_ref, ja, jb, off, coef_ref, k, dst_ref, da, db, split=((0, 1, 2, 6), (3, 4, 5))):
    lane = iota((8, CELLS), 1)
    take = lane >= off
    keep_a = (lane >= off + SECTIONS) & (lane < off + CELLS - SECTIONS)
    keep_b = (lane < off - SECTIONS) & (lane >= off + SECTIONS - CELLS)

    def load(row):
        rows = pl.ds(row, 8)
        return pltpu.roll(
            jnp.where(take, src_ref[ja, rows, :], src_ref[jb, rows, :]), CELLS - off, 1
        )

    def store(row, value):
        back = pltpu.roll(value, off, 1)
        rows = pl.ds(row, 8)
        pltpu.store(dst_ref.at[da, rows, :], back, mask=keep_a)
        pltpu.store(dst_ref.at[db, rows, :], back, mask=keep_b)

    for groups in split:
        cf = {g: [coef_ref[i, k, pl.ds(8 * g, 8), :] for i in (0, 5, 6)] for g in groups}
        q = {}
        for g in groups:
            di = coef_ref[2, k, pl.ds(8 * g, 8), :]
            ei = coef_ref[3, k, pl.ds(8 * g, 8), :]
            if g < FULL:
                q[g] = [load(64 * g + 8 * f) * (di if f % 2 == 0 else ei) for f in range(FIELDS)]
            else:
                q[g] = [load(64 * g) * di, load(64 * g + 8) * ei]
        for _ in range(SECTIONS):
            for g in groups:
                a, k1, k2 = cf[g]
                x = [
                    a * v + pltpu.roll(v, 1 if f % 2 == 0 else CELLS - 1, 1)
                    for f, v in enumerate(q[g])
                ]
                if g < FULL:
                    x[1] = x[1] + k1 * x[2]
                    x[2] = x[2] - k2 * x[1]
                else:
                    x[1] = x[1] + k1 * pltpu.roll(x[0], 7, 0)
                    x[0] = x[0] - k2 * pltpu.roll(x[1], 1, 0)
                q[g] = x
        for g in groups:
            d = coef_ref[1, k, pl.ds(8 * g, 8), :]
            e = coef_ref[4, k, pl.ds(8 * g, 8), :]
            for f, v in enumerate(q[g]):
                store(64 * g + 8 * f, v * (d if f % 2 == 0 else e))


def place(k):
    start = FIRST + NET * k
    return start // CELLS, start % CELLS


def courant_tile(c_ref, t):
    sub = iota((8, CELLS), 0)
    out = [c_ref[pl.ds(64 * g + t, 8, stride=8), :] for g in range(FULL)]
    a = jnp.broadcast_to(c_ref[pl.ds(64 * FULL + t, 1), :], (8, CELLS))
    b = jnp.broadcast_to(c_ref[pl.ds(64 * FULL + 8 + t, 1), :], (8, CELLS))
    return out + [jnp.where(sub < 4, a, b)]


def pack_kernel(x_ref, c_ref, list_ref, count_ref, first_ref, last_ref, sem):
    copies = []
    for i, (ref, t) in enumerate(((first_ref, 0), (last_ref, TILES - 1))):
        copy = pltpu.make_async_copy(
            x_ref.at[:, pl.ds(8 * t, 8), :], ref.at[pl.ds(0, LEVELS)], sem.at[i]
        )
        copy.start()
        copies.append(copy)
    sub = iota((8, CELLS), 0)
    for ref, t in ((first_ref, 0), (last_ref, TILES - 1)):
        for g, value in enumerate(courant_tile(c_ref, t)):
            ref[LEVELS + g] = value
        flags = []
        for cycle in range(CYCLES):
            hit = jnp.int32(0)
            for slot in range(4):
                named = (slot < count_ref[cycle]) & (list_ref[cycle, slot] == t)
                hit = jnp.where(named, jnp.int32(1), hit)
            flags.append(hit)
        ref[LEVELS + FULL + 1] = jnp.where(sub < 4, flags[0], flags[1]).astype(F32)
    for copy in copies:
        copy.wait()


def inner_kernel(
    x_ref, c_ref, lm_ref, fm_ref, list_ref, count_ref,
    out_ref, edge_ref, coef_ref, w_ref,
    n_ref, s_ref, v_ref, r_ref, ct_ref, sem,
):
    copy = pltpu.make_async_copy(x_ref, n_ref, sem)
    copy.start()
    build_weights(lm_ref[...], fm_ref[...], w_ref)
    for t in range(TILES):
        for g, value in enumerate(courant_tile(c_ref, t)):
            ct_ref[t + 1, pl.ds(8 * g, 8), :] = value

    def coef_body(k, carry):
        j, off = place(k)
        coefficients(ct_ref, j, j + 1, off, coef_ref, k)
        return carry

    lax.fori_loop(1, WINDOWS - 2, coef_body, 0)
    copy.wait()

    def convert(t, carry):
        for i, rows in enumerate(natural_rows(8 * t, 64)):
            s_ref[t + 1, pl.ds(8 * i, 8), :] = n_ref[rows, :]
        for half in range(2):
            lo = n_ref[pl.ds(64 * 8 * FULL + 8 * t + half, 4, stride=2), :]
            hi = n_ref[pl.ds(64 * 8 * FULL + 64 + 8 * t + half, 4, stride=2), :]
            s_ref[t + 1, pl.ds(64 * FULL + 8 * half, 4), :] = lo
            s_ref[t + 1, pl.ds(64 * FULL + 8 * half + 4, 4), :] = hi
        return carry

    lax.fori_loop(0, TILES, convert, 0)
    count = count_ref[0]

    def pair(p, carry):
        ja = list_ref[0, 2 * p] + 1
        jb = list_ref[0, jnp.minimum(2 * p + 1, count - 1)] + 1
        physics_pair(s_ref, ja, jb, w_ref, v_ref, r_ref)
        return carry

    lax.fori_loop(0, (count + 1) // 2, pair, 0)
    edge_ref[0] = s_ref[1]
    edge_ref[1] = s_ref[TILES]

    def window_body(k, carry):
        j, off = place(k)
        window(s_ref, j, j + 1, off, coef_ref, k, out_ref, j, j + 1)
        return carry

    lax.fori_loop(1, WINDOWS - 2, window_body, 0)


def payload_tile(pay_ref, s_ref, j):
    for i, rows in enumerate(natural_rows(0, 8)):
        s_ref[j, pl.ds(8 * i, 8), :] = pay_ref[rows, :]
    for half in range(2):
        s_ref[j, pl.ds(64 * FULL + 8 * half, 8), :] = pay_ref[
            pl.ds(64 * FULL + half, 8, stride=2), :
        ]


def outer_kernel(
    in_ref, edge_ref, coef_in_ref, w_ref, left_ref, right_ref, c_ref, list_ref, count_ref,
    out_ref,
    s_ref, e_ref, d_ref, v_ref, r_ref, ct_ref, coef_ref, n_ref, sem, osem,
):
    copy = pltpu.make_async_copy(in_ref, s_ref.at[pl.ds(0, TILES + 2)], sem.at[0])
    copy.start()
    lane = iota((8, CELLS), 1)
    payload_tile(left_ref, e_ref, 0)
    e_ref[1] = edge_ref[0]
    e_ref[2] = edge_ref[1]
    payload_tile(right_ref, e_ref, 3)
    for g in range(FULL + 1):
        rows = pl.ds(8 * g, 8)
        ct_ref[0, rows, :] = left_ref[pl.ds(ROWS + 8 * g, 8), :]
        ct_ref[3, rows, :] = right_ref[pl.ds(ROWS + 8 * g, 8), :]
    for j, t in ((1, 0), (2, TILES - 1)):
        for g, value in enumerate(courant_tile(c_ref, t)):
            ct_ref[j, pl.ds(8 * g, 8), :] = value
    for k, j in ((0, 0), (WINDOWS - 2, 2), (WINDOWS - 1, 2)):
        coefficients(ct_ref, j, j + 1, place(k)[1], coef_ref, k)

    def body(k, carry):
        coef_ref[:, k] = coef_in_ref[:, k]
        return carry

    lax.fori_loop(1, WINDOWS - 2, body, 0)
    frow = ROWS + 8 * (FULL + 1)
    listed = []
    for cycle in range(CYCLES):
        row = pl.ds(frow + 4 * cycle, 1)
        listed.append((left_ref[row, :], right_ref[row, :]))

    def compose(ref, left, right, to):
        for r in range(0, ROWS, 8):
            rows = pl.ds(r, 8)
            ref[to, rows, :] = jnp.where(lane < CELLS // 2, ref[right, rows, :], ref[left, rows, :])

    def restore(ref, left, right, frm, flags):
        ml = (jnp.broadcast_to(flags[0], (8, CELLS)) > 0.5) & (lane >= CELLS // 2)
        mr = (jnp.broadcast_to(flags[1], (8, CELLS)) > 0.5) & (lane < CELLS // 2)
        for r in range(0, ROWS, 8):
            rows = pl.ds(r, 8)
            done = ref[frm, rows, :]
            ref[left, rows, :] = jnp.where(ml, done, ref[left, rows, :])
            ref[right, rows, :] = jnp.where(mr, done, ref[right, rows, :])

    any_flag = [jnp.max(jnp.maximum(l, r)) > 0.5 for l, r in listed]

    @pl.when(any_flag[0])
    def _():
        compose(e_ref, 0, 3, 4)
        physics_pair(e_ref, 4, 4, w_ref, v_ref, r_ref)
        restore(e_ref, 0, 3, 4, listed[0])

    copy.wait()
    for k, a, b in ((0, 0, 1), (WINDOWS - 2, 2, 3), (WINDOWS - 1, 2, 3)):
        j, off = place(k)
        window(e_ref, a, b, off, coef_ref, k, s_ref, j, j + 1)

    count = count_ref[1]
    total = count + any_flag[1].astype(jnp.int32)
    HALO = TILES + 2

    @pl.when(any_flag[1])
    def _():
        compose(s_ref, 0, TILES + 1, HALO)

    def entry(i):
        i = jnp.minimum(i, total - 1)
        named = list_ref[1, jnp.minimum(i, 3)] + 1
        return jnp.where(i < count, named, HALO)

    def pair(p, carry):
        physics_pair(s_ref, entry(2 * p), entry(2 * p + 1), w_ref, v_ref, r_ref)
        return carry

    lax.fori_loop(0, (total + 1) // 2, pair, 0)

    @pl.when(any_flag[1])
    def _():
        restore(s_ref, 0, TILES + 1, HALO, listed[1])

    def window_body(k, carry):
        j, off = place(k)
        window(s_ref, j, j + 1, off, coef_ref, k, d_ref, j, j + 1)
        return carry

    lax.fori_loop(0, WINDOWS - 1, window_body, 0)

    def convert(t, carry):
        for i, rows in enumerate(natural_rows(8 * t, 64)):
            n_ref[rows, :] = d_ref[t + 1, pl.ds(8 * i, 8), :]
        for half in range(2):
            n_ref[pl.ds(64 * 8 * FULL + 8 * t + half, 4, stride=2), :] = d_ref[
                t + 1, pl.ds(64 * FULL + 8 * half, 4), :
            ]
            n_ref[pl.ds(64 * 8 * FULL + 64 + 8 * t + half, 4, stride=2), :] = d_ref[
                t + 1, pl.ds(64 * FULL + 8 * half + 4, 4), :
            ]
        return carry

    lax.fori_loop(0, TILES, convert, 0)
    pltpu.sync_copy(n_ref, out_ref)


VM = pl.BlockSpec(memory_space=pltpu.VMEM)
SM = pl.BlockSpec(memory_space=pltpu.SMEM)
ANY = pl.BlockSpec(memory_space=pl.ANY)
LIMIT = 40 << 20


def local(state, courant, level_mix, field_mix, send_list, send_count):
    shape = jax.ShapeDtypeStruct
    x = state.reshape(FIELDS, LEVELS, TILES, CELLS).transpose(1, 2, 0, 3)
    c = courant.reshape(LEVELS * TILES, CELLS)
    chosen = send_list.reshape(CYCLES, 4)
    count = send_count.reshape(CYCLES)
    first, last = pl.pallas_call(
        pack_kernel,
        name="pack",
        out_shape=(shape((PAY // 8, 8, CELLS), F32),) * 2,
        in_specs=[ANY, VM, SM, SM],
        out_specs=(VM, VM),
        scratch_shapes=[pltpu.SemaphoreType.DMA((2,))],
        compiler_params=pltpu.CompilerParams(vmem_limit_bytes=8 << 20),
    )(x.reshape(LEVELS, TILES * FIELDS, CELLS), c, chosen, count)
    n = lax.axis_size("pos")
    left = lax.ppermute(last, "pos", [(i, (i + 1) % n) for i in range(n)])
    right = lax.ppermute(first, "pos", [((i + 1) % n, i) for i in range(n)])
    mid, edge, coef, w = pl.pallas_call(
        inner_kernel,
        name="inner",
        out_shape=(
            shape((TILES + 2, ROWS, CELLS), F32),
            shape((2, ROWS, CELLS), F32),
            shape((7, WINDOWS, CROWS, CELLS), F32),
            shape((ROWS, 3 * ROWS), BF16),
        ),
        in_specs=[ANY, VM, VM, VM, SM, SM],
        out_specs=(VM,) * 4,
        scratch_shapes=[
            pltpu.VMEM((LEVELS * 64, CELLS), F32),
            pltpu.VMEM((TILES + 2, ROWS, CELLS), F32),
            pltpu.VMEM((ROWS, 2 * CELLS), F32),
            pltpu.VMEM((3 * ROWS, 2 * CELLS), BF16),
            pltpu.VMEM((TILES + 2, CROWS, CELLS), F32),
            pltpu.SemaphoreType.DMA,
        ],
        compiler_params=pltpu.CompilerParams(vmem_limit_bytes=LIMIT),
        cost_estimate=pl.CostEstimate(flops=4_000_000_000, bytes_accessed=8_000_000, transcendentals=0),
    )(x.reshape(LEVELS * 64, CELLS), c, level_mix, field_mix, chosen, count)
    out = pl.pallas_call(
        outer_kernel,
        name="outer",
        out_shape=shape((LEVELS * 64, CELLS), F32),
        in_specs=[ANY, VM, VM, VM, VM, VM, VM, SM, SM],
        out_specs=ANY,
        scratch_shapes=[
            pltpu.VMEM((TILES + 3, ROWS, CELLS), F32),
            pltpu.VMEM((5, ROWS, CELLS), F32),
            pltpu.VMEM((TILES + 2, ROWS, CELLS), F32),
            pltpu.VMEM((ROWS, 2 * CELLS), F32),
            pltpu.VMEM((3 * ROWS, 2 * CELLS), BF16),
            pltpu.VMEM((4, CROWS, CELLS), F32),
            pltpu.VMEM((7, WINDOWS, CROWS, CELLS), F32),
            pltpu.VMEM((LEVELS * 64, CELLS), F32),
            pltpu.SemaphoreType.DMA((1,)),
            pltpu.SemaphoreType.DMA((1,)),
        ],
        compiler_params=pltpu.CompilerParams(vmem_limit_bytes=LIMIT),
    )(mid, edge, coef, w, left.reshape(PAY, CELLS), right.reshape(PAY, CELLS), c, chosen, count)
    out = out.reshape(LEVELS, TILES, FIELDS, CELLS).transpose(2, 0, 1, 3)
    return out.reshape(1, FIELDS, LEVELS, TILES * CELLS)


def solution(mesh):
    in_specs = (
        P("chan", None, None, "pos"),
        P("chan", None, "pos"),
        P(),
        P(),
        P(None, "chan", "pos", None),
        P(None, "chan", "pos"),
    )
    out_specs = P("chan", None, None, "pos")
    return jax.shard_map(local, mesh=mesh, in_specs=in_specs, out_specs=out_specs, check_vma=False)
```

```python
import functools

import jax
import jax.numpy as jnp
from jax import lax
from jax.experimental import pallas as pl
from jax.experimental.pallas import tpu as pltpu
from jax.sharding import PartitionSpec as P

LEVELS = 50
FIELDS = 8
CELLS = 128
SECTIONS = 12
SWEEPS = 4
CYCLES = 2
TILES = 8
ROWS = LEVELS * FIELDS
CROWS = 56
NET = CELLS - 2 * SECTIONS
WINDOWS = 11
FIRST = CELLS - 2 * SECTIONS
BUOYANCY = 0.4
FULL = 6
PAY = 464

F32 = jnp.float32
BF16 = jnp.bfloat16


def iota(shape, dim):
    return lax.broadcasted_iota(jnp.int32, shape, dim)


def level_field(u):
    tail = u - 64 * FULL
    half = tail // 8
    rest = tail % 8
    level = jnp.where(tail < 0, 8 * (u // 64) + u % 8, 8 * FULL + rest // 4)
    field = jnp.where(tail < 0, (u // 8) % 8, 2 * (rest % 4) + half)
    return level, field


def natural_rows(base, level_stride):
    out = []
    for g in range(FULL):
        for f in range(FIELDS):
            out.append(pl.ds(base + 8 * g * level_stride + f, 8, stride=level_stride))
    return out


def build_weights(lm, fm, w_ref):
    split = lambda v: (v.astype(BF16).astype(F32), v - v.astype(BF16).astype(F32))
    dot = functools.partial(jnp.dot, preferred_element_type=F32)
    lv, fv = level_field(iota((ROWS, LEVELS), 0))
    el = (lv == iota((ROWS, LEVELS), 1)).astype(F32).astype(BF16)
    lv, fv = level_field(iota((ROWS, FIELDS), 0))
    ef = (fv == iota((ROWS, FIELDS), 1)).astype(F32).astype(BF16)
    lt, ft = level_field(iota((LEVELS, ROWS), 1))
    elt = (lt == iota((LEVELS, ROWS), 0)).astype(F32).astype(BF16)
    lt, ft = level_field(iota((FIELDS, ROWS), 1))
    eft = (ft == iota((FIELDS, ROWS), 0)).astype(F32).astype(BF16)
    lhi, llo = split(lm)
    fhi, flo = split(fm)
    wl = dot(dot(el, lhi.astype(BF16)).astype(BF16), elt) + dot(
        dot(el, llo.astype(BF16)).astype(BF16), elt
    )
    wf = dot(dot(ef, fhi.astype(BF16)).astype(BF16), eft) + dot(
        dot(ef, flo.astype(BF16)).astype(BF16), eft
    )
    lr, fr = level_field(iota((ROWS, ROWS), 0))
    lc, fc = level_field(iota((ROWS, ROWS), 1))
    w = jnp.where(fr == fc, wl, 0.0) + jnp.where(lr == lc, wf, 0.0)
    whi, wlo = split(w)
    w_ref[...] = jnp.concatenate([whi, whi, wlo], axis=1).astype(BF16)


def physics_pair(s_ref, ja, jb, w_ref, v_ref, r_ref):
    v_ref[:, :CELLS] = s_ref[ja]
    v_ref[:, CELLS:] = s_ref[jb]

    def sweep(_, carry):
        for r in range(0, ROWS, 16):
            t = jnp.tanh(v_ref[r : r + 16, :])
            hi = t.astype(BF16)
            r_ref[r : r + 16, :] = hi
            r_ref[ROWS + r : ROWS + r + 16, :] = (t - hi.astype(F32)).astype(BF16)
            r_ref[2 * ROWS + r : 2 * ROWS + r + 16, :] = hi
        v_ref[...] += jnp.dot(w_ref[...], r_ref[...], preferred_element_type=F32)
        return carry

    lax.fori_loop(0, SWEEPS, sweep, 0)
    s_ref[ja] = v_ref[:, :CELLS]
    s_ref[jb] = v_ref[:, CELLS:]


def coefficients(ct_ref, ja, jb, off, coef_ref, k):
    lane = iota((8, CELLS), 1)
    sub = iota((8, CELLS), 0)
    for g in range(FULL + 1):
        rows = pl.ds(8 * g, 8)
        c = pltpu.roll(
            jnp.where(lane >= off, ct_ref[ja, rows, :], ct_ref[jb, rows, :]), CELLS - off, 1
        )
        p = c
        for sh in (1, 2, 4, 8, 16, 32, 64):
            p = p * jnp.where(lane >= sh, pltpu.roll(p, sh, 1), 1.0)
        mid = jnp.sum(jnp.where(lane == CELLS // 2 - 1, p, 0.0), axis=1, keepdims=True)
        scale = jnp.broadcast_to(1.0 / mid, (8, CELLS))
        ei = p * scale
        d = jnp.where(lane >= 1, pltpu.roll(ei, 1, 1), scale)
        e = 1.0 / ei
        di = 1.0 / d
        k1 = BUOYANCY * (d * ei)
        k2 = BUOYANCY * (e * di)
        if g == FULL:
            k1 = jnp.where(sub % 4 == 0, k1, 0.0)
            k2 = jnp.where(sub % 4 == 1, k2, 0.0)
        for i, value in enumerate((1.0 - c, d, di, ei, e, k1, k2)):
            coef_ref[i, k, rows, :] = value


def window(src_ref, ja, jb, off, coef_ref, k, dst_ref, da, db, split=((0, 1, 2, 6), (3, 4, 5))):
    lane = iota((8, CELLS), 1)
    take = lane >= off
    keep_a = (lane >= off + SECTIONS) & (lane < off + CELLS - SECTIONS)
    keep_b = (lane < off - SECTIONS) & (lane >= off + SECTIONS - CELLS)

    def load(row):
        rows = pl.ds(row, 8)
        return pltpu.roll(
            jnp.where(take, src_ref[ja, rows, :], src_ref[jb, rows, :]), CELLS - off, 1
        )

    def store(row, value):
        back = pltpu.roll(value, off, 1)
        rows = pl.ds(row, 8)
        pltpu.store(dst_ref.at[da, rows, :], back, mask=keep_a)
        pltpu.store(dst_ref.at[db, rows, :], back, mask=keep_b)

    for groups in split:
        cf = {g: [coef_ref[i, k, pl.ds(8 * g, 8), :] for i in (0, 5, 6)] for g in groups}
        q = {}
        for g in groups:
            di = coef_ref[2, k, pl.ds(8 * g, 8), :]
            ei = coef_ref[3, k, pl.ds(8 * g, 8), :]
            if g < FULL:
                q[g] = [load(64 * g + 8 * f) * (di if f % 2 == 0 else ei) for f in range(FIELDS)]
            else:
                q[g] = [load(64 * g) * di, load(64 * g + 8) * ei]
        for _ in range(SECTIONS):
            for g in groups:
                a, k1, k2 = cf[g]
                x = [
                    a * v + pltpu.roll(v, 1 if f % 2 == 0 else CELLS - 1, 1)
                    for f, v in enumerate(q[g])
                ]
                if g < FULL:
                    x[1] = x[1] + k1 * x[2]
                    x[2] = x[2] - k2 * x[1]
                else:
                    x[1] = x[1] + k1 * pltpu.roll(x[0], 7, 0)
                    x[0] = x[0] - k2 * pltpu.roll(x[1], 1, 0)
                q[g] = x
        for g in groups:
            d = coef_ref[1, k, pl.ds(8 * g, 8), :]
            e = coef_ref[4, k, pl.ds(8 * g, 8), :]
            for f, v in enumerate(q[g]):
                store(64 * g + 8 * f, v * (d if f % 2 == 0 else e))


def place(k):
    start = FIRST + NET * k
    return start // CELLS, start % CELLS


def courant_tile(c_ref, t):
    sub = iota((8, CELLS), 0)
    out = [c_ref[pl.ds(64 * g + t, 8, stride=8), :] for g in range(FULL)]
    a = jnp.broadcast_to(c_ref[pl.ds(64 * FULL + t, 1), :], (8, CELLS))
    b = jnp.broadcast_to(c_ref[pl.ds(64 * FULL + 8 + t, 1), :], (8, CELLS))
    return out + [jnp.where(sub < 4, a, b)]


def fetch(pairs, sem):
    copies = [pltpu.make_async_copy(a, b, sem.at[i]) for i, (a, b) in enumerate(pairs)]
    for copy in copies:
        copy.start()
    return copies


def pack_kernel(
    x_ref, c_hbm, list_hbm, count_hbm, first_ref, last_ref, c_ref, list_ref, count_ref, sem, lsem
):
    copies = []
    small = fetch(((c_hbm, c_ref), (list_hbm, list_ref), (count_hbm, count_ref)), lsem)
    for i, (ref, t) in enumerate(((first_ref, 0), (last_ref, TILES - 1))):
        copy = pltpu.make_async_copy(
            x_ref.at[:, pl.ds(8 * t, 8), :], ref.at[pl.ds(0, LEVELS)], sem.at[i]
        )
        copy.start()
        copies.append(copy)
    for copy in small:
        copy.wait()
    sub = iota((8, CELLS), 0)
    for ref, t in ((first_ref, 0), (last_ref, TILES - 1)):
        for g, value in enumerate(courant_tile(c_ref, t)):
            ref[LEVELS + g] = value
        flags = []
        for cycle in range(CYCLES):
            hit = jnp.int32(0)
            for slot in range(4):
                named = (slot < count_ref[cycle]) & (list_ref[cycle, slot] == t)
                hit = jnp.where(named, jnp.int32(1), hit)
            flags.append(hit)
        ref[LEVELS + FULL + 1] = jnp.where(sub < 4, flags[0], flags[1]).astype(F32)
    for copy in copies:
        copy.wait()


def inner_kernel(
    x_ref, c_hbm, lm_hbm, fm_hbm, list_hbm, count_hbm,
    out_ref, edge_ref, coef_ref, w_ref,
    n_ref, s_ref, v_ref, r_ref, ct_ref, c_ref, lm_ref, fm_ref, list_ref, count_ref, sem,
):
    lm_copy, fm_copy, c_copy, list_copy, count_copy, copy = fetch(
        (
            (lm_hbm, lm_ref), (fm_hbm, fm_ref), (c_hbm, c_ref),
            (list_hbm, list_ref), (count_hbm, count_ref), (x_ref, n_ref),
        ),
        sem,
    )
    lm_copy.wait()
    fm_copy.wait()
    build_weights(lm_ref[...], fm_ref[...], w_ref)
    c_copy.wait()
    for t in range(TILES):
        for g, value in enumerate(courant_tile(c_ref, t)):
            ct_ref[t + 1, pl.ds(8 * g, 8), :] = value

    def coef_body(k, carry):
        j, off = place(k)
        coefficients(ct_ref, j, j + 1, off, coef_ref, k)
        return carry

    lax.fori_loop(1, WINDOWS - 2, coef_body, 0)
    copy.wait()

    def convert(t, carry):
        for i, rows in enumerate(natural_rows(8 * t, 64)):
            s_ref[t + 1, pl.ds(8 * i, 8), :] = n_ref[rows, :]
        for half in range(2):
            lo = n_ref[pl.ds(64 * 8 * FULL + 8 * t + half, 4, stride=2), :]
            hi = n_ref[pl.ds(64 * 8 * FULL + 64 + 8 * t + half, 4, stride=2), :]
            s_ref[t + 1, pl.ds(64 * FULL + 8 * half, 4), :] = lo
            s_ref[t + 1, pl.ds(64 * FULL + 8 * half + 4, 4), :] = hi
        return carry

    lax.fori_loop(0, TILES, convert, 0)
    list_copy.wait()
    count_copy.wait()
    count = count_ref[0]

    def pair(p, carry):
        ja = list_ref[0, 2 * p] + 1
        jb = list_ref[0, jnp.minimum(2 * p + 1, count - 1)] + 1
        physics_pair(s_ref, ja, jb, w_ref, v_ref, r_ref)
        return carry

    lax.fori_loop(0, (count + 1) // 2, pair, 0)
    edge_ref[0] = s_ref[1]
    edge_ref[1] = s_ref[TILES]

    def window_body(k, carry):
        j, off = place(k)
        window(s_ref, j, j + 1, off, coef_ref, k, out_ref, j, j + 1)
        return carry

    lax.fori_loop(1, WINDOWS - 2, window_body, 0)


def payload_tile(pay_ref, s_ref, j):
    for i, rows in enumerate(natural_rows(0, 8)):
        s_ref[j, pl.ds(8 * i, 8), :] = pay_ref[rows, :]
    for half in range(2):
        s_ref[j, pl.ds(64 * FULL + 8 * half, 8), :] = pay_ref[
            pl.ds(64 * FULL + half, 8, stride=2), :
        ]


def outer_kernel(
    in_ref, edge_ref, coef_in_ref, w_ref, left_ref, right_ref, c_hbm, list_hbm, count_hbm,
    out_ref,
    s_ref, e_ref, d_ref, v_ref, r_ref, ct_ref, coef_ref, n_ref, c_ref, list_ref, count_ref, sem,
):
    c_copy, list_copy, count_copy, copy = fetch(
        (
            (c_hbm, c_ref), (list_hbm, list_ref), (count_hbm, count_ref),
            (in_ref, s_ref.at[pl.ds(0, TILES + 2)]),
        ),
        sem,
    )
    lane = iota((8, CELLS), 1)
    payload_tile(left_ref, e_ref, 0)
    e_ref[1] = edge_ref[0]
    e_ref[2] = edge_ref[1]
    payload_tile(right_ref, e_ref, 3)
    for g in range(FULL + 1):
        rows = pl.ds(8 * g, 8)
        ct_ref[0, rows, :] = left_ref[pl.ds(ROWS + 8 * g, 8), :]
        ct_ref[3, rows, :] = right_ref[pl.ds(ROWS + 8 * g, 8), :]
    c_copy.wait()
    for j, t in ((1, 0), (2, TILES - 1)):
        for g, value in enumerate(courant_tile(c_ref, t)):
            ct_ref[j, pl.ds(8 * g, 8), :] = value
    for k, j in ((0, 0), (WINDOWS - 2, 2), (WINDOWS - 1, 2)):
        coefficients(ct_ref, j, j + 1, place(k)[1], coef_ref, k)

    def body(k, carry):
        coef_ref[:, k] = coef_in_ref[:, k]
        return carry

    lax.fori_loop(1, WINDOWS - 2, body, 0)
    frow = ROWS + 8 * (FULL + 1)
    listed = []
    for cycle in range(CYCLES):
        row = pl.ds(frow + 4 * cycle, 1)
        listed.append((left_ref[row, :], right_ref[row, :]))

    def compose(ref, left, right, to):
        for r in range(0, ROWS, 8):
            rows = pl.ds(r, 8)
            ref[to, rows, :] = jnp.where(lane < CELLS // 2, ref[right, rows, :], ref[left, rows, :])

    def restore(ref, left, right, frm, flags):
        ml = (jnp.broadcast_to(flags[0], (8, CELLS)) > 0.5) & (lane >= CELLS // 2)
        mr = (jnp.broadcast_to(flags[1], (8, CELLS)) > 0.5) & (lane < CELLS // 2)
        for r in range(0, ROWS, 8):
            rows = pl.ds(r, 8)
            done = ref[frm, rows, :]
            ref[left, rows, :] = jnp.where(ml, done, ref[left, rows, :])
            ref[right, rows, :] = jnp.where(mr, done, ref[right, rows, :])

    any_flag = [jnp.max(jnp.maximum(l, r)) > 0.5 for l, r in listed]

    @pl.when(any_flag[0])
    def _():
        compose(e_ref, 0, 3, 4)
        physics_pair(e_ref, 4, 4, w_ref, v_ref, r_ref)
        restore(e_ref, 0, 3, 4, listed[0])

    list_copy.wait()
    count_copy.wait()
    copy.wait()
    for k, a, b in ((0, 0, 1), (WINDOWS - 2, 2, 3), (WINDOWS - 1, 2, 3)):
        j, off = place(k)
        window(e_ref, a, b, off, coef_ref, k, s_ref, j, j + 1)

    count = count_ref[1]
    total = count + any_flag[1].astype(jnp.int32)
    HALO = TILES + 2

    @pl.when(any_flag[1])
    def _():
        compose(s_ref, 0, TILES + 1, HALO)

    def entry(i):
        i = jnp.minimum(i, total - 1)
        named = list_ref[1, jnp.minimum(i, 3)] + 1
        return jnp.where(i < count, named, HALO)

    def pair(p, carry):
        physics_pair(s_ref, entry(2 * p), entry(2 * p + 1), w_ref, v_ref, r_ref)
        return carry

    lax.fori_loop(0, (total + 1) // 2, pair, 0)

    @pl.when(any_flag[1])
    def _():
        restore(s_ref, 0, TILES + 1, HALO, listed[1])

    def window_body(k, carry):
        j, off = place(k)
        window(s_ref, j, j + 1, off, coef_ref, k, d_ref, j, j + 1)
        return carry

    lax.fori_loop(0, WINDOWS - 1, window_body, 0)

    def convert(t, carry):
        for i, rows in enumerate(natural_rows(8 * t, 64)):
            n_ref[rows, :] = d_ref[t + 1, pl.ds(8 * i, 8), :]
        for half in range(2):
            n_ref[pl.ds(64 * 8 * FULL + 8 * t + half, 4, stride=2), :] = d_ref[
                t + 1, pl.ds(64 * FULL + 8 * half, 4), :
            ]
            n_ref[pl.ds(64 * 8 * FULL + 64 + 8 * t + half, 4, stride=2), :] = d_ref[
                t + 1, pl.ds(64 * FULL + 8 * half + 4, 4), :
            ]
        return carry

    lax.fori_loop(0, TILES, convert, 0)
    pltpu.sync_copy(n_ref, out_ref)


VM = pl.BlockSpec(memory_space=pltpu.VMEM)
SM = pl.BlockSpec(memory_space=pltpu.SMEM)
ANY = pl.BlockSpec(memory_space=pl.ANY)
HBM = pl.BlockSpec(memory_space=pltpu.HBM)
SMALL = [
    pltpu.VMEM((LEVELS * TILES, CELLS), F32),
    pltpu.SMEM((CYCLES, 4), jnp.int32),
    pltpu.SMEM((CYCLES,), jnp.int32),
]
LIMIT = 40 << 20


def local(state, courant, level_mix, field_mix, send_list, send_count):
    shape = jax.ShapeDtypeStruct
    hbm = lambda v: pltpu.with_memory_space_constraint(v, pltpu.HBM)
    x = state.reshape(FIELDS, LEVELS, TILES, CELLS).transpose(1, 2, 0, 3)
    c = courant.reshape(LEVELS * TILES, CELLS)
    chosen = send_list.reshape(CYCLES, 4)
    count = send_count.reshape(CYCLES)
    c, chosen, count, level_mix, field_mix = map(hbm, (c, chosen, count, level_mix, field_mix))
    x3, x2 = hbm(x.reshape(LEVELS, TILES * FIELDS, CELLS)), hbm(x.reshape(LEVELS * 64, CELLS))
    first, last = pl.pallas_call(
        pack_kernel,
        name="pack",
        out_shape=(shape((PAY // 8, 8, CELLS), F32),) * 2,
        in_specs=[HBM] * 4,
        out_specs=(VM, VM),
        scratch_shapes=SMALL + [pltpu.SemaphoreType.DMA((2,)), pltpu.SemaphoreType.DMA((3,))],
        compiler_params=pltpu.CompilerParams(vmem_limit_bytes=8 << 20),
    )(x3, c, chosen, count)
    n = lax.axis_size("pos")
    left = lax.ppermute(last, "pos", [(i, (i + 1) % n) for i in range(n)])
    right = lax.ppermute(first, "pos", [((i + 1) % n, i) for i in range(n)])
    mid, edge, coef, w = pl.pallas_call(
        inner_kernel,
        name="inner",
        out_shape=(
            shape((TILES + 2, ROWS, CELLS), F32),
            shape((2, ROWS, CELLS), F32),
            shape((7, WINDOWS, CROWS, CELLS), F32),
            shape((ROWS, 3 * ROWS), BF16),
        ),
        in_specs=[HBM] * 6,
        out_specs=(VM,) * 4,
        scratch_shapes=[
            pltpu.VMEM((LEVELS * 64, CELLS), F32),
            pltpu.VMEM((TILES + 2, ROWS, CELLS), F32),
            pltpu.VMEM((ROWS, 2 * CELLS), F32),
            pltpu.VMEM((3 * ROWS, 2 * CELLS), BF16),
            pltpu.VMEM((TILES + 2, CROWS, CELLS), F32),
            SMALL[0],
            pltpu.VMEM((LEVELS, LEVELS), F32),
            pltpu.VMEM((FIELDS, FIELDS), F32),
            *SMALL[1:],
            pltpu.SemaphoreType.DMA((6,)),
        ],
        compiler_params=pltpu.CompilerParams(vmem_limit_bytes=LIMIT),
        cost_estimate=pl.CostEstimate(flops=4_000_000_000, bytes_accessed=8_000_000, transcendentals=0),
    )(x2, c, level_mix, field_mix, chosen, count)
    out = pl.pallas_call(
        outer_kernel,
        name="outer",
        out_shape=shape((LEVELS * 64, CELLS), F32),
        in_specs=[ANY, VM, VM, VM, VM, VM, HBM, HBM, HBM],
        out_specs=ANY,
        scratch_shapes=[
            pltpu.VMEM((TILES + 3, ROWS, CELLS), F32),
            pltpu.VMEM((5, ROWS, CELLS), F32),
            pltpu.VMEM((TILES + 2, ROWS, CELLS), F32),
            pltpu.VMEM((ROWS, 2 * CELLS), F32),
            pltpu.VMEM((3 * ROWS, 2 * CELLS), BF16),
            pltpu.VMEM((4, CROWS, CELLS), F32),
            pltpu.VMEM((7, WINDOWS, CROWS, CELLS), F32),
            pltpu.VMEM((LEVELS * 64, CELLS), F32),
            *SMALL,
            pltpu.SemaphoreType.DMA((4,)),
        ],
        compiler_params=pltpu.CompilerParams(vmem_limit_bytes=LIMIT),
    )(mid, edge, coef, w, left.reshape(PAY, CELLS), right.reshape(PAY, CELLS), c, chosen, count)
    out = out.reshape(LEVELS, TILES, FIELDS, CELLS).transpose(2, 0, 1, 3)
    return out.reshape(1, FIELDS, LEVELS, TILES * CELLS)


def solution(mesh):
    in_specs = (
        P("chan", None, None, "pos"),
        P("chan", None, "pos"),
        P(),
        P(),
        P(None, "chan", "pos", None),
        P(None, "chan", "pos"),
    )
    out_specs = P("chan", None, None, "pos")
    return jax.shard_map(local, mesh=mesh, in_specs=in_specs, out_specs=out_specs, check_vma=False)
```

```python
import functools

import jax
import jax.numpy as jnp
from jax import lax
from jax.experimental import pallas as pl
from jax.experimental.pallas import tpu as pltpu
from jax.sharding import PartitionSpec as P

LEVELS = 50
FIELDS = 8
CELLS = 128
SECTIONS = 12
SWEEPS = 4
CYCLES = 2
TILES = 8
BUOYANCY = 0.4
F32 = jnp.float32
BF16 = jnp.bfloat16

BLOCKS = ((2, 0), (1, 3), (4, 6), (5, 7))
HALF = 64
HALO = CYCLES * SECTIONS
OFF = HALO + 8
OWN = TILES * CELLS
XROWS = OFF + OWN + HALO + 8
EROWS = 8 + 4 * HALO + 8
NB = len(BLOCKS)
WIDE = NB * CELLS
PLEV = 56
PAY = 464


def iota(shape, dim):
    return lax.broadcasted_iota(jnp.int32, shape, dim)


def fetch(pairs, sem):
    copies = [pltpu.make_async_copy(a, b, sem.at[i]) for i, (a, b) in enumerate(pairs)]
    for copy in copies:
        copy.start()
    return copies


def strips(ref, index, row):
    take = [ref[(*index, pl.ds(64 * g + row, 8, stride=8), slice(None))] for g in range(PLEV // 8)]
    return take + [jnp.zeros((8, CELLS), F32)]


def build_weights(lm_ref, fm_ref, q_ref, w_ref):
    q_ref[...] = jnp.zeros((CELLS, CELLS), F32)
    lm = lm_ref[...]
    q_ref[:LEVELS, :LEVELS] = lm
    q_ref[HALF : HALF + LEVELS, :LEVELS] = lm
    q_ref[...] = q_ref[...].T
    lane = iota((16, CELLS), 1)
    sub = iota((16, CELLS), 0)
    low = lane < HALF
    for r in range(0, HALF, 16):
        eye = (lane % HALF == sub + r) & (sub + r < LEVELS)
        lt = q_ref[r : r + 16, :]
        for kb, pair_k in enumerate(BLOCKS):
            for kh, g in enumerate(pair_k):
                row = CELLS * kb + HALF * kh + r
                for nb, (fa, fb) in enumerate(BLOCKS):
                    w = jnp.where(eye, jnp.where(low, fm_ref[fa, g], fm_ref[fb, g]), 0.0)
                    if g == fa:
                        w = w + jnp.where(low, lt, 0.0)
                    if g == fb:
                        w = w + jnp.where(low, 0.0, lt)
                    hi = w.astype(BF16)
                    lo = (w - hi.astype(F32)).astype(BF16)
                    cols = slice(CELLS * nb, CELLS * (nb + 1))
                    w_ref[row : row + 16, cols] = hi
                    w_ref[WIDE + row : WIDE + row + 16, cols] = hi
                    w_ref[2 * WIDE + row : 2 * WIDE + row + 16, cols] = lo


def physics(s_ref, row, rows, w_ref, r_ref):
    def sweep(_, carry):
        for b in range(NB):
            for r in range(0, rows, 16):
                t = jnp.tanh(s_ref[b, pl.ds(row + r, 16), :])
                hi = t.astype(BF16)
                lo = (t - hi.astype(F32)).astype(BF16)
                r_ref[r : r + 16, CELLS * b : CELLS * (b + 1)] = hi
                r_ref[r : r + 16, WIDE + CELLS * b : WIDE + CELLS * (b + 1)] = lo
                r_ref[r : r + 16, 2 * WIDE + CELLS * b : 2 * WIDE + CELLS * (b + 1)] = hi
        acc = jnp.dot(r_ref[:rows, :], w_ref[...], preferred_element_type=F32)
        for b in range(NB):
            s_ref[b, pl.ds(row, rows), :] += acc[:, CELLS * b : CELLS * (b + 1)]
        return carry

    lax.fori_loop(0, SWEEPS, sweep, 0)


def section(src, dst, c_ref, d_ref, kv, base, groups):
    for i in range(groups):
        row = base + 8 * i
        here, before, after = pl.ds(row, 8), pl.ds(row - 1, 8), pl.ds(row + 1, 8)
        d, cm, cp = d_ref[here, :], c_ref[before, :], c_ref[after, :]
        x = []
        for b in range(NB):
            side, coef = (before, cm) if b % 2 == 0 else (after, cp)
            x.append(d * src[b, here, :] + coef * src[b, side, :])
        x[1] = x[1] + kv * x[0]
        x[0] = x[0] - kv * x[1]
        for b in range(NB):
            dst[b, here, :] = x[b]


def transport(a_ref, b_ref, c_ref, d_ref, base, groups, unroll):
    kv = jnp.where(iota((8, CELLS), 1) < HALF, BUOYANCY, 0.0)

    def sweep(src, dst):
        def body(i, carry):
            row = pl.multiple_of(base + i * (8 * unroll), 8)
            section(src, dst, c_ref, d_ref, kv, row, unroll)
            return carry

        if groups == unroll:
            section(src, dst, c_ref, d_ref, kv, base, groups)
        else:
            lax.fori_loop(0, groups // unroll, body, 0)

    def two(_, carry):
        sweep(a_ref, b_ref)
        sweep(b_ref, a_ref)
        return carry

    lax.fori_loop(0, SECTIONS // 2, two, 0)


def put_courant(c_ref, d_ref, row, block):
    c = jnp.concatenate(block + block, axis=0).T
    c_ref[pl.ds(row, CELLS), :] = c
    d_ref[pl.ds(row, CELLS), :] = 1.0 - c


def tile_block(ref, index, pair):
    return jnp.concatenate(strips(ref, index, pair[0]) + strips(ref, index, pair[1]), axis=0).T


def pack_kernel(
    x_ref, c_hbm, list_hbm, count_hbm, first_ref, last_ref, c_ref, list_ref, count_ref, sem, lsem
):
    small = fetch(
        ((c_hbm, c_ref.at[pl.ds(0, LEVELS * TILES)]), (list_hbm, list_ref), (count_hbm, count_ref)),
        lsem,
    )
    ends = ((first_ref, 0), (last_ref, TILES - 1))
    copies = fetch(
        [(x_ref.at[:, pl.ds(8 * t, 8), :], ref.at[pl.ds(0, LEVELS)]) for ref, t in ends], sem
    )
    c_ref[LEVELS * TILES :, :] = jnp.zeros((48, CELLS), F32)
    for copy in small:
        copy.wait()
    sub = iota((8, CELLS), 0)
    for ref, t in ends:
        for g, value in enumerate(strips(c_ref, (), t)[: PLEV // 8]):
            ref[LEVELS + g] = value
        flags = []
        for cycle in range(CYCLES):
            hit = jnp.int32(0)
            for slot in range(4):
                named = (slot < count_ref[cycle]) & (list_ref[cycle, slot] == t)
                hit = jnp.where(named, jnp.int32(1), hit)
            flags.append(hit)
        ref[LEVELS + PLEV // 8] = jnp.where(sub < 4, flags[0], flags[1]).astype(F32)
    for copy in copies:
        copy.wait()


def inner_kernel(
    x_ref, c_hbm, lm_hbm, fm_hbm, list_hbm, count_hbm,
    a_ref, edge_ref, w_ref,
    n_ref, b_ref, r_ref, q_ref, cx_ref, dx_ref, c_ref, lm_ref, fm_ref, list_ref, count_ref,
    sem, xsem,
):
    lm_copy, fm_copy, c_copy, list_copy, count_copy = fetch(
        (
            (lm_hbm, lm_ref), (fm_hbm, fm_ref), (c_hbm, c_ref.at[pl.ds(0, LEVELS * TILES)]),
            (list_hbm, list_ref), (count_hbm, count_ref),
        ),
        sem,
    )
    tiles = fetch(
        [
            (x_ref.at[:, pl.ds(8 * t, 8), :], n_ref.at[t, pl.ds(0, LEVELS)])
            for t in range(TILES)
        ],
        xsem,
    )
    c_ref[LEVELS * TILES :, :] = jnp.zeros((48, CELLS), F32)
    n_ref[:, LEVELS:] = jnp.zeros((TILES, PLEV - LEVELS, 8, CELLS), F32)
    lm_copy.wait()
    fm_copy.wait()
    build_weights(lm_ref, fm_ref, q_ref, w_ref)
    c_copy.wait()
    for t in range(TILES):
        put_courant(cx_ref, dx_ref, OFF + CELLS * t, strips(c_ref, (), t))
    flat = n_ref.reshape(TILES, PLEV * 8, CELLS)
    for t, copy in enumerate(tiles):
        copy.wait()
        for b, pair in enumerate(BLOCKS):
            a_ref[b, pl.ds(OFF + CELLS * t, CELLS), :] = tile_block(flat, (t,), pair)
    list_copy.wait()
    count_copy.wait()

    def one(k, carry):
        row = pl.multiple_of(OFF + CELLS * list_ref[0, k], 8)
        physics(a_ref, row, CELLS, w_ref, r_ref)
        return carry

    lax.fori_loop(0, count_ref[0], one, 0)
    edge_ref[:, 0] = a_ref[:, OFF : OFF + HALO, :]
    edge_ref[:, 1] = a_ref[:, OFF + OWN - HALO : OFF + OWN, :]
    transport(a_ref, b_ref, cx_ref, dx_ref, OFF, OWN // 8, 32)


def outer_kernel(
    in_ref, edge_ref, w_ref, left_ref, right_ref, c_hbm, list_hbm, count_hbm,
    out_ref,
    a_ref, b_ref, ea_ref, eb_ref, h_ref, r_ref, cx_ref, dx_ref, ec_ref, ed_ref, n_ref,
    c_ref, list_ref, count_ref, sem, xsem,
):
    c_copy, list_copy, count_copy, copy = fetch(
        (
            (c_hbm, c_ref.at[pl.ds(0, LEVELS * TILES)]),
            (list_hbm, list_ref), (count_hbm, count_ref), (in_ref, a_ref),
        ),
        sem,
    )
    c_ref[LEVELS * TILES :, :] = jnp.zeros((48, CELLS), F32)
    for b, pair in enumerate(BLOCKS):
        ea_ref[b, 8 : 8 + HALO, :] = tile_block(left_ref, (), pair)[CELLS - HALO :]
        ea_ref[b, 8 + HALO : 8 + 2 * HALO, :] = edge_ref[b, 0]
        ea_ref[b, 8 + 2 * HALO : 8 + 3 * HALO, :] = edge_ref[b, 1]
        ea_ref[b, 8 + 3 * HALO : 8 + 4 * HALO, :] = tile_block(right_ref, (), pair)[:HALO]

    def pay_courant(ref):
        zero = jnp.zeros((8, CELLS), F32)
        rows = [ref[pl.ds(8 * LEVELS + 8 * g, 8), :] for g in range(PLEV // 8)] + [zero]
        return jnp.concatenate(rows + rows, axis=0).T

    ends = ((0, pay_courant(left_ref)[CELLS - HALO :]), (OFF + OWN, pay_courant(right_ref)[:HALO]))
    c_copy.wait()
    for t in range(TILES):
        put_courant(cx_ref, dx_ref, OFF + CELLS * t, strips(c_ref, (), t))
    for row, c in ((OFF - HALO, ends[0][1]), (OFF + OWN, ends[1][1])):
        cx_ref[row : row + HALO, :] = c
        dx_ref[row : row + HALO, :] = 1.0 - c
    for frm, to, s in ((cx_ref, ec_ref, 0), (dx_ref, ed_ref, 0)):
        to[8 : 8 + 2 * HALO, :] = frm[OFF - HALO : OFF + HALO, :]
        to[8 + 2 * HALO : 8 + 4 * HALO, :] = frm[OFF + OWN - HALO : OFF + OWN + HALO, :]

    frow = 8 * LEVELS + PLEV
    listed = []
    for cycle in range(CYCLES):
        row = pl.ds(frow + 4 * cycle, 1)
        listed.append([jnp.max(ref[row, :]) > 0.5 for ref in (left_ref, right_ref)])

    def halo_physics(ref, first, second, rows, flags):
        for cond in (flags[0] | flags[1],):

            @pl.when(cond)
            def _():
                h_ref[:, :rows] = ref[:, pl.ds(first, rows), :]
                h_ref[:, rows : 2 * rows] = ref[:, pl.ds(second, rows), :]
                physics(h_ref, 0, 2 * rows, w_ref, r_ref)

        for flag, to, frm in ((flags[0], first, 0), (flags[1], second, rows)):

            @pl.when(flag)
            def _():
                ref[:, pl.ds(to, rows), :] = h_ref[:, frm : frm + rows]

    halo_physics(ea_ref, 8, 8 + 3 * HALO, HALO, listed[0])
    transport(ea_ref, eb_ref, ec_ref, ed_ref, 8, 4 * HALO // 8, 4 * HALO // 8)
    list_copy.wait()
    count_copy.wait()
    copy.wait()
    sub = iota((8, CELLS), 0)
    for b in range(NB):
        for row in (16, 24, 32):
            a_ref[b, row : row + 8, :] = ea_ref[b, row : row + 8, :]
        a_ref[b, 40:48, :] = jnp.where(sub < 4, ea_ref[b, 40:48, :], a_ref[b, 40:48, :])
        back = OFF + OWN - HALO - (8 + 2 * HALO)
        row = OFF + OWN - 16
        a_ref[b, row : row + 8, :] = jnp.where(
            sub >= 4, ea_ref[b, row - back : row - back + 8, :], a_ref[b, row : row + 8, :]
        )
        for row in (OFF + OWN - 8, OFF + OWN, OFF + OWN + 8):
            a_ref[b, row : row + 8, :] = ea_ref[b, row - back : row - back + 8, :]
    halo_physics(a_ref, OFF - 16, OFF + OWN, 16, listed[1])

    def one(k, carry):
        row = pl.multiple_of(OFF + CELLS * list_ref[1, k], 8)
        physics(a_ref, row, CELLS, w_ref, r_ref)
        return carry

    lax.fori_loop(0, count_ref[1], one, 0)
    transport(a_ref, b_ref, cx_ref, dx_ref, OFF - 16, OWN // 8 + 4, 33)
    flat = n_ref.reshape(TILES, PLEV * 8, CELLS)
    copies = []
    for t in range(TILES):
        for b, pair in enumerate(BLOCKS):
            block = a_ref[b, pl.ds(OFF + CELLS * t, CELLS), :].T
            for h, f in enumerate(pair):
                for g in range(PLEV // 8):
                    flat[t, pl.ds(64 * g + f, 8, stride=8), :] = block[
                        HALF * h + 8 * g : HALF * h + 8 * g + 8
                    ]
        copies += fetch(
            [(n_ref.at[t, pl.ds(0, LEVELS)], out_ref.at[:, pl.ds(8 * t, 8), :])],
            xsem.at[pl.ds(t, 1)],
        )
    for copy in copies:
        copy.wait()


VM = pl.BlockSpec(memory_space=pltpu.VMEM)
HBM = pl.BlockSpec(memory_space=pltpu.HBM)
ANY = pl.BlockSpec(memory_space=pl.ANY)
SMALL = [
    pltpu.VMEM((PLEV * TILES, CELLS), F32),
    pltpu.SMEM((CYCLES, 4), jnp.int32),
    pltpu.SMEM((CYCLES,), jnp.int32),
]
LIMIT = 40 << 20
STATE = (NB, XROWS, CELLS)


def local(state, courant, level_mix, field_mix, send_list, send_count):
    shape = jax.ShapeDtypeStruct
    hbm = lambda v: pltpu.with_memory_space_constraint(v, pltpu.HBM)
    x = state.reshape(FIELDS, LEVELS, TILES, CELLS).transpose(1, 2, 0, 3)
    x = hbm(x.reshape(LEVELS, TILES * FIELDS, CELLS))
    c = hbm(courant.reshape(LEVELS * TILES, CELLS))
    chosen, count = hbm(send_list.reshape(CYCLES, 4)), hbm(send_count.reshape(CYCLES))
    level_mix, field_mix = hbm(level_mix), hbm(field_mix)
    first, last = pl.pallas_call(
        pack_kernel,
        name="pack",
        out_shape=(shape((PAY // 8, 8, CELLS), F32),) * 2,
        in_specs=[HBM] * 4,
        out_specs=(VM, VM),
        scratch_shapes=SMALL + [pltpu.SemaphoreType.DMA((2,)), pltpu.SemaphoreType.DMA((3,))],
        compiler_params=pltpu.CompilerParams(vmem_limit_bytes=8 << 20),
    )(x, c, chosen, count)
    n = lax.axis_size("pos")
    left = lax.ppermute(last, "pos", [(i, (i + 1) % n) for i in range(n)])
    right = lax.ppermute(first, "pos", [((i + 1) % n, i) for i in range(n)])
    mid, edge, w = pl.pallas_call(
        inner_kernel,
        name="inner",
        out_shape=(
            shape(STATE, F32),
            shape((NB, 2, HALO, CELLS), F32),
            shape((3 * WIDE, WIDE), BF16),
        ),
        in_specs=[HBM] * 6,
        out_specs=(VM,) * 3,
        scratch_shapes=[
            pltpu.VMEM((TILES, PLEV, 8, CELLS), F32),
            pltpu.VMEM(STATE, F32),
            pltpu.VMEM((CELLS, 3 * WIDE), BF16),
            pltpu.VMEM((CELLS, CELLS), F32),
            pltpu.VMEM((XROWS, CELLS), F32),
            pltpu.VMEM((XROWS, CELLS), F32),
            SMALL[0],
            pltpu.VMEM((LEVELS, LEVELS), F32),
            pltpu.SMEM((FIELDS, FIELDS), F32),
            *SMALL[1:],
            pltpu.SemaphoreType.DMA((5,)),
            pltpu.SemaphoreType.DMA((TILES,)),
        ],
        compiler_params=pltpu.CompilerParams(vmem_limit_bytes=LIMIT),
        cost_estimate=pl.CostEstimate(
            flops=4_000_000_000, bytes_accessed=8_000_000, transcendentals=0
        ),
    )(x, c, level_mix, field_mix, chosen, count)
    out = pl.pallas_call(
        outer_kernel,
        name="outer",
        out_shape=shape((LEVELS, TILES * FIELDS, CELLS), F32),
        in_specs=[ANY, VM, VM, VM, VM, HBM, HBM, HBM],
        out_specs=ANY,
        scratch_shapes=[
            pltpu.VMEM(STATE, F32),
            pltpu.VMEM(STATE, F32),
            pltpu.VMEM((NB, EROWS, CELLS), F32),
            pltpu.VMEM((NB, EROWS, CELLS), F32),
            pltpu.VMEM((NB, 2 * HALO, CELLS), F32),
            pltpu.VMEM((CELLS, 3 * WIDE), BF16),
            pltpu.VMEM((XROWS, CELLS), F32),
            pltpu.VMEM((XROWS, CELLS), F32),
            pltpu.VMEM((EROWS, CELLS), F32),
            pltpu.VMEM((EROWS, CELLS), F32),
            pltpu.VMEM((TILES, PLEV, 8, CELLS), F32),
            *SMALL,
            pltpu.SemaphoreType.DMA((4,)),
            pltpu.SemaphoreType.DMA((TILES,)),
        ],
        compiler_params=pltpu.CompilerParams(vmem_limit_bytes=LIMIT),
    )(mid, edge, w, left.reshape(PAY, CELLS), right.reshape(PAY, CELLS), c, chosen, count)
    out = out.reshape(LEVELS, TILES, FIELDS, CELLS).transpose(2, 0, 1, 3)
    return out.reshape(1, FIELDS, LEVELS, TILES * CELLS)


def solution(mesh):
    in_specs = (
        P("chan", None, None, "pos"),
        P("chan", None, "pos"),
        P(),
        P(),
        P(None, "chan", "pos", None),
        P(None, "chan", "pos"),
    )
    out_specs = P("chan", None, None, "pos")
    return jax.shard_map(local, mesh=mesh, in_specs=in_specs, out_specs=out_specs, check_vma=False)
```

```python
import functools

import jax
import jax.numpy as jnp
from jax import lax
from jax.experimental import pallas as pl
from jax.experimental.pallas import tpu as pltpu
from jax.sharding import PartitionSpec as P

LEVELS = 50
FIELDS = 8
CELLS = 128
SECTIONS = 12
SWEEPS = 4
CYCLES = 2
TILES = 8
BUOYANCY = 0.4
F32 = jnp.float32
BF16 = jnp.bfloat16

BLOCKS = ((2, 0), (1, 3), (4, 6), (5, 7))
HALF = 64
HALO = CYCLES * SECTIONS
OFF = HALO + 8
OWN = TILES * CELLS
XROWS = OFF + OWN + HALO + 8
EROWS = 8 + 4 * HALO + 8
NB = len(BLOCKS)
WIDE = NB * CELLS
PLEV = 56
PAY = 464


def iota(shape, dim):
    return lax.broadcasted_iota(jnp.int32, shape, dim)


def fetch(pairs, sem):
    copies = [pltpu.make_async_copy(a, b, sem.at[i]) for i, (a, b) in enumerate(pairs)]
    for copy in copies:
        copy.start()
    return copies


def strips(ref, index, row):
    take = [ref[(*index, pl.ds(64 * g + row, 8, stride=8), slice(None))] for g in range(PLEV // 8)]
    return take + [jnp.zeros((8, CELLS), F32)]


def build_weights(lm_ref, fm_ref, q_ref, w_ref):
    q_ref[...] = jnp.zeros((CELLS, CELLS), F32)
    lm = lm_ref[...]
    q_ref[:LEVELS, :LEVELS] = lm
    q_ref[HALF : HALF + LEVELS, :LEVELS] = lm
    q_ref[...] = q_ref[...].T
    lane = iota((16, CELLS), 1)
    sub = iota((16, CELLS), 0)
    low = lane < HALF
    for r in range(0, HALF, 16):
        eye = (lane % HALF == sub + r) & (sub + r < LEVELS)
        lt = q_ref[r : r + 16, :]
        for kb, pair_k in enumerate(BLOCKS):
            for kh, g in enumerate(pair_k):
                row = CELLS * kb + HALF * kh + r
                for nb, (fa, fb) in enumerate(BLOCKS):
                    w = jnp.where(eye, jnp.where(low, fm_ref[fa, g], fm_ref[fb, g]), 0.0)
                    if g == fa:
                        w = w + jnp.where(low, lt, 0.0)
                    if g == fb:
                        w = w + jnp.where(low, 0.0, lt)
                    hi = w.astype(BF16)
                    lo = (w - hi.astype(F32)).astype(BF16)
                    cols = slice(CELLS * nb, CELLS * (nb + 1))
                    w_ref[row : row + 16, cols] = hi
                    w_ref[WIDE + row : WIDE + row + 16, cols] = hi
                    w_ref[2 * WIDE + row : 2 * WIDE + row + 16, cols] = lo


def physics(parts, w_ref, r_ref):
    total = sum(rows for _, _, rows in parts)

    def sweep(_, carry):
        at = 0
        for ref, row, rows in parts:
            for b in range(NB):
                for r in range(0, rows, 16):
                    t = jnp.tanh(ref[b, pl.ds(row + r, 16), :])
                    hi = t.astype(BF16)
                    lo = (t - hi.astype(F32)).astype(BF16)
                    r_ref[at + r : at + r + 16, CELLS * b : CELLS * (b + 1)] = hi
                    r_ref[at + r : at + r + 16, WIDE + CELLS * b : WIDE + CELLS * (b + 1)] = lo
            at += rows
        lhs = jnp.concatenate([r_ref[:total, :], r_ref[:total, :WIDE]], axis=1)
        acc = jnp.dot(lhs, w_ref[...], preferred_element_type=F32)
        at = 0
        for ref, row, rows in parts:
            for b in range(NB):
                ref[b, pl.ds(row, rows), :] += acc[at : at + rows, CELLS * b : CELLS * (b + 1)]
            at += rows
        return carry

    lax.fori_loop(0, SWEEPS, sweep, 0)


def listed_physics(ref, cycle, list_ref, count_ref, w_ref, r_ref, more=()):
    for count in range(0 if more else 1, 5):

        @pl.when(count_ref[cycle] == count)
        def _():
            rows = [pl.multiple_of(OFF + CELLS * list_ref[cycle, k], 8) for k in range(count)]
            physics([(ref, row, CELLS) for row in rows] + list(more), w_ref, r_ref)


def section(src, dst, c_ref, d_ref, kv, base, groups):
    for i in range(groups):
        row = base + 8 * i
        here, before, after = pl.ds(row, 8), pl.ds(row - 1, 8), pl.ds(row + 1, 8)
        d, cm, cp = d_ref[here, :], c_ref[before, :], c_ref[after, :]
        x = []
        for b in range(NB):
            side, coef = (before, cm) if b % 2 == 0 else (after, cp)
            x.append(d * src[b, here, :] + coef * src[b, side, :])
        x[1] = x[1] + kv * x[0]
        x[0] = x[0] - kv * x[1]
        for b in range(NB):
            dst[b, here, :] = x[b]


def transport(a_ref, b_ref, c_ref, d_ref, base, groups, unroll):
    kv = jnp.where(iota((8, CELLS), 1) < HALF, BUOYANCY, 0.0)

    def sweep(src, dst):
        def body(i, carry):
            row = pl.multiple_of(base + i * (8 * unroll), 8)
            section(src, dst, c_ref, d_ref, kv, row, unroll)
            return carry

        if groups == unroll:
            section(src, dst, c_ref, d_ref, kv, base, groups)
        else:
            lax.fori_loop(0, groups // unroll, body, 0)

    def two(_, carry):
        sweep(a_ref, b_ref)
        sweep(b_ref, a_ref)
        return carry

    lax.fori_loop(0, SECTIONS // 2, two, 0)


def put_courant(c_ref, d_ref, row, block):
    c = jnp.concatenate(block + block, axis=0).T
    c_ref[pl.ds(row, CELLS), :] = c
    d_ref[pl.ds(row, CELLS), :] = 1.0 - c


def tile_block(ref, index, pair):
    return jnp.concatenate(strips(ref, index, pair[0]) + strips(ref, index, pair[1]), axis=0).T


def pack_kernel(
    x_ref, c_hbm, list_hbm, count_hbm, first_ref, last_ref, c_ref, list_ref, count_ref, sem, lsem
):
    small = fetch(
        ((c_hbm, c_ref.at[pl.ds(0, LEVELS * TILES)]), (list_hbm, list_ref), (count_hbm, count_ref)),
        lsem,
    )
    ends = ((first_ref, 0), (last_ref, TILES - 1))
    copies = fetch(
        [(x_ref.at[:, pl.ds(8 * t, 8), :], ref.at[pl.ds(0, LEVELS)]) for ref, t in ends], sem
    )
    c_ref[LEVELS * TILES :, :] = jnp.zeros((48, CELLS), F32)
    for copy in small:
        copy.wait()
    sub = iota((8, CELLS), 0)
    for ref, t in ends:
        for g, value in enumerate(strips(c_ref, (), t)[: PLEV // 8]):
            ref[LEVELS + g] = value
        flags = []
        for cycle in range(CYCLES):
            hit = jnp.int32(0)
            for slot in range(4):
                named = (slot < count_ref[cycle]) & (list_ref[cycle, slot] == t)
                hit = jnp.where(named, jnp.int32(1), hit)
            flags.append(hit)
        ref[LEVELS + PLEV // 8] = jnp.where(sub < 4, flags[0], flags[1]).astype(F32)
    for copy in copies:
        copy.wait()


def inner_kernel(
    x_ref, c_hbm, lm_hbm, fm_hbm, list_hbm, count_hbm,
    a_ref, edge_ref, w_ref,
    n_ref, b_ref, r_ref, q_ref, cx_ref, dx_ref, c_ref, lm_ref, fm_ref, list_ref, count_ref,
    sem, xsem,
):
    lm_copy, fm_copy, c_copy, list_copy, count_copy = fetch(
        (
            (lm_hbm, lm_ref), (fm_hbm, fm_ref), (c_hbm, c_ref.at[pl.ds(0, LEVELS * TILES)]),
            (list_hbm, list_ref), (count_hbm, count_ref),
        ),
        sem,
    )
    tiles = fetch(
        [
            (x_ref.at[:, pl.ds(8 * t, 8), :], n_ref.at[t, pl.ds(0, LEVELS)])
            for t in range(TILES)
        ],
        xsem,
    )
    c_ref[LEVELS * TILES :, :] = jnp.zeros((48, CELLS), F32)
    n_ref[:, LEVELS:] = jnp.zeros((TILES, PLEV - LEVELS, 8, CELLS), F32)
    lm_copy.wait()
    fm_copy.wait()
    build_weights(lm_ref, fm_ref, q_ref, w_ref)
    c_copy.wait()
    for t in range(TILES):
        put_courant(cx_ref, dx_ref, OFF + CELLS * t, strips(c_ref, (), t))
    flat = n_ref.reshape(TILES, PLEV * 8, CELLS)
    for t, copy in enumerate(tiles):
        copy.wait()
        for b, pair in enumerate(BLOCKS):
            a_ref[b, pl.ds(OFF + CELLS * t, CELLS), :] = tile_block(flat, (t,), pair)
    list_copy.wait()
    count_copy.wait()

    listed_physics(a_ref, 0, list_ref, count_ref, w_ref, r_ref)
    edge_ref[:, 0] = a_ref[:, OFF : OFF + HALO, :]
    edge_ref[:, 1] = a_ref[:, OFF + OWN - HALO : OFF + OWN, :]
    transport(a_ref, b_ref, cx_ref, dx_ref, OFF, OWN // 8, 32)


def outer_kernel(
    in_ref, edge_ref, w_ref, left_ref, right_ref, c_hbm, list_hbm, count_hbm,
    out_ref,
    a_ref, b_ref, ea_ref, eb_ref, h_ref, r_ref, cx_ref, dx_ref, ec_ref, ed_ref, n_ref,
    c_ref, list_ref, count_ref, sem, xsem,
):
    c_copy, list_copy, count_copy, copy = fetch(
        (
            (c_hbm, c_ref.at[pl.ds(0, LEVELS * TILES)]),
            (list_hbm, list_ref), (count_hbm, count_ref), (in_ref, a_ref),
        ),
        sem,
    )
    c_ref[LEVELS * TILES :, :] = jnp.zeros((48, CELLS), F32)
    for b, pair in enumerate(BLOCKS):
        ea_ref[b, 8 : 8 + HALO, :] = tile_block(left_ref, (), pair)[CELLS - HALO :]
        ea_ref[b, 8 + HALO : 8 + 2 * HALO, :] = edge_ref[b, 0]
        ea_ref[b, 8 + 2 * HALO : 8 + 3 * HALO, :] = edge_ref[b, 1]
        ea_ref[b, 8 + 3 * HALO : 8 + 4 * HALO, :] = tile_block(right_ref, (), pair)[:HALO]

    def pay_courant(ref):
        zero = jnp.zeros((8, CELLS), F32)
        rows = [ref[pl.ds(8 * LEVELS + 8 * g, 8), :] for g in range(PLEV // 8)] + [zero]
        return jnp.concatenate(rows + rows, axis=0).T

    ends = ((0, pay_courant(left_ref)[CELLS - HALO :]), (OFF + OWN, pay_courant(right_ref)[:HALO]))
    c_copy.wait()
    for t in range(TILES):
        put_courant(cx_ref, dx_ref, OFF + CELLS * t, strips(c_ref, (), t))
    for row, c in ((OFF - HALO, ends[0][1]), (OFF + OWN, ends[1][1])):
        cx_ref[row : row + HALO, :] = c
        dx_ref[row : row + HALO, :] = 1.0 - c
    for frm, to, s in ((cx_ref, ec_ref, 0), (dx_ref, ed_ref, 0)):
        to[8 : 8 + 2 * HALO, :] = frm[OFF - HALO : OFF + HALO, :]
        to[8 + 2 * HALO : 8 + 4 * HALO, :] = frm[OFF + OWN - HALO : OFF + OWN + HALO, :]

    frow = 8 * LEVELS + PLEV
    listed = []
    for cycle in range(CYCLES):
        row = pl.ds(frow + 4 * cycle, 1)
        listed.append([jnp.max(ref[row, :]) > 0.5 for ref in (left_ref, right_ref)])

    def take_halo(ref, first, second, rows):
        h_ref[:, :rows] = ref[:, pl.ds(first, rows), :]
        h_ref[:, rows : 2 * rows] = ref[:, pl.ds(second, rows), :]

    def put_halo(ref, first, second, rows, flags):
        for flag, to, frm in ((flags[0], first, 0), (flags[1], second, rows)):

            @pl.when(flag)
            def _():
                ref[:, pl.ds(to, rows), :] = h_ref[:, frm : frm + rows]

    @pl.when(listed[0][0] | listed[0][1])
    def _():
        take_halo(ea_ref, 8, 8 + 3 * HALO, HALO)
        physics([(h_ref, 0, 2 * HALO)], w_ref, r_ref)
        put_halo(ea_ref, 8, 8 + 3 * HALO, HALO, listed[0])

    transport(ea_ref, eb_ref, ec_ref, ed_ref, 8, 4 * HALO // 8, 4 * HALO // 8)
    list_copy.wait()
    count_copy.wait()
    copy.wait()
    sub = iota((8, CELLS), 0)
    for b in range(NB):
        for row in (16, 24, 32):
            a_ref[b, row : row + 8, :] = ea_ref[b, row : row + 8, :]
        a_ref[b, 40:48, :] = jnp.where(sub < 4, ea_ref[b, 40:48, :], a_ref[b, 40:48, :])
        back = OFF + OWN - HALO - (8 + 2 * HALO)
        row = OFF + OWN - 16
        a_ref[b, row : row + 8, :] = jnp.where(
            sub >= 4, ea_ref[b, row - back : row - back + 8, :], a_ref[b, row : row + 8, :]
        )
        for row in (OFF + OWN - 8, OFF + OWN, OFF + OWN + 8):
            a_ref[b, row : row + 8, :] = ea_ref[b, row - back : row - back + 8, :]
    take_halo(a_ref, OFF - 16, OFF + OWN, 16)
    listed_physics(a_ref, 1, list_ref, count_ref, w_ref, r_ref, [(h_ref, 0, 32)])
    put_halo(a_ref, OFF - 16, OFF + OWN, 16, listed[1])
    transport(a_ref, b_ref, cx_ref, dx_ref, OFF - 16, OWN // 8 + 4, 33)
    flat = n_ref.reshape(TILES, PLEV * 8, CELLS)
    copies = []
    for t in range(TILES):
        for b, pair in enumerate(BLOCKS):
            block = a_ref[b, pl.ds(OFF + CELLS * t, CELLS), :].T
            for h, f in enumerate(pair):
                for g in range(PLEV // 8):
                    flat[t, pl.ds(64 * g + f, 8, stride=8), :] = block[
                        HALF * h + 8 * g : HALF * h + 8 * g + 8
                    ]
        copies += fetch(
            [(n_ref.at[t, pl.ds(0, LEVELS)], out_ref.at[:, pl.ds(8 * t, 8), :])],
            xsem.at[pl.ds(t, 1)],
        )
    for copy in copies:
        copy.wait()


VM = pl.BlockSpec(memory_space=pltpu.VMEM)
HBM = pl.BlockSpec(memory_space=pltpu.HBM)
ANY = pl.BlockSpec(memory_space=pl.ANY)
SMALL = [
    pltpu.VMEM((PLEV * TILES, CELLS), F32),
    pltpu.SMEM((CYCLES, 4), jnp.int32),
    pltpu.SMEM((CYCLES,), jnp.int32),
]
LIMIT = 40 << 20
STATE = (NB, XROWS, CELLS)


def local(state, courant, level_mix, field_mix, send_list, send_count):
    shape = jax.ShapeDtypeStruct
    hbm = lambda v: pltpu.with_memory_space_constraint(v, pltpu.HBM)
    x = state.reshape(FIELDS, LEVELS, TILES, CELLS).transpose(1, 2, 0, 3)
    x = hbm(x.reshape(LEVELS, TILES * FIELDS, CELLS))
    c = hbm(courant.reshape(LEVELS * TILES, CELLS))
    chosen, count = hbm(send_list.reshape(CYCLES, 4)), hbm(send_count.reshape(CYCLES))
    level_mix, field_mix = hbm(level_mix), hbm(field_mix)
    first, last = pl.pallas_call(
        pack_kernel,
        name="pack",
        out_shape=(shape((PAY // 8, 8, CELLS), F32),) * 2,
        in_specs=[HBM] * 4,
        out_specs=(VM, VM),
        scratch_shapes=SMALL + [pltpu.SemaphoreType.DMA((2,)), pltpu.SemaphoreType.DMA((3,))],
        compiler_params=pltpu.CompilerParams(vmem_limit_bytes=8 << 20),
    )(x, c, chosen, count)
    n = lax.axis_size("pos")
    left = lax.ppermute(last, "pos", [(i, (i + 1) % n) for i in range(n)])
    right = lax.ppermute(first, "pos", [((i + 1) % n, i) for i in range(n)])
    mid, edge, w = pl.pallas_call(
        inner_kernel,
        name="inner",
        out_shape=(
            shape(STATE, F32),
            shape((NB, 2, HALO, CELLS), F32),
            shape((3 * WIDE, WIDE), BF16),
        ),
        in_specs=[HBM] * 6,
        out_specs=(VM,) * 3,
        scratch_shapes=[
            pltpu.VMEM((TILES, PLEV, 8, CELLS), F32),
            pltpu.VMEM(STATE, F32),
            pltpu.VMEM((4 * CELLS + 2 * HALO, 2 * WIDE), BF16),
            pltpu.VMEM((CELLS, CELLS), F32),
            pltpu.VMEM((XROWS, CELLS), F32),
            pltpu.VMEM((XROWS, CELLS), F32),
            SMALL[0],
            pltpu.VMEM((LEVELS, LEVELS), F32),
            pltpu.SMEM((FIELDS, FIELDS), F32),
            *SMALL[1:],
            pltpu.SemaphoreType.DMA((5,)),
            pltpu.SemaphoreType.DMA((TILES,)),
        ],
        compiler_params=pltpu.CompilerParams(vmem_limit_bytes=LIMIT),
        cost_estimate=pl.CostEstimate(
            flops=4_000_000_000, bytes_accessed=8_000_000, transcendentals=0
        ),
    )(x, c, level_mix, field_mix, chosen, count)
    out = pl.pallas_call(
        outer_kernel,
        name="outer",
        out_shape=shape((LEVELS, TILES * FIELDS, CELLS), F32),
        in_specs=[ANY, VM, VM, VM, VM, HBM, HBM, HBM],
        out_specs=ANY,
        scratch_shapes=[
            pltpu.VMEM(STATE, F32),
            pltpu.VMEM(STATE, F32),
            pltpu.VMEM((NB, EROWS, CELLS), F32),
            pltpu.VMEM((NB, EROWS, CELLS), F32),
            pltpu.VMEM((NB, 2 * HALO, CELLS), F32),
            pltpu.VMEM((4 * CELLS + 2 * HALO, 2 * WIDE), BF16),
            pltpu.VMEM((XROWS, CELLS), F32),
            pltpu.VMEM((XROWS, CELLS), F32),
            pltpu.VMEM((EROWS, CELLS), F32),
            pltpu.VMEM((EROWS, CELLS), F32),
            pltpu.VMEM((TILES, PLEV, 8, CELLS), F32),
            *SMALL,
            pltpu.SemaphoreType.DMA((4,)),
            pltpu.SemaphoreType.DMA((TILES,)),
        ],
        compiler_params=pltpu.CompilerParams(vmem_limit_bytes=LIMIT),
    )(mid, edge, w, left.reshape(PAY, CELLS), right.reshape(PAY, CELLS), c, chosen, count)
    out = out.reshape(LEVELS, TILES, FIELDS, CELLS).transpose(2, 0, 1, 3)
    return out.reshape(1, FIELDS, LEVELS, TILES * CELLS)


def solution(mesh):
    in_specs = (
        P("chan", None, None, "pos"),
        P("chan", None, "pos"),
        P(),
        P(),
        P(None, "chan", "pos", None),
        P(None, "chan", "pos"),
    )
    out_specs = P("chan", None, None, "pos")
    return jax.shard_map(local, mesh=mesh, in_specs=in_specs, out_specs=out_specs, check_vma=False)
```

```python
import functools

import jax
import jax.numpy as jnp
from jax import lax
from jax.experimental import pallas as pl
from jax.experimental.pallas import tpu as pltpu
from jax.sharding import PartitionSpec as P

LEVELS = 50
FIELDS = 8
CELLS = 128
SECTIONS = 12
SWEEPS = 4
CYCLES = 2
TILES = 8
BUOYANCY = 0.4
F32 = jnp.float32
BF16 = jnp.bfloat16

BLOCKS = ((2, 0), (1, 3), (4, 6), (5, 7))
HALF = 64
HALO = CYCLES * SECTIONS
OFF = HALO + 8
OWN = TILES * CELLS
XROWS = OFF + OWN + HALO + 8
EROWS = 8 + 4 * HALO + 8
NB = len(BLOCKS)
WIDE = NB * CELLS
PLEV = 56
PAY = 464


def iota(shape, dim):
    return lax.broadcasted_iota(jnp.int32, shape, dim)


def fetch(pairs, sem):
    copies = [pltpu.make_async_copy(a, b, sem.at[i]) for i, (a, b) in enumerate(pairs)]
    for copy in copies:
        copy.start()
    return copies


def strips(ref, index, row):
    take = [ref[(*index, pl.ds(64 * g + row, 8, stride=8), slice(None))] for g in range(PLEV // 8)]
    return take + [jnp.zeros((8, CELLS), F32)]


def build_weights(lm_ref, fm_ref, q_ref, w_ref):
    q_ref[...] = jnp.zeros((CELLS, CELLS), F32)
    lm = lm_ref[...]
    q_ref[:LEVELS, :LEVELS] = lm
    q_ref[HALF : HALF + LEVELS, :LEVELS] = lm
    q_ref[...] = q_ref[...].T
    lane = iota((16, CELLS), 1)
    sub = iota((16, CELLS), 0)
    low = lane < HALF
    eyes = [(lane % HALF == sub + r) & (sub + r < LEVELS) for r in range(0, HALF, 16)]
    for kb, pair_k in enumerate(BLOCKS):
        for kh, g in enumerate(pair_k):
            for nb, (fa, fb) in enumerate(BLOCKS):
                mix = jnp.where(low, fm_ref[fa, g], fm_ref[fb, g])
                for i, eye in enumerate(eyes):
                    row = CELLS * kb + HALF * kh + 16 * i
                    w = jnp.where(eye, mix, 0.0)
                    if g in (fa, fb):
                        lt = q_ref[16 * i : 16 * i + 16, :]
                        w = w + (jnp.where(low, lt, 0.0) if g == fa else jnp.where(low, 0.0, lt))
                    hi = w.astype(BF16)
                    cols = slice(CELLS * nb, CELLS * (nb + 1))
                    w_ref[row : row + 16, cols] = hi
                    w_ref[WIDE + row : WIDE + row + 16, cols] = (w - hi.astype(F32)).astype(BF16)


def physics(parts, w_ref, r_ref):
    total = sum(rows for _, _, rows in parts)

    def sweep(_, carry):
        at = 0
        for ref, row, rows in parts:
            for b in range(NB):
                for r in range(0, rows, 16):
                    t = jnp.tanh(ref[b, pl.ds(row + r, 16), :])
                    hi = t.astype(BF16)
                    lo = (t - hi.astype(F32)).astype(BF16)
                    r_ref[at + r : at + r + 16, CELLS * b : CELLS * (b + 1)] = hi
                    r_ref[at + r : at + r + 16, WIDE + CELLS * b : WIDE + CELLS * (b + 1)] = lo
            at += rows
        lhs = jnp.concatenate([r_ref[:total, :], r_ref[:total, :WIDE]], axis=1)
        high = w_ref[:WIDE, :]
        rhs = jnp.concatenate([high, high, w_ref[WIDE:, :]], axis=0)
        acc = jnp.dot(lhs, rhs, preferred_element_type=F32)
        at = 0
        for ref, row, rows in parts:
            for b in range(NB):
                ref[b, pl.ds(row, rows), :] += acc[at : at + rows, CELLS * b : CELLS * (b + 1)]
            at += rows
        return carry

    lax.fori_loop(0, SWEEPS, sweep, 0)


def listed_physics(ref, cycle, list_ref, count_ref, w_ref, r_ref, more=()):
    for count in range(0 if more else 1, 5):

        @pl.when(count_ref[cycle] == count)
        def _():
            rows = [pl.multiple_of(OFF + CELLS * list_ref[cycle, k], 8) for k in range(count)]
            physics([(ref, row, CELLS) for row in rows] + list(more), w_ref, r_ref)


def section(src, dst, c_ref, d_ref, kv, base, groups):
    for i in range(groups):
        row = base + 8 * i
        here, before, after = pl.ds(row, 8), pl.ds(row - 1, 8), pl.ds(row + 1, 8)
        d, cm, cp = d_ref[here, :], c_ref[before, :], c_ref[after, :]
        x = []
        for b in range(NB):
            side, coef = (before, cm) if b % 2 == 0 else (after, cp)
            x.append(d * src[b, here, :] + coef * src[b, side, :])
        x[1] = x[1] + kv * x[0]
        x[0] = x[0] - kv * x[1]
        for b in range(NB):
            dst[b, here, :] = x[b]


def transport(from_ref, a_ref, b_ref, c_ref, d_ref, base, groups, unroll):
    kv = jnp.where(iota((8, CELLS), 1) < HALF, BUOYANCY, 0.0)

    def sweep(src, dst):
        def body(i, carry):
            row = pl.multiple_of(base + i * (8 * unroll), 8)
            section(src, dst, c_ref, d_ref, kv, row, unroll)
            return carry

        if groups == unroll:
            section(src, dst, c_ref, d_ref, kv, base, groups)
        else:
            lax.fori_loop(0, groups // unroll, body, 0)

    def two(_, carry):
        sweep(a_ref, b_ref)
        sweep(b_ref, a_ref)
        return carry

    if from_ref is not a_ref:
        sweep(from_ref, b_ref)
        sweep(b_ref, a_ref)
        lax.fori_loop(1, SECTIONS // 2, two, 0)
    else:
        lax.fori_loop(0, SECTIONS // 2, two, 0)


def put_courant(c_ref, d_ref, row, block):
    c = jnp.concatenate(block + block, axis=0).T
    c_ref[pl.ds(row, CELLS), :] = c
    d_ref[pl.ds(row, CELLS), :] = 1.0 - c


def tile_block(ref, index, pair):
    return jnp.concatenate(strips(ref, index, pair[0]) + strips(ref, index, pair[1]), axis=0).T


def column_kernel(
    x_ref, c_hbm, lm_hbm, fm_hbm, list_hbm, count_hbm,
    a_ref, cx_ref, dx_ref, w_ref, first_ref, last_ref,
    n_ref, r_ref, q_ref, c_ref, lm_ref, fm_ref, list_ref, count_ref, sem, xsem,
):
    lm_copy, fm_copy, c_copy, list_copy, count_copy = fetch(
        (
            (lm_hbm, lm_ref), (fm_hbm, fm_ref), (c_hbm, c_ref.at[pl.ds(0, LEVELS * TILES)]),
            (list_hbm, list_ref), (count_hbm, count_ref),
        ),
        sem,
    )
    tiles = fetch(
        [
            (x_ref.at[:, pl.ds(8 * t, 8), :], n_ref.at[t, pl.ds(0, LEVELS)])
            for t in range(TILES)
        ],
        xsem,
    )
    c_ref[LEVELS * TILES :, :] = jnp.zeros((48, CELLS), F32)
    n_ref[:, LEVELS:] = jnp.zeros((TILES, PLEV - LEVELS, 8, CELLS), F32)
    lm_copy.wait()
    fm_copy.wait()
    build_weights(lm_ref, fm_ref, q_ref, w_ref)
    c_copy.wait()
    for t in range(TILES):
        put_courant(cx_ref, dx_ref, OFF + CELLS * t, strips(c_ref, (), t))
    flat = n_ref.reshape(TILES, PLEV * 8, CELLS)
    for t, copy in enumerate(tiles):
        copy.wait()
        for b, pair in enumerate(BLOCKS):
            a_ref[b, pl.ds(OFF + CELLS * t, CELLS), :] = tile_block(flat, (t,), pair)
    list_copy.wait()
    count_copy.wait()
    listed_physics(a_ref, 0, list_ref, count_ref, w_ref, r_ref)
    for ref, row, t in ((first_ref, OFF, 0), (last_ref, OFF + OWN - HALO, TILES - 1)):
        for b in range(NB):
            ref[HALO * b : HALO * (b + 1), :] = a_ref[b, row : row + HALO, :]
        ref[HALO * NB : HALO * (NB + 1), :] = cx_ref[row : row + HALO, :]
        hit = jnp.int32(0)
        for slot in range(4):
            named = (slot < count_ref[1]) & (list_ref[1, slot] == t)
            hit = jnp.where(named, jnp.int32(1), hit)
        ref[HALO * (NB + 1) :, :] = jnp.broadcast_to(hit.astype(F32), (8, CELLS))


def inside_kernel(in_ref, cx_ref, dx_ref, out_ref, b_ref):
    transport(in_ref, out_ref, b_ref, cx_ref, dx_ref, OFF, OWN // 8, 64)


def finish_kernel(
    a_in, cx_in, dx_in, w_ref, first_ref, last_ref, left_ref, right_ref, list_hbm, count_hbm,
    out_ref, a_ref, cx_ref, dx_ref,
    b_ref, ea_ref, eb_ref, h_ref, r_ref, ec_ref, ed_ref, n_ref, list_ref, count_ref, sem, xsem,
):
    list_copy, count_copy = fetch(((list_hbm, list_ref), (count_hbm, count_ref)), sem)
    parts = (left_ref, first_ref, last_ref, right_ref)
    for i, ref in enumerate(parts):
        rows = slice(8 + HALO * i, 8 + HALO * (i + 1))
        for b in range(NB):
            ea_ref[b, rows, :] = ref[HALO * b : HALO * (b + 1), :]
        c = ref[HALO * NB : HALO * (NB + 1), :]
        ec_ref[rows, :] = c
        ed_ref[rows, :] = 1.0 - c
    for ref, row in ((left_ref, OFF - HALO), (right_ref, OFF + OWN)):
        c = ref[HALO * NB : HALO * (NB + 1), :]
        cx_ref[row : row + HALO, :] = c
        dx_ref[row : row + HALO, :] = 1.0 - c
    flags = [jnp.max(ref[HALO * (NB + 1) :, :]) > 0.5 for ref in (left_ref, right_ref)]
    transport(ea_ref, ea_ref, eb_ref, ec_ref, ed_ref, 8, 4 * HALO // 8, 4 * HALO // 8)
    sub = iota((8, CELLS), 0)
    for b in range(NB):
        for row in (16, 24, 32):
            a_ref[b, row : row + 8, :] = ea_ref[b, row : row + 8, :]
        a_ref[b, 40:48, :] = jnp.where(sub < 4, ea_ref[b, 40:48, :], a_ref[b, 40:48, :])
        back = OFF + OWN - HALO - (8 + 2 * HALO)
        row = OFF + OWN - 16
        a_ref[b, row : row + 8, :] = jnp.where(
            sub >= 4, ea_ref[b, row - back : row - back + 8, :], a_ref[b, row : row + 8, :]
        )
        for row in (OFF + OWN - 8, OFF + OWN, OFF + OWN + 8):
            a_ref[b, row : row + 8, :] = ea_ref[b, row - back : row - back + 8, :]
    list_copy.wait()
    count_copy.wait()
    near = (OFF - 16, OFF + OWN)
    for i, row in enumerate(near):
        h_ref[:, 16 * i : 16 * i + 16] = a_ref[:, row : row + 16, :]
    listed_physics(a_ref, 1, list_ref, count_ref, w_ref, r_ref, [(h_ref, 0, 32)])
    for i, row in enumerate(near):

        @pl.when(flags[i])
        def _():
            a_ref[:, row : row + 16, :] = h_ref[:, 16 * i : 16 * i + 16]

    transport(a_ref, a_ref, b_ref, cx_ref, dx_ref, OFF - 16, OWN // 8 + 4, 66)
    flat = n_ref.reshape(TILES, PLEV * 8, CELLS)
    copies = []
    for t in range(TILES):
        for b, pair in enumerate(BLOCKS):
            block = a_ref[b, pl.ds(OFF + CELLS * t, CELLS), :].T
            for h, f in enumerate(pair):
                for g in range(PLEV // 8):
                    flat[t, pl.ds(64 * g + f, 8, stride=8), :] = block[
                        HALF * h + 8 * g : HALF * h + 8 * g + 8
                    ]
        copies += fetch(
            [(n_ref.at[t, pl.ds(0, LEVELS)], out_ref.at[:, pl.ds(8 * t, 8), :])],
            xsem.at[pl.ds(t, 1)],
        )
    for copy in copies:
        copy.wait()


VM = pl.BlockSpec(memory_space=pltpu.VMEM)
HBM = pl.BlockSpec(memory_space=pltpu.HBM)
ANY = pl.BlockSpec(memory_space=pl.ANY)
SMALL = [
    pltpu.VMEM((PLEV * TILES, CELLS), F32),
    pltpu.SMEM((CYCLES, 4), jnp.int32),
    pltpu.SMEM((CYCLES,), jnp.int32),
]
LIMIT = 40 << 20
STATE = (NB, XROWS, CELLS)
COLUMN = (XROWS, CELLS)
ENDS = (HALO * (NB + 1) + 8, CELLS)
BATCH = pltpu.VMEM((4 * CELLS + 32, 2 * WIDE), BF16)
NATURAL = pltpu.VMEM((TILES, PLEV, 8, CELLS), F32)


def local(state, courant, level_mix, field_mix, send_list, send_count):
    shape = jax.ShapeDtypeStruct
    hbm = lambda v: pltpu.with_memory_space_constraint(v, pltpu.HBM)
    x = state.reshape(FIELDS, LEVELS, TILES, CELLS).transpose(1, 2, 0, 3)
    x = hbm(x.reshape(LEVELS, TILES * FIELDS, CELLS))
    c = hbm(courant.reshape(LEVELS * TILES, CELLS))
    chosen, count = hbm(send_list.reshape(CYCLES, 4)), hbm(send_count.reshape(CYCLES))
    a, cx, dx, w, first, last = pl.pallas_call(
        column_kernel,
        name="column",
        out_shape=(
            shape(STATE, F32), shape(COLUMN, F32), shape(COLUMN, F32),
            shape((2 * WIDE, WIDE), BF16), shape(ENDS, F32), shape(ENDS, F32),
        ),
        in_specs=[HBM] * 6,
        out_specs=(VM,) * 6,
        scratch_shapes=[
            NATURAL,
            BATCH,
            pltpu.VMEM((CELLS, CELLS), F32),
            SMALL[0],
            pltpu.VMEM((LEVELS, LEVELS), F32),
            pltpu.SMEM((FIELDS, FIELDS), F32),
            *SMALL[1:],
            pltpu.SemaphoreType.DMA((5,)),
            pltpu.SemaphoreType.DMA((TILES,)),
        ],
        compiler_params=pltpu.CompilerParams(vmem_limit_bytes=LIMIT),
    )(x, c, hbm(level_mix), hbm(field_mix), chosen, count)
    n = lax.axis_size("pos")
    left = lax.ppermute(last, "pos", [(i, (i + 1) % n) for i in range(n)])
    right = lax.ppermute(first, "pos", [((i + 1) % n, i) for i in range(n)])
    mid = pl.pallas_call(
        inside_kernel,
        name="inside",
        out_shape=shape(STATE, F32),
        in_specs=[VM] * 3,
        out_specs=VM,
        scratch_shapes=[pltpu.VMEM(STATE, F32)],
        compiler_params=pltpu.CompilerParams(vmem_limit_bytes=LIMIT),
        cost_estimate=pl.CostEstimate(
            flops=4_000_000_000, bytes_accessed=8_000_000, transcendentals=0
        ),
    )(a, cx, dx)
    out, *_ = pl.pallas_call(
        finish_kernel,
        name="finish",
        out_shape=(
            shape((LEVELS, TILES * FIELDS, CELLS), F32),
            shape(STATE, F32), shape(COLUMN, F32), shape(COLUMN, F32),
        ),
        in_specs=[VM] * 8 + [HBM] * 2,
        out_specs=(ANY, VM, VM, VM),
        input_output_aliases={0: 1, 1: 2, 2: 3},
        scratch_shapes=[
            pltpu.VMEM(STATE, F32),
            pltpu.VMEM((NB, EROWS, CELLS), F32),
            pltpu.VMEM((NB, EROWS, CELLS), F32),
            pltpu.VMEM((NB, 32, CELLS), F32),
            BATCH,
            pltpu.VMEM((EROWS, CELLS), F32),
            pltpu.VMEM((EROWS, CELLS), F32),
            NATURAL,
            *SMALL[1:],
            pltpu.SemaphoreType.DMA((2,)),
            pltpu.SemaphoreType.DMA((TILES,)),
        ],
        compiler_params=pltpu.CompilerParams(vmem_limit_bytes=LIMIT),
    )(mid, cx, dx, w, first, last, left, right, chosen, count)
    out = out.reshape(LEVELS, TILES, FIELDS, CELLS).transpose(2, 0, 1, 3)
    return out.reshape(1, FIELDS, LEVELS, TILES * CELLS)


def solution(mesh):
    in_specs = (
        P("chan", None, None, "pos"),
        P("chan", None, "pos"),
        P(),
        P(),
        P(None, "chan", "pos", None),
        P(None, "chan", "pos"),
    )
    out_specs = P("chan", None, None, "pos")
    return jax.shard_map(local, mesh=mesh, in_specs=in_specs, out_specs=out_specs, check_vma=False)
```

```python
import functools

import jax
import jax.numpy as jnp
from jax import lax
from jax.experimental import pallas as pl
from jax.experimental.pallas import tpu as pltpu
from jax.sharding import PartitionSpec as P

LEVELS = 50
FIELDS = 8
CELLS = 128
SECTIONS = 12
SWEEPS = 4
CYCLES = 2
TILES = 8
BUOYANCY = 0.4
F32 = jnp.float32
BF16 = jnp.bfloat16

BLOCKS = ((2, 0), (1, 3), (4, 6), (5, 7))
HALF = 64
HALO = CYCLES * SECTIONS
OFF = HALO + 8
OWN = TILES * CELLS
XROWS = OFF + OWN + HALO + 8
EROWS = 8 + 4 * HALO + 8
NB = len(BLOCKS)
WIDE = NB * CELLS
PLEV = 56
PAY = 464


def iota(shape, dim):
    return lax.broadcasted_iota(jnp.int32, shape, dim)


def fetch(pairs, sem):
    copies = [pltpu.make_async_copy(a, b, sem.at[i]) for i, (a, b) in enumerate(pairs)]
    for copy in copies:
        copy.start()
    return copies


def strips(ref, index, row):
    take = [ref[(*index, pl.ds(64 * g + row, 8, stride=8), slice(None))] for g in range(PLEV // 8)]
    return take + [jnp.zeros((8, CELLS), F32)]


def build_weights(lm_ref, fm_ref, q_ref, w_ref):
    q_ref[...] = jnp.zeros((CELLS, CELLS), F32)
    lm = lm_ref[...]
    q_ref[:LEVELS, :LEVELS] = lm
    q_ref[HALF : HALF + LEVELS, :LEVELS] = lm
    q_ref[...] = q_ref[...].T
    lane = iota((16, CELLS), 1)
    sub = iota((16, CELLS), 0)
    low = lane < HALF
    eyes = [(lane % HALF == sub + r) & (sub + r < LEVELS) for r in range(0, HALF, 16)]
    for kb, pair_k in enumerate(BLOCKS):
        for kh, g in enumerate(pair_k):
            for nb, (fa, fb) in enumerate(BLOCKS):
                mix = jnp.where(low, fm_ref[fa, g], fm_ref[fb, g])
                for i, eye in enumerate(eyes):
                    row = CELLS * kb + HALF * kh + 16 * i
                    w = jnp.where(eye, mix, 0.0)
                    if g in (fa, fb):
                        lt = q_ref[16 * i : 16 * i + 16, :]
                        w = w + (jnp.where(low, lt, 0.0) if g == fa else jnp.where(low, 0.0, lt))
                    hi = w.astype(BF16)
                    cols = slice(CELLS * nb, CELLS * (nb + 1))
                    w_ref[row : row + 16, cols] = hi
                    w_ref[WIDE + row : WIDE + row + 16, cols] = (w - hi.astype(F32)).astype(BF16)


def physics(parts, w_ref, r_ref):
    total = sum(rows for _, _, rows in parts)

    def sweep(_, carry):
        at = 0
        for ref, row, rows in parts:
            for b in range(NB):
                for r in range(0, rows, 16):
                    t = jnp.tanh(ref[b, pl.ds(row + r, 16), :])
                    hi = t.astype(BF16)
                    lo = (t - hi.astype(F32)).astype(BF16)
                    r_ref[at + r : at + r + 16, CELLS * b : CELLS * (b + 1)] = hi
                    r_ref[at + r : at + r + 16, WIDE + CELLS * b : WIDE + CELLS * (b + 1)] = lo
            at += rows
        lhs = jnp.concatenate([r_ref[:total, :], r_ref[:total, :WIDE]], axis=1)
        high = w_ref[:WIDE, :]
        rhs = jnp.concatenate([high, high, w_ref[WIDE:, :]], axis=0)
        acc = jnp.dot(lhs, rhs, preferred_element_type=F32)
        at = 0
        for ref, row, rows in parts:
            for b in range(NB):
                ref[b, pl.ds(row, rows), :] += acc[at : at + rows, CELLS * b : CELLS * (b + 1)]
            at += rows
        return carry

    lax.fori_loop(0, SWEEPS, sweep, 0)


def listed_physics(ref, cycle, list_ref, count_ref, w_ref, r_ref):
    for count in range(1, 5):

        @pl.when(count_ref[cycle] == count)
        def _():
            rows = [pl.multiple_of(OFF + CELLS * list_ref[cycle, k], 8) for k in range(count)]
            physics([(ref, row, CELLS) for row in rows], w_ref, r_ref)


def section(src, dst, c_ref, d_ref, kv, base, groups):
    for i in range(groups):
        row = base + 8 * i
        here, before, after = pl.ds(row, 8), pl.ds(row - 1, 8), pl.ds(row + 1, 8)
        d, cm, cp = d_ref[here, :], c_ref[before, :], c_ref[after, :]
        x = []
        for b in range(NB):
            side, coef = (before, cm) if b % 2 == 0 else (after, cp)
            x.append(d * src[b, here, :] + coef * src[b, side, :])
        x[1] = x[1] + kv * x[0]
        x[0] = x[0] - kv * x[1]
        for b in range(NB):
            dst[b, here, :] = x[b]


def transport(from_ref, a_ref, b_ref, c_ref, d_ref, base, groups, unroll):
    kv = jnp.where(iota((8, CELLS), 1) < HALF, BUOYANCY, 0.0)

    def sweep(src, dst):
        def body(i, carry):
            row = pl.multiple_of(base + i * (8 * unroll), 8)
            section(src, dst, c_ref, d_ref, kv, row, unroll)
            return carry

        if groups == unroll:
            section(src, dst, c_ref, d_ref, kv, base, groups)
        else:
            lax.fori_loop(0, groups // unroll, body, 0)

    def two(_, carry):
        sweep(a_ref, b_ref)
        sweep(b_ref, a_ref)
        return carry

    if from_ref is not a_ref:
        sweep(from_ref, b_ref)
        sweep(b_ref, a_ref)
        lax.fori_loop(1, SECTIONS // 2, two, 0)
    else:
        lax.fori_loop(0, SECTIONS // 2, two, 0)


def put_courant(c_ref, d_ref, row, block):
    c = jnp.concatenate(block + block, axis=0).T
    c_ref[pl.ds(row, CELLS), :] = c
    d_ref[pl.ds(row, CELLS), :] = 1.0 - c


def tile_block(ref, index, pair):
    return jnp.concatenate(strips(ref, index, pair[0]) + strips(ref, index, pair[1]), axis=0).T


def column_kernel(
    x_ref, c_hbm, lm_hbm, fm_hbm, list_hbm, count_hbm,
    a_ref, cx_ref, dx_ref, w_ref, first_ref, last_ref,
    n_ref, r_ref, q_ref, c_ref, lm_ref, fm_ref, list_ref, count_ref, sem, xsem,
):
    lm_copy, fm_copy, c_copy, list_copy, count_copy = fetch(
        (
            (lm_hbm, lm_ref), (fm_hbm, fm_ref), (c_hbm, c_ref.at[pl.ds(0, LEVELS * TILES)]),
            (list_hbm, list_ref), (count_hbm, count_ref),
        ),
        sem,
    )
    tiles = fetch(
        [
            (x_ref.at[:, pl.ds(8 * t, 8), :], n_ref.at[t, pl.ds(0, LEVELS)])
            for t in range(TILES)
        ],
        xsem,
    )
    c_ref[LEVELS * TILES :, :] = jnp.zeros((48, CELLS), F32)
    n_ref[:, LEVELS:] = jnp.zeros((TILES, PLEV - LEVELS, 8, CELLS), F32)
    lm_copy.wait()
    fm_copy.wait()
    build_weights(lm_ref, fm_ref, q_ref, w_ref)
    c_copy.wait()
    for t in range(TILES):
        put_courant(cx_ref, dx_ref, OFF + CELLS * t, strips(c_ref, (), t))
    flat = n_ref.reshape(TILES, PLEV * 8, CELLS)
    for t, copy in enumerate(tiles):
        copy.wait()
        for b, pair in enumerate(BLOCKS):
            a_ref[b, pl.ds(OFF + CELLS * t, CELLS), :] = tile_block(flat, (t,), pair)
    list_copy.wait()
    count_copy.wait()
    listed_physics(a_ref, 0, list_ref, count_ref, w_ref, r_ref)
    for ref, row, t in ((first_ref, OFF, 0), (last_ref, OFF + OWN - HALO, TILES - 1)):
        for b in range(NB):
            ref[HALO * b : HALO * (b + 1), :] = a_ref[b, row : row + HALO, :]
        ref[HALO * NB : HALO * (NB + 1), :] = cx_ref[row : row + HALO, :]
        hit = jnp.int32(0)
        for slot in range(4):
            named = (slot < count_ref[1]) & (list_ref[1, slot] == t)
            hit = jnp.where(named, jnp.int32(1), hit)
        ref[HALO * (NB + 1) :, :] = jnp.broadcast_to(hit.astype(F32), (8, CELLS))


def inside_kernel(
    in_ref, cx_ref, dx_ref, w_ref, list_hbm, count_hbm,
    out_ref,
    b_ref, r_ref, list_ref, count_ref, sem,
):
    copies = fetch(((list_hbm, list_ref), (count_hbm, count_ref)), sem)
    transport(in_ref, out_ref, b_ref, cx_ref, dx_ref, OFF, OWN // 8, 64)
    for copy in copies:
        copy.wait()
    listed_physics(out_ref, 1, list_ref, count_ref, w_ref, r_ref)


def finish_kernel(
    a_in, cx_in, dx_in, w_ref, first_ref, last_ref, left_ref, right_ref,
    out_ref, a_ref, cx_ref, dx_ref,
    b_ref, ea_ref, eb_ref, h_ref, r_ref, ec_ref, ed_ref, n_ref, xsem,
):
    parts = (left_ref, first_ref, last_ref, right_ref)
    for i, ref in enumerate(parts):
        rows = slice(8 + HALO * i, 8 + HALO * (i + 1))
        for b in range(NB):
            ea_ref[b, rows, :] = ref[HALO * b : HALO * (b + 1), :]
        c = ref[HALO * NB : HALO * (NB + 1), :]
        ec_ref[rows, :] = c
        ed_ref[rows, :] = 1.0 - c
    for ref, row in ((left_ref, OFF - HALO), (right_ref, OFF + OWN)):
        c = ref[HALO * NB : HALO * (NB + 1), :]
        cx_ref[row : row + HALO, :] = c
        dx_ref[row : row + HALO, :] = 1.0 - c
    flags = [jnp.max(ref[HALO * (NB + 1) :, :]) > 0.5 for ref in parts]
    transport(ea_ref, ea_ref, eb_ref, ec_ref, ed_ref, 8, 4 * HALO // 8, 4 * HALO // 8)
    near = [8 + HALO - 16, 8 + HALO, 8 + 3 * HALO - 16, 8 + 3 * HALO]

    @pl.when(flags[0] | flags[1] | flags[2] | flags[3])
    def _():
        for i, row in enumerate(near):
            h_ref[:, 16 * i : 16 * i + 16] = ea_ref[:, row : row + 16, :]
        physics([(h_ref, 0, 64)], w_ref, r_ref)
        for i, row in enumerate(near):

            @pl.when(flags[i])
            def _():
                ea_ref[:, row : row + 16, :] = h_ref[:, 16 * i : 16 * i + 16]

    sub = iota((8, CELLS), 0)
    for b in range(NB):
        for row in (16, 24, 32):
            a_ref[b, row : row + 8, :] = ea_ref[b, row : row + 8, :]
        a_ref[b, 40:48, :] = jnp.where(sub < 4, ea_ref[b, 40:48, :], a_ref[b, 40:48, :])
        back = OFF + OWN - HALO - (8 + 2 * HALO)
        row = OFF + OWN - 16
        a_ref[b, row : row + 8, :] = jnp.where(
            sub >= 4, ea_ref[b, row - back : row - back + 8, :], a_ref[b, row : row + 8, :]
        )
        for row in (OFF + OWN - 8, OFF + OWN, OFF + OWN + 8):
            a_ref[b, row : row + 8, :] = ea_ref[b, row - back : row - back + 8, :]
    transport(a_ref, a_ref, b_ref, cx_ref, dx_ref, OFF - 16, OWN // 8 + 4, 66)
    flat = n_ref.reshape(TILES, PLEV * 8, CELLS)
    copies = []
    for t in range(TILES):
        for b, pair in enumerate(BLOCKS):
            block = a_ref[b, pl.ds(OFF + CELLS * t, CELLS), :].T
            for h, f in enumerate(pair):
                for g in range(PLEV // 8):
                    flat[t, pl.ds(64 * g + f, 8, stride=8), :] = block[
                        HALF * h + 8 * g : HALF * h + 8 * g + 8
                    ]
        copies += fetch(
            [(n_ref.at[t, pl.ds(0, LEVELS)], out_ref.at[:, pl.ds(8 * t, 8), :])],
            xsem.at[pl.ds(t, 1)],
        )
    for copy in copies:
        copy.wait()


VM = pl.BlockSpec(memory_space=pltpu.VMEM)
HBM = pl.BlockSpec(memory_space=pltpu.HBM)
ANY = pl.BlockSpec(memory_space=pl.ANY)
SMALL = [
    pltpu.VMEM((PLEV * TILES, CELLS), F32),
    pltpu.SMEM((CYCLES, 4), jnp.int32),
    pltpu.SMEM((CYCLES,), jnp.int32),
]
LIMIT = 40 << 20
STATE = (NB, XROWS, CELLS)
COLUMN = (XROWS, CELLS)
ENDS = (HALO * (NB + 1) + 8, CELLS)
BATCH = pltpu.VMEM((4 * CELLS, 2 * WIDE), BF16)
NATURAL = pltpu.VMEM((TILES, PLEV, 8, CELLS), F32)


def local(state, courant, level_mix, field_mix, send_list, send_count):
    shape = jax.ShapeDtypeStruct
    hbm = lambda v: pltpu.with_memory_space_constraint(v, pltpu.HBM)
    x = state.reshape(FIELDS, LEVELS, TILES, CELLS).transpose(1, 2, 0, 3)
    x = hbm(x.reshape(LEVELS, TILES * FIELDS, CELLS))
    c = hbm(courant.reshape(LEVELS * TILES, CELLS))
    chosen, count = hbm(send_list.reshape(CYCLES, 4)), hbm(send_count.reshape(CYCLES))
    a, cx, dx, w, first, last = pl.pallas_call(
        column_kernel,
        name="column",
        out_shape=(
            shape(STATE, F32), shape(COLUMN, F32), shape(COLUMN, F32),
            shape((2 * WIDE, WIDE), BF16), shape(ENDS, F32), shape(ENDS, F32),
        ),
        in_specs=[HBM] * 6,
        out_specs=(VM,) * 6,
        scratch_shapes=[
            NATURAL,
            BATCH,
            pltpu.VMEM((CELLS, CELLS), F32),
            SMALL[0],
            pltpu.VMEM((LEVELS, LEVELS), F32),
            pltpu.SMEM((FIELDS, FIELDS), F32),
            *SMALL[1:],
            pltpu.SemaphoreType.DMA((5,)),
            pltpu.SemaphoreType.DMA((TILES,)),
        ],
        compiler_params=pltpu.CompilerParams(vmem_limit_bytes=LIMIT),
    )(x, c, hbm(level_mix), hbm(field_mix), chosen, count)
    n = lax.axis_size("pos")
    left = lax.ppermute(last, "pos", [(i, (i + 1) % n) for i in range(n)])
    right = lax.ppermute(first, "pos", [((i + 1) % n, i) for i in range(n)])
    mid = pl.pallas_call(
        inside_kernel,
        name="inside",
        out_shape=shape(STATE, F32),
        in_specs=[VM] * 4 + [HBM] * 2,
        out_specs=VM,
        scratch_shapes=[
            pltpu.VMEM(STATE, F32), BATCH, *SMALL[1:], pltpu.SemaphoreType.DMA((2,))
        ],
        compiler_params=pltpu.CompilerParams(vmem_limit_bytes=LIMIT),
        cost_estimate=pl.CostEstimate(
            flops=4_000_000_000, bytes_accessed=8_000_000, transcendentals=0
        ),
    )(a, cx, dx, w, chosen, count)
    out, *_ = pl.pallas_call(
        finish_kernel,
        name="finish",
        out_shape=(
            shape((LEVELS, TILES * FIELDS, CELLS), F32),
            shape(STATE, F32), shape(COLUMN, F32), shape(COLUMN, F32),
        ),
        in_specs=[VM] * 8,
        out_specs=(ANY, VM, VM, VM),
        input_output_aliases={0: 1, 1: 2, 2: 3},
        scratch_shapes=[
            pltpu.VMEM(STATE, F32),
            pltpu.VMEM((NB, EROWS, CELLS), F32),
            pltpu.VMEM((NB, EROWS, CELLS), F32),
            pltpu.VMEM((NB, 64, CELLS), F32),
            pltpu.VMEM((64, 2 * WIDE), BF16),
            pltpu.VMEM((EROWS, CELLS), F32),
            pltpu.VMEM((EROWS, CELLS), F32),
            NATURAL,
            pltpu.SemaphoreType.DMA((TILES,)),
        ],
        compiler_params=pltpu.CompilerParams(vmem_limit_bytes=LIMIT),
    )(mid, cx, dx, w, first, last, left, right)
    out = out.reshape(LEVELS, TILES, FIELDS, CELLS).transpose(2, 0, 1, 3)
    return out.reshape(1, FIELDS, LEVELS, TILES * CELLS)


def solution(mesh):
    in_specs = (
        P("chan", None, None, "pos"),
        P("chan", None, "pos"),
        P(),
        P(),
        P(None, "chan", "pos", None),
        P(None, "chan", "pos"),
    )
    out_specs = P("chan", None, None, "pos")
    return jax.shard_map(local, mesh=mesh, in_specs=in_specs, out_specs=out_specs, check_vma=False)
```

```python
import functools

import jax
import jax.numpy as jnp
from jax import lax
from jax.experimental import pallas as pl
from jax.experimental.pallas import tpu as pltpu
from jax.sharding import PartitionSpec as P

LEVELS = 50
FIELDS = 8
CELLS = 128
SECTIONS = 12
SWEEPS = 4
CYCLES = 2
TILES = 8
BUOYANCY = 0.4
F32 = jnp.float32
BF16 = jnp.bfloat16

BLOCKS = ((2, 0), (1, 3), (4, 6), (5, 7))
HALF = 64
HALO = CYCLES * SECTIONS
OFF = HALO + 8
OWN = TILES * CELLS
XROWS = OFF + OWN + HALO + 8
EROWS = 8 + 4 * HALO + 8
NB = len(BLOCKS)
WIDE = NB * CELLS
PLEV = 56
PAY = 464


def iota(shape, dim):
    return lax.broadcasted_iota(jnp.int32, shape, dim)


def fetch(pairs, sem):
    copies = [pltpu.make_async_copy(a, b, sem.at[i]) for i, (a, b) in enumerate(pairs)]
    for copy in copies:
        copy.start()
    return copies


def strips(ref, index, row):
    take = [ref[(*index, pl.ds(64 * g + row, 8, stride=8), slice(None))] for g in range(PLEV // 8)]
    return take + [jnp.zeros((8, CELLS), F32)]


def build_weights(lm_ref, fm_ref, q_ref, w_ref):
    q_ref[...] = jnp.zeros((CELLS, CELLS), F32)
    lm = lm_ref[...]
    q_ref[:LEVELS, :LEVELS] = lm
    q_ref[HALF : HALF + LEVELS, :LEVELS] = lm
    q_ref[...] = q_ref[...].T
    lane = iota((16, CELLS), 1)
    sub = iota((16, CELLS), 0)
    low = lane < HALF
    eyes = [(lane % HALF == sub + r) & (sub + r < LEVELS) for r in range(0, HALF, 16)]
    for kb, pair_k in enumerate(BLOCKS):
        for kh, g in enumerate(pair_k):
            for nb, (fa, fb) in enumerate(BLOCKS):
                mix = jnp.where(low, fm_ref[fa, g], fm_ref[fb, g])
                for i, eye in enumerate(eyes):
                    row = CELLS * kb + HALF * kh + 16 * i
                    w = jnp.where(eye, mix, 0.0)
                    if g in (fa, fb):
                        lt = q_ref[16 * i : 16 * i + 16, :]
                        w = w + (jnp.where(low, lt, 0.0) if g == fa else jnp.where(low, 0.0, lt))
                    hi = w.astype(BF16)
                    cols = slice(CELLS * nb, CELLS * (nb + 1))
                    w_ref[row : row + 16, cols] = hi
                    w_ref[WIDE + row : WIDE + row + 16, cols] = (w - hi.astype(F32)).astype(BF16)


def physics(parts, w_ref, r_ref):
    total = sum(rows for _, _, rows in parts)

    def sweep(_, carry):
        at = 0
        for ref, row, rows in parts:
            for b in range(NB):
                for r in range(0, rows, 16):
                    t = jnp.tanh(ref[b, pl.ds(row + r, 16), :])
                    hi = t.astype(BF16)
                    lo = (t - hi.astype(F32)).astype(BF16)
                    r_ref[at + r : at + r + 16, CELLS * b : CELLS * (b + 1)] = hi
                    r_ref[at + r : at + r + 16, WIDE + CELLS * b : WIDE + CELLS * (b + 1)] = lo
            at += rows
        lhs = jnp.concatenate([r_ref[:total, :], r_ref[:total, :WIDE]], axis=1)
        high = w_ref[:WIDE, :]
        rhs = jnp.concatenate([high, high, w_ref[WIDE:, :]], axis=0)
        acc = jnp.dot(lhs, rhs, preferred_element_type=F32)
        at = 0
        for ref, row, rows in parts:
            for b in range(NB):
                ref[b, pl.ds(row, rows), :] += acc[at : at + rows, CELLS * b : CELLS * (b + 1)]
            at += rows
        return carry

    lax.fori_loop(0, SWEEPS, sweep, 0)


def listed_physics(ref, cycle, list_ref, count_ref, w_ref, r_ref):
    for count in range(1, 5):

        @pl.when(count_ref[cycle] == count)
        def _():
            rows = [pl.multiple_of(OFF + CELLS * list_ref[cycle, k], 8) for k in range(count)]
            physics([(ref, row, CELLS) for row in rows], w_ref, r_ref)


def section(src, dst, c_ref, d_ref, kv, base, groups):
    for i in range(groups):
        row = base + 8 * i
        here, before, after = pl.ds(row, 8), pl.ds(row - 1, 8), pl.ds(row + 1, 8)
        d, cm, cp = d_ref[here, :], c_ref[before, :], c_ref[after, :]
        x = []
        for b in range(NB):
            side, coef = (before, cm) if b % 2 == 0 else (after, cp)
            x.append(d * src[b, here, :] + coef * src[b, side, :])
        x[1] = x[1] + kv * x[0]
        x[0] = x[0] - kv * x[1]
        for b in range(NB):
            dst[b, here, :] = x[b]


def transport(from_ref, a_ref, b_ref, c_ref, d_ref, base, groups, unroll):
    kv = jnp.where(iota((8, CELLS), 1) < HALF, BUOYANCY, 0.0)

    def sweep(src, dst):
        def body(i, carry):
            row = pl.multiple_of(base + i * (8 * unroll), 8)
            section(src, dst, c_ref, d_ref, kv, row, unroll)
            return carry

        if groups == unroll:
            section(src, dst, c_ref, d_ref, kv, base, groups)
        else:
            lax.fori_loop(0, groups // unroll, body, 0)

    def two(_, carry):
        sweep(a_ref, b_ref)
        sweep(b_ref, a_ref)
        return carry

    if from_ref is not a_ref:
        sweep(from_ref, b_ref)
        sweep(b_ref, a_ref)
        lax.fori_loop(1, SECTIONS // 2, two, 0)
    else:
        lax.fori_loop(0, SECTIONS // 2, two, 0)


def put_courant(c_ref, d_ref, row, block):
    c = jnp.concatenate(block + block, axis=0).T
    c_ref[pl.ds(row, CELLS), :] = c
    d_ref[pl.ds(row, CELLS), :] = 1.0 - c


def tile_block(ref, index, pair):
    return jnp.concatenate(strips(ref, index, pair[0]) + strips(ref, index, pair[1]), axis=0).T


def column_kernel(
    x_ref, c_hbm, lm_hbm, fm_hbm, list_hbm, count_hbm,
    a_ref, cx_ref, dx_ref, w_ref, first_ref, last_ref, near_ref, far_ref,
    n_ref, r_ref, q_ref, c_ref, lm_ref, fm_ref, list_ref, count_ref, sem, xsem,
):
    lm_copy, fm_copy, c_copy, list_copy, count_copy = fetch(
        (
            (lm_hbm, lm_ref), (fm_hbm, fm_ref), (c_hbm, c_ref.at[pl.ds(0, LEVELS * TILES)]),
            (list_hbm, list_ref), (count_hbm, count_ref),
        ),
        sem,
    )
    tiles = fetch(
        [
            (x_ref.at[:, pl.ds(8 * t, 8), :], n_ref.at[t, pl.ds(0, LEVELS)])
            for t in range(TILES)
        ],
        xsem,
    )
    c_ref[LEVELS * TILES :, :] = jnp.zeros((48, CELLS), F32)
    n_ref[:, LEVELS:] = jnp.zeros((TILES, PLEV - LEVELS, 8, CELLS), F32)
    lm_copy.wait()
    fm_copy.wait()
    build_weights(lm_ref, fm_ref, q_ref, w_ref)
    c_copy.wait()
    for t in range(TILES):
        put_courant(cx_ref, dx_ref, OFF + CELLS * t, strips(c_ref, (), t))
    flat = n_ref.reshape(TILES, PLEV * 8, CELLS)
    for t, copy in enumerate(tiles):
        copy.wait()
        for b, pair in enumerate(BLOCKS):
            a_ref[b, pl.ds(OFF + CELLS * t, CELLS), :] = tile_block(flat, (t,), pair)
    list_copy.wait()
    count_copy.wait()
    listed_physics(a_ref, 0, list_ref, count_ref, w_ref, r_ref)
    for ref, row, t in ((first_ref, OFF, 0), (last_ref, OFF + OWN - HALO, TILES - 1)):
        for b in range(NB):
            ref[HALO * b : HALO * (b + 1), :] = a_ref[b, row : row + HALO, :]
        ref[HALO * NB : HALO * (NB + 1), :] = cx_ref[row : row + HALO, :]
        hit = jnp.int32(0)
        for slot in range(4):
            named = (slot < count_ref[1]) & (list_ref[1, slot] == t)
            hit = jnp.where(named, jnp.int32(1), hit)
        ref[HALO * (NB + 1) :, :] = jnp.broadcast_to(hit.astype(F32), (8, CELLS))
    odd = lax.axis_index("pos") % 2 == 1

    @pl.when(odd)
    def _():
        near_ref[...] = first_ref[...]
        far_ref[...] = last_ref[...]

    @pl.when(jnp.logical_not(odd))
    def _():
        near_ref[...] = last_ref[...]
        far_ref[...] = first_ref[...]


def inside_kernel(
    in_ref, cx_ref, dx_ref, w_ref, list_hbm, count_hbm,
    out_ref,
    b_ref, r_ref, list_ref, count_ref, sem,
):
    copies = fetch(((list_hbm, list_ref), (count_hbm, count_ref)), sem)
    transport(in_ref, out_ref, b_ref, cx_ref, dx_ref, OFF, OWN // 8, 64)
    for copy in copies:
        copy.wait()
    listed_physics(out_ref, 1, list_ref, count_ref, w_ref, r_ref)


def finish_kernel(
    a_in, cx_in, dx_in, w_ref, first_ref, last_ref, near_ref, far_ref,
    out_ref, a_ref, cx_ref, dx_ref,
    left_ref, right_ref, b_ref, ea_ref, eb_ref, h_ref, r_ref, ec_ref, ed_ref, n_ref, xsem,
):
    odd = lax.axis_index("pos") % 2 == 1

    @pl.when(odd)
    def _():
        left_ref[...] = near_ref[...]
        right_ref[...] = far_ref[...]

    @pl.when(jnp.logical_not(odd))
    def _():
        left_ref[...] = far_ref[...]
        right_ref[...] = near_ref[...]

    parts = (left_ref, first_ref, last_ref, right_ref)
    for i, ref in enumerate(parts):
        rows = slice(8 + HALO * i, 8 + HALO * (i + 1))
        for b in range(NB):
            ea_ref[b, rows, :] = ref[HALO * b : HALO * (b + 1), :]
        c = ref[HALO * NB : HALO * (NB + 1), :]
        ec_ref[rows, :] = c
        ed_ref[rows, :] = 1.0 - c
    for ref, row in ((left_ref, OFF - HALO), (right_ref, OFF + OWN)):
        c = ref[HALO * NB : HALO * (NB + 1), :]
        cx_ref[row : row + HALO, :] = c
        dx_ref[row : row + HALO, :] = 1.0 - c
    flags = [jnp.max(ref[HALO * (NB + 1) :, :]) > 0.5 for ref in parts]
    transport(ea_ref, ea_ref, eb_ref, ec_ref, ed_ref, 8, 4 * HALO // 8, 4 * HALO // 8)
    near = [8 + HALO - 16, 8 + HALO, 8 + 3 * HALO - 16, 8 + 3 * HALO]

    @pl.when(flags[0] | flags[1] | flags[2] | flags[3])
    def _():
        for i, row in enumerate(near):
            h_ref[:, 16 * i : 16 * i + 16] = ea_ref[:, row : row + 16, :]
        physics([(h_ref, 0, 64)], w_ref, r_ref)
        for i, row in enumerate(near):

            @pl.when(flags[i])
            def _():
                ea_ref[:, row : row + 16, :] = h_ref[:, 16 * i : 16 * i + 16]

    sub = iota((8, CELLS), 0)
    for b in range(NB):
        for row in (16, 24, 32):
            a_ref[b, row : row + 8, :] = ea_ref[b, row : row + 8, :]
        a_ref[b, 40:48, :] = jnp.where(sub < 4, ea_ref[b, 40:48, :], a_ref[b, 40:48, :])
        back = OFF + OWN - HALO - (8 + 2 * HALO)
        row = OFF + OWN - 16
        a_ref[b, row : row + 8, :] = jnp.where(
            sub >= 4, ea_ref[b, row - back : row - back + 8, :], a_ref[b, row : row + 8, :]
        )
        for row in (OFF + OWN - 8, OFF + OWN, OFF + OWN + 8):
            a_ref[b, row : row + 8, :] = ea_ref[b, row - back : row - back + 8, :]
    transport(a_ref, a_ref, b_ref, cx_ref, dx_ref, OFF - 16, OWN // 8 + 4, 66)
    flat = n_ref.reshape(TILES, PLEV * 8, CELLS)
    copies = []
    for t in range(TILES):
        for b, pair in enumerate(BLOCKS):
            block = a_ref[b, pl.ds(OFF + CELLS * t, CELLS), :].T
            for h, f in enumerate(pair):
                for g in range(PLEV // 8):
                    flat[t, pl.ds(64 * g + f, 8, stride=8), :] = block[
                        HALF * h + 8 * g : HALF * h + 8 * g + 8
                    ]
        copies += fetch(
            [(n_ref.at[t, pl.ds(0, LEVELS)], out_ref.at[:, pl.ds(8 * t, 8), :])],
            xsem.at[pl.ds(t, 1)],
        )
    for copy in copies:
        copy.wait()


VM = pl.BlockSpec(memory_space=pltpu.VMEM)
HBM = pl.BlockSpec(memory_space=pltpu.HBM)
ANY = pl.BlockSpec(memory_space=pl.ANY)
SMALL = [
    pltpu.VMEM((PLEV * TILES, CELLS), F32),
    pltpu.SMEM((CYCLES, 4), jnp.int32),
    pltpu.SMEM((CYCLES,), jnp.int32),
]
LIMIT = 40 << 20
STATE = (NB, XROWS, CELLS)
COLUMN = (XROWS, CELLS)
ENDS = (HALO * (NB + 1) + 8, CELLS)
BATCH = pltpu.VMEM((4 * CELLS, 2 * WIDE), BF16)
NATURAL = pltpu.VMEM((TILES, PLEV, 8, CELLS), F32)


def local(state, courant, level_mix, field_mix, send_list, send_count):
    shape = jax.ShapeDtypeStruct
    hbm = lambda v: pltpu.with_memory_space_constraint(v, pltpu.HBM)
    x = state.reshape(FIELDS, LEVELS, TILES, CELLS).transpose(1, 2, 0, 3)
    x = hbm(x.reshape(LEVELS, TILES * FIELDS, CELLS))
    c = hbm(courant.reshape(LEVELS * TILES, CELLS))
    chosen, count = hbm(send_list.reshape(CYCLES, 4)), hbm(send_count.reshape(CYCLES))
    a, cx, dx, w, first, last, near, far = pl.pallas_call(
        column_kernel,
        name="column",
        out_shape=(
            shape(STATE, F32), shape(COLUMN, F32), shape(COLUMN, F32),
            shape((2 * WIDE, WIDE), BF16), *(shape(ENDS, F32),) * 4,
        ),
        in_specs=[HBM] * 6,
        out_specs=(VM,) * 8,
        scratch_shapes=[
            NATURAL,
            BATCH,
            pltpu.VMEM((CELLS, CELLS), F32),
            SMALL[0],
            pltpu.VMEM((LEVELS, LEVELS), F32),
            pltpu.SMEM((FIELDS, FIELDS), F32),
            *SMALL[1:],
            pltpu.SemaphoreType.DMA((5,)),
            pltpu.SemaphoreType.DMA((TILES,)),
        ],
        compiler_params=pltpu.CompilerParams(vmem_limit_bytes=LIMIT),
    )(x, c, hbm(level_mix), hbm(field_mix), chosen, count)
    n = lax.axis_size("pos")
    near = lax.ppermute(near, "pos", [(i, i ^ 1) for i in range(n)])
    far = lax.ppermute(far, "pos", [(i, (i + (1 if i % 2 else -1)) % n) for i in range(n)])
    mid = pl.pallas_call(
        inside_kernel,
        name="inside",
        out_shape=shape(STATE, F32),
        in_specs=[VM] * 4 + [HBM] * 2,
        out_specs=VM,
        scratch_shapes=[
            pltpu.VMEM(STATE, F32), BATCH, *SMALL[1:], pltpu.SemaphoreType.DMA((2,))
        ],
        compiler_params=pltpu.CompilerParams(vmem_limit_bytes=LIMIT),
        cost_estimate=pl.CostEstimate(
            flops=4_000_000_000, bytes_accessed=8_000_000, transcendentals=0
        ),
    )(a, cx, dx, w, chosen, count)
    out, *_ = pl.pallas_call(
        finish_kernel,
        name="finish",
        out_shape=(
            shape((LEVELS, TILES * FIELDS, CELLS), F32),
            shape(STATE, F32), shape(COLUMN, F32), shape(COLUMN, F32),
        ),
        in_specs=[VM] * 8,
        out_specs=(ANY, VM, VM, VM),
        input_output_aliases={0: 1, 1: 2, 2: 3},
        scratch_shapes=[
            pltpu.VMEM(ENDS, F32),
            pltpu.VMEM(ENDS, F32),
            pltpu.VMEM(STATE, F32),
            pltpu.VMEM((NB, EROWS, CELLS), F32),
            pltpu.VMEM((NB, EROWS, CELLS), F32),
            pltpu.VMEM((NB, 64, CELLS), F32),
            pltpu.VMEM((64, 2 * WIDE), BF16),
            pltpu.VMEM((EROWS, CELLS), F32),
            pltpu.VMEM((EROWS, CELLS), F32),
            NATURAL,
            pltpu.SemaphoreType.DMA((TILES,)),
        ],
        compiler_params=pltpu.CompilerParams(vmem_limit_bytes=LIMIT),
    )(mid, cx, dx, w, first, last, near, far)
    out = out.reshape(LEVELS, TILES, FIELDS, CELLS).transpose(2, 0, 1, 3)
    return out.reshape(1, FIELDS, LEVELS, TILES * CELLS)


def solution(mesh):
    in_specs = (
        P("chan", None, None, "pos"),
        P("chan", None, "pos"),
        P(),
        P(),
        P(None, "chan", "pos", None),
        P(None, "chan", "pos"),
    )
    out_specs = P("chan", None, None, "pos")
    return jax.shard_map(local, mesh=mesh, in_specs=in_specs, out_specs=out_specs, check_vma=False)
```

```python
import functools

import jax
import jax.numpy as jnp
from jax import lax
from jax.experimental import pallas as pl
from jax.experimental.pallas import tpu as pltpu
from jax.sharding import PartitionSpec as P

LEVELS = 50
FIELDS = 8
CELLS = 128
SECTIONS = 12
SWEEPS = 4
CYCLES = 2
TILES = 8
BUOYANCY = 0.4
F32 = jnp.float32
BF16 = jnp.bfloat16

BLOCKS = ((2, 0), (1, 3), (4, 6), (5, 7))
HALF = 64
HALO = CYCLES * SECTIONS
OFF = HALO + 8
OWN = TILES * CELLS
XROWS = OFF + OWN + HALO + 8
EROWS = 8 + 4 * HALO + 8
NB = len(BLOCKS)
WIDE = NB * CELLS
PLEV = 56
PAY = 464


def iota(shape, dim):
    return lax.broadcasted_iota(jnp.int32, shape, dim)


def fetch(pairs, sem):
    copies = [pltpu.make_async_copy(a, b, sem.at[i]) for i, (a, b) in enumerate(pairs)]
    for copy in copies:
        copy.start()
    return copies


def strips(ref, index, row):
    take = [ref[(*index, pl.ds(64 * g + row, 8, stride=8), slice(None))] for g in range(PLEV // 8)]
    return take + [jnp.zeros((8, CELLS), F32)]


def build_weights(lm_ref, fm_ref, q_ref, w_ref):
    q_ref[...] = jnp.zeros((CELLS, CELLS), F32)
    lm = lm_ref[...]
    q_ref[:LEVELS, :LEVELS] = lm
    q_ref[HALF : HALF + LEVELS, :LEVELS] = lm
    q_ref[...] = q_ref[...].T
    lane = iota((16, CELLS), 1)
    sub = iota((16, CELLS), 0)
    low = lane < HALF
    eyes = [(lane % HALF == sub + r) & (sub + r < LEVELS) for r in range(0, HALF, 16)]
    for kb, pair_k in enumerate(BLOCKS):
        for kh, g in enumerate(pair_k):
            for nb, (fa, fb) in enumerate(BLOCKS):
                mix = jnp.where(low, fm_ref[fa, g], fm_ref[fb, g])
                for i, eye in enumerate(eyes):
                    row = CELLS * kb + HALF * kh + 16 * i
                    w = jnp.where(eye, mix, 0.0)
                    if g in (fa, fb):
                        lt = q_ref[16 * i : 16 * i + 16, :]
                        w = w + (jnp.where(low, lt, 0.0) if g == fa else jnp.where(low, 0.0, lt))
                    hi = w.astype(BF16)
                    cols = slice(CELLS * nb, CELLS * (nb + 1))
                    w_ref[row : row + 16, cols] = hi
                    w_ref[WIDE + row : WIDE + row + 16, cols] = (w - hi.astype(F32)).astype(BF16)


def physics(parts, w_ref, v_ref):
    starts = [sum(rows for _, _, rows in parts[:i]) for i in range(len(parts))]
    total = sum(rows for _, _, rows in parts)
    high = w_ref[:WIDE, :]
    rhs = jnp.concatenate([high, high, w_ref[WIDE:, :]], axis=0)

    def block(sweep_index, b):
        if sweep_index > 0:
            return v_ref[b, :total]
        return jnp.concatenate([ref[b, pl.ds(row, rows), :] for ref, row, rows in parts], axis=0)

    for sweep_index in range(SWEEPS):
        highs, lows = [], []
        for b in range(NB):
            t = jnp.tanh(block(sweep_index, b))
            hi = t.astype(BF16)
            highs.append(hi)
            lows.append((t - hi.astype(F32)).astype(BF16))
        lhs = jnp.concatenate(highs + lows + highs, axis=1)
        acc = jnp.dot(lhs, rhs, preferred_element_type=F32)
        for b in range(NB):
            new = block(sweep_index, b) + acc[:, CELLS * b : CELLS * (b + 1)]
            if sweep_index < SWEEPS - 1:
                v_ref[b, :total] = new
            else:
                for at, (ref, row, rows) in zip(starts, parts):
                    ref[b, pl.ds(row, rows), :] = new[at : at + rows]


def listed_physics(ref, cycle, list_ref, count_ref, w_ref, v_ref):
    for count in range(1, 5):

        @pl.when(count_ref[cycle] == count)
        def _():
            rows = [pl.multiple_of(OFF + CELLS * list_ref[cycle, k], 8) for k in range(count)]
            physics([(ref, row, CELLS) for row in rows], w_ref, v_ref)


def section(src, dst, c_ref, d_ref, kv, base, groups):
    for i in range(groups):
        row = base + 8 * i
        here, before, after = pl.ds(row, 8), pl.ds(row - 1, 8), pl.ds(row + 1, 8)
        d, cm, cp = d_ref[here, :], c_ref[before, :], c_ref[after, :]
        x = []
        for b in range(NB):
            side, coef = (before, cm) if b % 2 == 0 else (after, cp)
            x.append(d * src[b, here, :] + coef * src[b, side, :])
        x[1] = x[1] + kv * x[0]
        x[0] = x[0] - kv * x[1]
        for b in range(NB):
            dst[b, here, :] = x[b]


def transport(from_ref, a_ref, b_ref, c_ref, d_ref, base, groups, unroll):
    kv = jnp.where(iota((8, CELLS), 1) < HALF, BUOYANCY, 0.0)

    def sweep(src, dst):
        def body(i, carry):
            row = pl.multiple_of(base + i * (8 * unroll), 8)
            section(src, dst, c_ref, d_ref, kv, row, unroll)
            return carry

        if groups == unroll:
            section(src, dst, c_ref, d_ref, kv, base, groups)
        else:
            lax.fori_loop(0, groups // unroll, body, 0)

    def two(_, carry):
        sweep(a_ref, b_ref)
        sweep(b_ref, a_ref)
        return carry

    if from_ref is not a_ref:
        sweep(from_ref, b_ref)
        sweep(b_ref, a_ref)
        lax.fori_loop(1, SECTIONS // 2, two, 0)
    else:
        lax.fori_loop(0, SECTIONS // 2, two, 0)


def put_courant(c_ref, d_ref, row, block):
    c = jnp.concatenate(block + block, axis=0).T
    c_ref[pl.ds(row, CELLS), :] = c
    d_ref[pl.ds(row, CELLS), :] = 1.0 - c


def tile_block(ref, index, pair):
    return jnp.concatenate(strips(ref, index, pair[0]) + strips(ref, index, pair[1]), axis=0).T


def column_kernel(
    x_ref, c_hbm, lm_hbm, fm_hbm, list_hbm, count_hbm,
    a_ref, cx_ref, dx_ref, w_ref, first_ref, last_ref, neav_ref, fav_ref,
    n_ref, v_ref, q_ref, c_ref, lm_ref, fm_ref, list_ref, count_ref, sem, xsem,
):
    lm_copy, fm_copy, c_copy, list_copy, count_copy = fetch(
        (
            (lm_hbm, lm_ref), (fm_hbm, fm_ref), (c_hbm, c_ref.at[pl.ds(0, LEVELS * TILES)]),
            (list_hbm, list_ref), (count_hbm, count_ref),
        ),
        sem,
    )
    tiles = fetch(
        [
            (x_ref.at[:, pl.ds(8 * t, 8), :], n_ref.at[t, pl.ds(0, LEVELS)])
            for t in range(TILES)
        ],
        xsem,
    )
    c_ref[LEVELS * TILES :, :] = jnp.zeros((48, CELLS), F32)
    n_ref[:, LEVELS:] = jnp.zeros((TILES, PLEV - LEVELS, 8, CELLS), F32)
    lm_copy.wait()
    fm_copy.wait()
    build_weights(lm_ref, fm_ref, q_ref, w_ref)
    for copy in (c_copy, list_copy, count_copy, *tiles):
        copy.wait()
    for t in range(TILES):
        put_courant(cx_ref, dx_ref, OFF + CELLS * t, strips(c_ref, (), t))
    flat = n_ref.reshape(TILES, PLEV * 8, CELLS)
    for t in range(TILES):
        for b, pair in enumerate(BLOCKS):
            a_ref[b, pl.ds(OFF + CELLS * t, CELLS), :] = tile_block(flat, (t,), pair)
    listed_physics(a_ref, 0, list_ref, count_ref, w_ref, v_ref)
    for ref, row, t in ((first_ref, OFF, 0), (last_ref, OFF + OWN - HALO, TILES - 1)):
        for b in range(NB):
            ref[HALO * b : HALO * (b + 1), :] = a_ref[b, row : row + HALO, :]
        ref[HALO * NB : HALO * (NB + 1), :] = cx_ref[row : row + HALO, :]
        hit = jnp.int32(0)
        for slot in range(4):
            named = (slot < count_ref[1]) & (list_ref[1, slot] == t)
            hit = jnp.where(named, jnp.int32(1), hit)
        ref[HALO * (NB + 1) :, :] = jnp.broadcast_to(hit.astype(F32), (8, CELLS))
    odd = lax.axis_index("pos") % 2 == 1

    @pl.when(odd)
    def _():
        neav_ref[...] = first_ref[...]
        fav_ref[...] = last_ref[...]

    @pl.when(jnp.logical_not(odd))
    def _():
        neav_ref[...] = last_ref[...]
        fav_ref[...] = first_ref[...]


def inside_kernel(
    in_ref, cx_ref, dx_ref, w_ref, list_hbm, count_hbm,
    out_ref,
    b_ref, v_ref, list_ref, count_ref, sem,
):
    copies = fetch(((list_hbm, list_ref), (count_hbm, count_ref)), sem)
    transport(in_ref, out_ref, b_ref, cx_ref, dx_ref, OFF, OWN // 8, 64)
    for copy in copies:
        copy.wait()
    listed_physics(out_ref, 1, list_ref, count_ref, w_ref, v_ref)


def finish_kernel(
    a_in, cx_in, dx_in, w_ref, first_ref, last_ref, neav_ref, fav_ref,
    out_ref, a_ref, cx_ref, dx_ref,
    left_ref, right_ref, b_ref, ea_ref, eb_ref, h_ref, v_ref, ec_ref, ed_ref, n_ref, xsem,
):
    odd = lax.axis_index("pos") % 2 == 1

    @pl.when(odd)
    def _():
        left_ref[...] = neav_ref[...]
        right_ref[...] = fav_ref[...]

    @pl.when(jnp.logical_not(odd))
    def _():
        left_ref[...] = fav_ref[...]
        right_ref[...] = neav_ref[...]

    parts = (left_ref, first_ref, last_ref, right_ref)
    for i, ref in enumerate(parts):
        rows = slice(8 + HALO * i, 8 + HALO * (i + 1))
        for b in range(NB):
            ea_ref[b, rows, :] = ref[HALO * b : HALO * (b + 1), :]
        c = ref[HALO * NB : HALO * (NB + 1), :]
        ec_ref[rows, :] = c
        ed_ref[rows, :] = 1.0 - c
    for ref, row in ((left_ref, OFF - HALO), (right_ref, OFF + OWN)):
        c = ref[HALO * NB : HALO * (NB + 1), :]
        cx_ref[row : row + HALO, :] = c
        dx_ref[row : row + HALO, :] = 1.0 - c
    flags = [jnp.max(ref[HALO * (NB + 1) :, :]) > 0.5 for ref in parts]
    transport(ea_ref, ea_ref, eb_ref, ec_ref, ed_ref, 8, 4 * HALO // 8, 4 * HALO // 8)
    near = [8 + HALO - 16, 8 + HALO, 8 + 3 * HALO - 16, 8 + 3 * HALO]

    @pl.when(flags[0] | flags[1] | flags[2] | flags[3])
    def _():
        for i, row in enumerate(near):
            h_ref[:, 16 * i : 16 * i + 16] = ea_ref[:, row : row + 16, :]
        physics([(h_ref, 0, 64)], w_ref, v_ref)
        for i, row in enumerate(near):

            @pl.when(flags[i])
            def _():
                ea_ref[:, row : row + 16, :] = h_ref[:, 16 * i : 16 * i + 16]

    sub = iota((8, CELLS), 0)
    for b in range(NB):
        for row in (16, 24, 32):
            a_ref[b, row : row + 8, :] = ea_ref[b, row : row + 8, :]
        a_ref[b, 40:48, :] = jnp.where(sub < 4, ea_ref[b, 40:48, :], a_ref[b, 40:48, :])
        back = OFF + OWN - HALO - (8 + 2 * HALO)
        row = OFF + OWN - 16
        a_ref[b, row : row + 8, :] = jnp.where(
            sub >= 4, ea_ref[b, row - back : row - back + 8, :], a_ref[b, row : row + 8, :]
        )
        for row in (OFF + OWN - 8, OFF + OWN, OFF + OWN + 8):
            a_ref[b, row : row + 8, :] = ea_ref[b, row - back : row - back + 8, :]
    transport(a_ref, a_ref, b_ref, cx_ref, dx_ref, OFF - 16, OWN // 8 + 4, 66)
    flat = n_ref.reshape(TILES, PLEV * 8, CELLS)
    copies = []
    for group in (range(0, 4), range(4, 7), range(7, 8)):
        for t in group:
            for b, pair in enumerate(BLOCKS):
                block = a_ref[b, pl.ds(OFF + CELLS * t, CELLS), :].T
                for h, f in enumerate(pair):
                    for g in range(PLEV // 8):
                        flat[t, pl.ds(64 * g + f, 8, stride=8), :] = block[
                            HALF * h + 8 * g : HALF * h + 8 * g + 8
                        ]
        for t in group:
            copies += fetch(
                [(n_ref.at[t, pl.ds(0, LEVELS)], out_ref.at[:, pl.ds(8 * t, 8), :])],
                xsem.at[pl.ds(t, 1)],
            )
    for copy in copies:
        copy.wait()


VM = pl.BlockSpec(memory_space=pltpu.VMEM)
HBM = pl.BlockSpec(memory_space=pltpu.HBM)
ANY = pl.BlockSpec(memory_space=pl.ANY)
SMALL = [
    pltpu.VMEM((PLEV * TILES, CELLS), F32),
    pltpu.SMEM((CYCLES, 4), jnp.int32),
    pltpu.SMEM((CYCLES,), jnp.int32),
]
LIMIT = 40 << 20
STATE = (NB, XROWS, CELLS)
COLUMN = (XROWS, CELLS)
ENDS = (HALO * (NB + 1) + 8, CELLS)
BATCH = pltpu.VMEM((NB, 4 * CELLS, CELLS), F32)
NATURAL = pltpu.VMEM((TILES, PLEV, 8, CELLS), F32)


def local(state, courant, level_mix, field_mix, send_list, send_count):
    shape = jax.ShapeDtypeStruct
    hbm = lambda v: pltpu.with_memory_space_constraint(v, pltpu.HBM)
    x = state.reshape(FIELDS, LEVELS, TILES, CELLS).transpose(1, 2, 0, 3)
    x = hbm(x.reshape(LEVELS, TILES * FIELDS, CELLS))
    c = hbm(courant.reshape(LEVELS * TILES, CELLS))
    chosen, count = hbm(send_list.reshape(CYCLES, 4)), hbm(send_count.reshape(CYCLES))
    a, cx, dx, w, first, last, near, far = pl.pallas_call(
        column_kernel,
        name="column",
        out_shape=(
            shape(STATE, F32), shape(COLUMN, F32), shape(COLUMN, F32),
            shape((2 * WIDE, WIDE), BF16), *(shape(ENDS, F32),) * 4,
        ),
        in_specs=[HBM] * 6,
        out_specs=(VM,) * 8,
        scratch_shapes=[
            NATURAL,
            BATCH,
            pltpu.VMEM((CELLS, CELLS), F32),
            SMALL[0],
            pltpu.VMEM((LEVELS, LEVELS), F32),
            pltpu.SMEM((FIELDS, FIELDS), F32),
            *SMALL[1:],
            pltpu.SemaphoreType.DMA((5,)),
            pltpu.SemaphoreType.DMA((TILES,)),
        ],
        compiler_params=pltpu.CompilerParams(vmem_limit_bytes=LIMIT),
    )(x, c, hbm(level_mix), hbm(field_mix), chosen, count)
    n = lax.axis_size("pos")
    near = lax.ppermute(near, "pos", [(i, i ^ 1) for i in range(n)])
    far = lax.ppermute(far, "pos", [(i, (i + (1 if i % 2 else -1)) % n) for i in range(n)])
    mid = pl.pallas_call(
        inside_kernel,
        name="inside",
        out_shape=shape(STATE, F32),
        in_specs=[VM] * 4 + [HBM] * 2,
        out_specs=VM,
        scratch_shapes=[
            pltpu.VMEM(STATE, F32), BATCH, *SMALL[1:], pltpu.SemaphoreType.DMA((2,))
        ],
        compiler_params=pltpu.CompilerParams(vmem_limit_bytes=LIMIT),
        cost_estimate=pl.CostEstimate(
            flops=4_000_000_000, bytes_accessed=8_000_000, transcendentals=0
        ),
    )(a, cx, dx, w, chosen, count)
    out, *_ = pl.pallas_call(
        finish_kernel,
        name="finish",
        out_shape=(
            shape((LEVELS, TILES * FIELDS, CELLS), F32),
            shape(STATE, F32), shape(COLUMN, F32), shape(COLUMN, F32),
        ),
        in_specs=[VM] * 8,
        out_specs=(ANY, VM, VM, VM),
        input_output_aliases={0: 1, 1: 2, 2: 3},
        scratch_shapes=[
            pltpu.VMEM(ENDS, F32),
            pltpu.VMEM(ENDS, F32),
            pltpu.VMEM(STATE, F32),
            pltpu.VMEM((NB, EROWS, CELLS), F32),
            pltpu.VMEM((NB, EROWS, CELLS), F32),
            pltpu.VMEM((NB, 64, CELLS), F32),
            pltpu.VMEM((NB, 64, CELLS), F32),
            pltpu.VMEM((EROWS, CELLS), F32),
            pltpu.VMEM((EROWS, CELLS), F32),
            NATURAL,
            pltpu.SemaphoreType.DMA((TILES,)),
        ],
        compiler_params=pltpu.CompilerParams(vmem_limit_bytes=LIMIT),
    )(mid, cx, dx, w, first, last, near, far)
    out = out.reshape(LEVELS, TILES, FIELDS, CELLS).transpose(2, 0, 1, 3)
    return out.reshape(1, FIELDS, LEVELS, TILES * CELLS)


def solution(mesh):
    in_specs = (
        P("chan", None, None, "pos"),
        P("chan", None, "pos"),
        P(),
        P(),
        P(None, "chan", "pos", None),
        P(None, "chan", "pos"),
    )
    out_specs = P("chan", None, None, "pos")
    return jax.shard_map(local, mesh=mesh, in_specs=in_specs, out_specs=out_specs, check_vma=False)
```

```python
import functools

import jax
import jax.numpy as jnp
from jax import lax
from jax.experimental import pallas as pl
from jax.experimental.pallas import tpu as pltpu
from jax.sharding import PartitionSpec as P

LEVELS = 50
FIELDS = 8
CELLS = 128
SECTIONS = 12
SWEEPS = 4
CYCLES = 2
TILES = 8
BUOYANCY = 0.4
F32 = jnp.float32
BF16 = jnp.bfloat16

BLOCKS = ((2, 0), (1, 3), (4, 6), (5, 7))
HALF = 64
HALO = CYCLES * SECTIONS
OFF = HALO + 8
OWN = TILES * CELLS
XROWS = OFF + OWN + HALO + 8
EROWS = 8 + 4 * HALO + 8
NB = len(BLOCKS)
WIDE = NB * CELLS
PLEV = 56
PAY = 464


def iota(shape, dim):
    return lax.broadcasted_iota(jnp.int32, shape, dim)


def fetch(pairs, sem):
    copies = [pltpu.make_async_copy(a, b, sem.at[i]) for i, (a, b) in enumerate(pairs)]
    for copy in copies:
        copy.start()
    return copies


def strips(ref, index, row):
    take = [ref[(*index, pl.ds(64 * g + row, 8, stride=8), slice(None))] for g in range(PLEV // 8)]
    return take + [jnp.zeros((8, CELLS), F32)]


def build_weights(lm_ref, fm_ref, q_ref, w_ref):
    q_ref[...] = jnp.zeros((CELLS, CELLS), F32)
    lm = lm_ref[...]
    q_ref[:LEVELS, :LEVELS] = lm
    q_ref[HALF : HALF + LEVELS, :LEVELS] = lm
    q_ref[...] = q_ref[...].T
    lane = iota((16, CELLS), 1)
    sub = iota((16, CELLS), 0)
    low = lane < HALF
    eyes = [(lane % HALF == sub + r) & (sub + r < LEVELS) for r in range(0, HALF, 16)]
    for kb, pair_k in enumerate(BLOCKS):
        for kh, g in enumerate(pair_k):
            for nb, (fa, fb) in enumerate(BLOCKS):
                mix = jnp.where(low, fm_ref[fa, g], fm_ref[fb, g])
                for i, eye in enumerate(eyes):
                    row = CELLS * kb + HALF * kh + 16 * i
                    w = jnp.where(eye, mix, 0.0)
                    if g in (fa, fb):
                        lt = q_ref[16 * i : 16 * i + 16, :]
                        w = w + (jnp.where(low, lt, 0.0) if g == fa else jnp.where(low, 0.0, lt))
                    hi = w.astype(BF16)
                    cols = slice(CELLS * nb, CELLS * (nb + 1))
                    w_ref[row : row + 16, cols] = hi
                    w_ref[WIDE + row : WIDE + row + 16, cols] = (w - hi.astype(F32)).astype(BF16)


def physics(parts, w_ref, v_ref):
    starts = [sum(rows for _, _, rows in parts[:i]) for i in range(len(parts))]
    total = sum(rows for _, _, rows in parts)
    high = w_ref[:WIDE, :]
    rhs = jnp.concatenate([high, high, w_ref[WIDE:, :]], axis=0)

    def block(sweep_index, b):
        if sweep_index > 0:
            return v_ref[b, :total]
        return jnp.concatenate([ref[b, pl.ds(row, rows), :] for ref, row, rows in parts], axis=0)

    for sweep_index in range(SWEEPS):
        highs, lows = [], []
        for b in range(NB):
            t = jnp.tanh(block(sweep_index, b))
            hi = t.astype(BF16)
            highs.append(hi)
            lows.append((t - hi.astype(F32)).astype(BF16))
        lhs = jnp.concatenate(highs + lows + highs, axis=1)
        acc = jnp.dot(lhs, rhs, preferred_element_type=F32)
        for b in range(NB):
            new = block(sweep_index, b) + acc[:, CELLS * b : CELLS * (b + 1)]
            if sweep_index < SWEEPS - 1:
                v_ref[b, :total] = new
            else:
                for at, (ref, row, rows) in zip(starts, parts):
                    ref[b, pl.ds(row, rows), :] = new[at : at + rows]


def listed_physics(ref, cycle, list_ref, count_ref, w_ref, v_ref):
    for count in range(1, 5):

        @pl.when(count_ref[cycle] == count)
        def _():
            rows = [pl.multiple_of(OFF + CELLS * list_ref[cycle, k], 8) for k in range(count)]
            physics([(ref, row, CELLS) for row in rows], w_ref, v_ref)


def section(src, dst, c_ref, d_ref, kv, base, groups):
    for i in range(groups):
        row = base + 8 * i
        here, before, after = pl.ds(row, 8), pl.ds(row - 1, 8), pl.ds(row + 1, 8)
        d, cm, cp = d_ref[here, :], c_ref[before, :], c_ref[after, :]
        x = []
        for b in range(NB):
            side, coef = (before, cm) if b % 2 == 0 else (after, cp)
            x.append(d * src[b, here, :] + coef * src[b, side, :])
        x[1] = x[1] + kv * x[0]
        x[0] = x[0] - kv * x[1]
        for b in range(NB):
            dst[b, here, :] = x[b]


def transport(from_ref, a_ref, b_ref, c_ref, d_ref, base, groups, unroll):
    kv = jnp.where(iota((8, CELLS), 1) < HALF, BUOYANCY, 0.0)

    def sweep(src, dst):
        def body(i, carry):
            row = pl.multiple_of(base + i * (8 * unroll), 8)
            section(src, dst, c_ref, d_ref, kv, row, unroll)
            return carry

        if groups == unroll:
            section(src, dst, c_ref, d_ref, kv, base, groups)
        else:
            lax.fori_loop(0, groups // unroll, body, 0)

    def two(_, carry):
        sweep(a_ref, b_ref)
        sweep(b_ref, a_ref)
        return carry

    if from_ref is not a_ref:
        sweep(from_ref, b_ref)
        sweep(b_ref, a_ref)
        lax.fori_loop(1, SECTIONS // 2, two, 0)
    else:
        lax.fori_loop(0, SECTIONS // 2, two, 0)


def put_courant(c_ref, d_ref, row, block):
    c = jnp.concatenate(block + block, axis=0).T
    c_ref[pl.ds(row, CELLS), :] = c
    d_ref[pl.ds(row, CELLS), :] = 1.0 - c


def tile_block(ref, index, pair):
    return jnp.concatenate(strips(ref, index, pair[0]) + strips(ref, index, pair[1]), axis=0).T


def column_kernel(
    x_ref, c_hbm, lm_hbm, fm_hbm, list_hbm, count_hbm,
    a_ref, cx_ref, dx_ref, w_ref, first_ref, last_ref, near_ref, far_ref,
    n_ref, v_ref, q_ref, c_ref, lm_ref, fm_ref, list_ref, count_ref, sem, xsem,
):
    lm_copy, fm_copy, c_copy, list_copy, count_copy = fetch(
        (
            (lm_hbm, lm_ref), (fm_hbm, fm_ref), (c_hbm, c_ref.at[pl.ds(0, LEVELS * TILES)]),
            (list_hbm, list_ref), (count_hbm, count_ref),
        ),
        sem,
    )
    tiles = fetch(
        [
            (x_ref.at[:, pl.ds(8 * t, 8), :], n_ref.at[t, pl.ds(0, LEVELS)])
            for t in range(TILES)
        ],
        xsem,
    )
    c_ref[LEVELS * TILES :, :] = jnp.zeros((48, CELLS), F32)
    n_ref[:, LEVELS:] = jnp.zeros((TILES, PLEV - LEVELS, 8, CELLS), F32)
    lm_copy.wait()
    fm_copy.wait()
    build_weights(lm_ref, fm_ref, q_ref, w_ref)
    for copy in (c_copy, list_copy, count_copy, *tiles):
        copy.wait()
    for t in range(TILES):
        put_courant(cx_ref, dx_ref, OFF + CELLS * t, strips(c_ref, (), t))
    flat = n_ref.reshape(TILES, PLEV * 8, CELLS)
    for t in range(TILES):
        for b, pair in enumerate(BLOCKS):
            a_ref[b, pl.ds(OFF + CELLS * t, CELLS), :] = tile_block(flat, (t,), pair)
    listed_physics(a_ref, 0, list_ref, count_ref, w_ref, v_ref)
    for ref, row, t in ((first_ref, OFF, 0), (last_ref, OFF + OWN - HALO, TILES - 1)):
        for b in range(NB):
            ref[HALO * b : HALO * (b + 1), :] = a_ref[b, row : row + HALO, :]
        ref[HALO * NB : HALO * (NB + 1), :] = cx_ref[row : row + HALO, :]
        hit = jnp.int32(0)
        for slot in range(4):
            named = (slot < count_ref[1]) & (list_ref[1, slot] == t)
            hit = jnp.where(named, jnp.int32(1), hit)
        ref[HALO * (NB + 1) :, :] = jnp.broadcast_to(hit.astype(F32), (8, CELLS))
    odd = lax.axis_index("pos") % 2 == 1

    @pl.when(odd)
    def _():
        near_ref[...] = first_ref[...]
        far_ref[...] = last_ref[...]

    @pl.when(jnp.logical_not(odd))
    def _():
        near_ref[...] = last_ref[...]
        far_ref[...] = first_ref[...]


def early(n):
    return (0, n // 2)


def is_early():
    pos = lax.axis_index("pos")
    first, second = early(lax.axis_size("pos"))
    return (pos == first) | (pos == second)


def ahead_kernel(in_ref, cx_ref, dx_ref, far_ref, out_ref, wrap_ref, b_ref):
    @pl.when(is_early())
    def _():
        transport(in_ref, out_ref, b_ref, cx_ref, dx_ref, OFF, OWN // 8, 64)

    wrap_ref[...] = far_ref[...]


def inside_kernel(
    mid_in, in_ref, cx_ref, dx_ref, w_ref, list_hbm, count_hbm,
    out_ref,
    b_ref, v_ref, list_ref, count_ref, sem,
):
    copies = fetch(((list_hbm, list_ref), (count_hbm, count_ref)), sem)

    @pl.when(jnp.logical_not(is_early()))
    def _():
        transport(in_ref, out_ref, b_ref, cx_ref, dx_ref, OFF, OWN // 8, 64)

    for copy in copies:
        copy.wait()
    listed_physics(out_ref, 1, list_ref, count_ref, w_ref, v_ref)


def finish_kernel(
    a_in, cx_in, dx_in, w_ref, first_ref, last_ref, near_ref, far_ref, wrap_ref,
    out_ref, a_ref, cx_ref, dx_ref,
    left_ref, right_ref, b_ref, ea_ref, eb_ref, h_ref, v_ref, ec_ref, ed_ref, n_ref, xsem,
):
    odd = lax.axis_index("pos") % 2 == 1

    n = lax.axis_size("pos")
    late = functools.reduce(
        jnp.logical_or, [lax.axis_index("pos") == (i - 1) % n for i in early(n)]
    )

    @pl.when(odd & late)
    def _():
        left_ref[...] = near_ref[...]
        right_ref[...] = wrap_ref[...]

    @pl.when(odd & jnp.logical_not(late))
    def _():
        left_ref[...] = near_ref[...]
        right_ref[...] = far_ref[...]

    @pl.when(jnp.logical_not(odd))
    def _():
        left_ref[...] = far_ref[...]
        right_ref[...] = near_ref[...]

    parts = (left_ref, first_ref, last_ref, right_ref)
    for i, ref in enumerate(parts):
        rows = slice(8 + HALO * i, 8 + HALO * (i + 1))
        for b in range(NB):
            ea_ref[b, rows, :] = ref[HALO * b : HALO * (b + 1), :]
        c = ref[HALO * NB : HALO * (NB + 1), :]
        ec_ref[rows, :] = c
        ed_ref[rows, :] = 1.0 - c
    for ref, row in ((left_ref, OFF - HALO), (right_ref, OFF + OWN)):
        c = ref[HALO * NB : HALO * (NB + 1), :]
        cx_ref[row : row + HALO, :] = c
        dx_ref[row : row + HALO, :] = 1.0 - c
    flags = [jnp.max(ref[HALO * (NB + 1) :, :]) > 0.5 for ref in parts]
    transport(ea_ref, ea_ref, eb_ref, ec_ref, ed_ref, 8, 4 * HALO // 8, 4 * HALO // 8)
    near = [8 + HALO - 16, 8 + HALO, 8 + 3 * HALO - 16, 8 + 3 * HALO]

    @pl.when(flags[0] | flags[1] | flags[2] | flags[3])
    def _():
        for i, row in enumerate(near):
            h_ref[:, 16 * i : 16 * i + 16] = ea_ref[:, row : row + 16, :]
        physics([(h_ref, 0, 64)], w_ref, v_ref)
        for i, row in enumerate(near):

            @pl.when(flags[i])
            def _():
                ea_ref[:, row : row + 16, :] = h_ref[:, 16 * i : 16 * i + 16]

    sub = iota((8, CELLS), 0)
    for b in range(NB):
        for row in (16, 24, 32):
            a_ref[b, row : row + 8, :] = ea_ref[b, row : row + 8, :]
        a_ref[b, 40:48, :] = jnp.where(sub < 4, ea_ref[b, 40:48, :], a_ref[b, 40:48, :])
        back = OFF + OWN - HALO - (8 + 2 * HALO)
        row = OFF + OWN - 16
        a_ref[b, row : row + 8, :] = jnp.where(
            sub >= 4, ea_ref[b, row - back : row - back + 8, :], a_ref[b, row : row + 8, :]
        )
        for row in (OFF + OWN - 8, OFF + OWN, OFF + OWN + 8):
            a_ref[b, row : row + 8, :] = ea_ref[b, row - back : row - back + 8, :]
    transport(a_ref, a_ref, b_ref, cx_ref, dx_ref, OFF - 16, OWN // 8 + 4, 66)
    flat = n_ref.reshape(TILES, PLEV * 8, CELLS)
    copies = []
    for group in (range(0, 4), range(4, 7), range(7, 8)):
        for t in group:
            for b, pair in enumerate(BLOCKS):
                block = a_ref[b, pl.ds(OFF + CELLS * t, CELLS), :].T
                for h, f in enumerate(pair):
                    for g in range(PLEV // 8):
                        flat[t, pl.ds(64 * g + f, 8, stride=8), :] = block[
                            HALF * h + 8 * g : HALF * h + 8 * g + 8
                        ]
        for t in group:
            copies += fetch(
                [(n_ref.at[t, pl.ds(0, LEVELS)], out_ref.at[:, pl.ds(8 * t, 8), :])],
                xsem.at[pl.ds(t, 1)],
            )
    for copy in copies:
        copy.wait()


VM = pl.BlockSpec(memory_space=pltpu.VMEM)
HBM = pl.BlockSpec(memory_space=pltpu.HBM)
ANY = pl.BlockSpec(memory_space=pl.ANY)
SMALL = [
    pltpu.VMEM((PLEV * TILES, CELLS), F32),
    pltpu.SMEM((CYCLES, 4), jnp.int32),
    pltpu.SMEM((CYCLES,), jnp.int32),
]
LIMIT = 40 << 20
STATE = (NB, XROWS, CELLS)
COLUMN = (XROWS, CELLS)
ENDS = (HALO * (NB + 1) + 8, CELLS)
BATCH = pltpu.VMEM((NB, 4 * CELLS, CELLS), F32)
NATURAL = pltpu.VMEM((TILES, PLEV, 8, CELLS), F32)


def local(state, courant, level_mix, field_mix, send_list, send_count):
    shape = jax.ShapeDtypeStruct
    hbm = lambda v: pltpu.with_memory_space_constraint(v, pltpu.HBM)
    x = state.reshape(FIELDS, LEVELS, TILES, CELLS).transpose(1, 2, 0, 3)
    x = hbm(x.reshape(LEVELS, TILES * FIELDS, CELLS))
    c = hbm(courant.reshape(LEVELS * TILES, CELLS))
    chosen, count = hbm(send_list.reshape(CYCLES, 4)), hbm(send_count.reshape(CYCLES))
    a, cx, dx, w, first, last, near, far = pl.pallas_call(
        column_kernel,
        name="column",
        out_shape=(
            shape(STATE, F32), shape(COLUMN, F32), shape(COLUMN, F32),
            shape((2 * WIDE, WIDE), BF16), *(shape(ENDS, F32),) * 4,
        ),
        in_specs=[HBM] * 6,
        out_specs=(VM,) * 8,
        scratch_shapes=[
            NATURAL,
            BATCH,
            pltpu.VMEM((CELLS, CELLS), F32),
            SMALL[0],
            pltpu.VMEM((LEVELS, LEVELS), F32),
            pltpu.SMEM((FIELDS, FIELDS), F32),
            *SMALL[1:],
            pltpu.SemaphoreType.DMA((5,)),
            pltpu.SemaphoreType.DMA((TILES,)),
        ],
        compiler_params=pltpu.CompilerParams(vmem_limit_bytes=LIMIT),
    )(x, c, hbm(level_mix), hbm(field_mix), chosen, count)
    n = lax.axis_size("pos")
    near = lax.ppermute(near, "pos", [(i, i ^ 1) for i in range(n)])
    swaps = [(i, (i + (1 if i % 2 else -1)) % n) for i in range(n)]
    got = lax.ppermute(far, "pos", [pair for pair in swaps if pair[0] not in early(n)])
    params = pltpu.CompilerParams(vmem_limit_bytes=LIMIT)
    cost = pl.CostEstimate(flops=4_000_000_000, bytes_accessed=8_000_000, transcendentals=0)
    mid, wrap = pl.pallas_call(
        ahead_kernel,
        name="ahead",
        out_shape=(shape(STATE, F32), shape(ENDS, F32)),
        in_specs=[VM] * 4,
        out_specs=(VM, VM),
        scratch_shapes=[pltpu.VMEM(STATE, F32)],
        compiler_params=params,
        cost_estimate=cost,
    )(a, cx, dx, far)
    wrap = lax.ppermute(wrap, "pos", [pair for pair in swaps if pair[0] in early(n)])
    mid = pl.pallas_call(
        inside_kernel,
        name="inside",
        out_shape=shape(STATE, F32),
        in_specs=[VM] * 5 + [HBM] * 2,
        out_specs=VM,
        input_output_aliases={0: 0},
        scratch_shapes=[
            pltpu.VMEM(STATE, F32), BATCH, *SMALL[1:], pltpu.SemaphoreType.DMA((2,))
        ],
        compiler_params=params,
        cost_estimate=cost,
    )(mid, a, cx, dx, w, chosen, count)
    out, *_ = pl.pallas_call(
        finish_kernel,
        name="finish",
        out_shape=(
            shape((LEVELS, TILES * FIELDS, CELLS), F32),
            shape(STATE, F32), shape(COLUMN, F32), shape(COLUMN, F32),
        ),
        in_specs=[VM] * 9,
        out_specs=(ANY, VM, VM, VM),
        input_output_aliases={0: 1, 1: 2, 2: 3},
        scratch_shapes=[
            pltpu.VMEM(ENDS, F32),
            pltpu.VMEM(ENDS, F32),
            pltpu.VMEM(STATE, F32),
            pltpu.VMEM((NB, EROWS, CELLS), F32),
            pltpu.VMEM((NB, EROWS, CELLS), F32),
            pltpu.VMEM((NB, 64, CELLS), F32),
            pltpu.VMEM((NB, 64, CELLS), F32),
            pltpu.VMEM((EROWS, CELLS), F32),
            pltpu.VMEM((EROWS, CELLS), F32),
            NATURAL,
            pltpu.SemaphoreType.DMA((TILES,)),
        ],
        compiler_params=pltpu.CompilerParams(vmem_limit_bytes=LIMIT),
    )(mid, cx, dx, w, first, last, near, got, wrap)
    out = out.reshape(LEVELS, TILES, FIELDS, CELLS).transpose(2, 0, 1, 3)
    return out.reshape(1, FIELDS, LEVELS, TILES * CELLS)


def solution(mesh):
    in_specs = (
        P("chan", None, None, "pos"),
        P("chan", None, "pos"),
        P(),
        P(),
        P(None, "chan", "pos", None),
        P(None, "chan", "pos"),
    )
    out_specs = P("chan", None, None, "pos")
    return jax.shard_map(local, mesh=mesh, in_specs=in_specs, out_specs=out_specs, check_vma=False)
```

```python
import functools

import jax
import jax.numpy as jnp
from jax import lax
from jax.experimental import pallas as pl
from jax.experimental.pallas import tpu as pltpu
from jax.sharding import PartitionSpec as P

LEVELS = 50
FIELDS = 8
CELLS = 128
SECTIONS = 12
SWEEPS = 4
CYCLES = 2
TILES = 8
BUOYANCY = 0.4
F32 = jnp.float32
BF16 = jnp.bfloat16

BLOCKS = ((2, 0), (1, 3), (4, 6), (5, 7))
HALF = 64
HALO = CYCLES * SECTIONS
OFF = HALO + 8
OWN = TILES * CELLS
XROWS = OFF + OWN + HALO + 8
EROWS = 8 + 4 * HALO + 8
NB = len(BLOCKS)
WIDE = NB * CELLS
PLEV = 56
PAY = 464


def iota(shape, dim):
    return lax.broadcasted_iota(jnp.int32, shape, dim)


def fetch(pairs, sem):
    copies = [pltpu.make_async_copy(a, b, sem.at[i]) for i, (a, b) in enumerate(pairs)]
    for copy in copies:
        copy.start()
    return copies


def strips(ref, index, row):
    take = [ref[(*index, pl.ds(64 * g + row, 8, stride=8), slice(None))] for g in range(PLEV // 8)]
    return take + [jnp.zeros((8, CELLS), F32)]


def build_weights(lm_ref, fm_ref, q_ref, w_ref):
    q_ref[...] = jnp.zeros((CELLS, CELLS), F32)
    lm = lm_ref[...]
    q_ref[:LEVELS, :LEVELS] = lm
    q_ref[HALF : HALF + LEVELS, :LEVELS] = lm
    q_ref[...] = q_ref[...].T
    lane = iota((16, CELLS), 1)
    sub = iota((16, CELLS), 0)
    low = lane < HALF
    eyes = [(lane % HALF == sub + r) & (sub + r < LEVELS) for r in range(0, HALF, 16)]
    for kb, pair_k in enumerate(BLOCKS):
        for kh, g in enumerate(pair_k):
            for nb, (fa, fb) in enumerate(BLOCKS):
                mix = jnp.where(low, fm_ref[fa, g], fm_ref[fb, g])
                for i, eye in enumerate(eyes):
                    row = CELLS * kb + HALF * kh + 16 * i
                    w = jnp.where(eye, mix, 0.0)
                    if g in (fa, fb):
                        lt = q_ref[16 * i : 16 * i + 16, :]
                        w = w + (jnp.where(low, lt, 0.0) if g == fa else jnp.where(low, 0.0, lt))
                    hi = w.astype(BF16)
                    cols = slice(CELLS * nb, CELLS * (nb + 1))
                    w_ref[row : row + 16, cols] = hi
                    w_ref[WIDE + row : WIDE + row + 16, cols] = (w - hi.astype(F32)).astype(BF16)


def physics(parts, w_ref, v_ref):
    starts = [sum(rows for _, _, rows in parts[:i]) for i in range(len(parts))]
    total = sum(rows for _, _, rows in parts)
    high = w_ref[:WIDE, :]
    rhs = jnp.concatenate([high, high, w_ref[WIDE:, :]], axis=0)

    def block(sweep_index, b):
        if sweep_index > 0:
            return v_ref[b, :total]
        return jnp.concatenate([ref[b, pl.ds(row, rows), :] for ref, row, rows in parts], axis=0)

    for sweep_index in range(SWEEPS):
        highs, lows = [], []
        for b in range(NB):
            t = jnp.tanh(block(sweep_index, b))
            hi = t.astype(BF16)
            highs.append(hi)
            lows.append((t - hi.astype(F32)).astype(BF16))
        lhs = jnp.concatenate(highs + lows + highs, axis=1)
        acc = jnp.dot(lhs, rhs, preferred_element_type=F32)
        for b in range(NB):
            new = block(sweep_index, b) + acc[:, CELLS * b : CELLS * (b + 1)]
            if sweep_index < SWEEPS - 1:
                v_ref[b, :total] = new
            else:
                for at, (ref, row, rows) in zip(starts, parts):
                    ref[b, pl.ds(row, rows), :] = new[at : at + rows]


def listed_physics(ref, cycle, list_ref, count_ref, w_ref, v_ref):
    for count in range(1, 5):

        @pl.when(count_ref[cycle] == count)
        def _():
            rows = [pl.multiple_of(OFF + CELLS * list_ref[cycle, k], 8) for k in range(count)]
            physics([(ref, row, CELLS) for row in rows], w_ref, v_ref)


def section(src, dst, c_ref, d_ref, kv, base, groups):
    for i in range(groups):
        row = base + 8 * i
        here, before, after = pl.ds(row, 8), pl.ds(row - 1, 8), pl.ds(row + 1, 8)
        d, cm, cp = d_ref[here, :], c_ref[before, :], c_ref[after, :]
        x = []
        for b in range(NB):
            side, coef = (before, cm) if b % 2 == 0 else (after, cp)
            x.append(d * src[b, here, :] + coef * src[b, side, :])
        x[1] = x[1] + kv * x[0]
        x[0] = x[0] - kv * x[1]
        for b in range(NB):
            dst[b, here, :] = x[b]


def transport(a_ref, b_ref, c_ref, d_ref, base, groups, unroll, first=0, last=SECTIONS // 2):
    kv = jnp.where(iota((8, CELLS), 1) < HALF, BUOYANCY, 0.0)

    def sweep(src, dst):
        def body(i, carry):
            row = pl.multiple_of(base + i * (8 * unroll), 8)
            section(src, dst, c_ref, d_ref, kv, row, unroll)
            return carry

        if groups == unroll:
            section(src, dst, c_ref, d_ref, kv, base, groups)
        else:
            lax.fori_loop(0, groups // unroll, body, 0)

    def two(_, carry):
        sweep(a_ref, b_ref)
        sweep(b_ref, a_ref)
        return carry

    lax.fori_loop(first, last, two, 0)


def put_courant(c_ref, d_ref, row, block):
    c = jnp.concatenate(block + block, axis=0).T
    c_ref[pl.ds(row, CELLS), :] = c
    d_ref[pl.ds(row, CELLS), :] = 1.0 - c


def tile_block(ref, index, pair):
    return jnp.concatenate(strips(ref, index, pair[0]) + strips(ref, index, pair[1]), axis=0).T


def column_kernel(
    x_ref, c_hbm, lm_hbm, fm_hbm, list_hbm, count_hbm,
    a_ref, cx_ref, dx_ref, w_ref, first_ref, last_ref, near_ref, far_ref,
    n_ref, v_ref, q_ref, c_ref, lm_ref, fm_ref, list_ref, count_ref, sem, xsem,
):
    lm_copy, fm_copy, c_copy, list_copy, count_copy = fetch(
        (
            (lm_hbm, lm_ref), (fm_hbm, fm_ref), (c_hbm, c_ref.at[pl.ds(0, LEVELS * TILES)]),
            (list_hbm, list_ref), (count_hbm, count_ref),
        ),
        sem,
    )
    tiles = fetch(
        [
            (x_ref.at[:, pl.ds(8 * t, 8), :], n_ref.at[t, pl.ds(0, LEVELS)])
            for t in range(TILES)
        ],
        xsem,
    )
    c_ref[LEVELS * TILES :, :] = jnp.zeros((48, CELLS), F32)
    n_ref[:, LEVELS:] = jnp.zeros((TILES, PLEV - LEVELS, 8, CELLS), F32)
    lm_copy.wait()
    fm_copy.wait()
    build_weights(lm_ref, fm_ref, q_ref, w_ref)
    for copy in (c_copy, list_copy, count_copy, *tiles):
        copy.wait()
    for t in range(TILES):
        put_courant(cx_ref, dx_ref, OFF + CELLS * t, strips(c_ref, (), t))
    flat = n_ref.reshape(TILES, PLEV * 8, CELLS)
    for t in range(TILES):
        for b, pair in enumerate(BLOCKS):
            a_ref[b, pl.ds(OFF + CELLS * t, CELLS), :] = tile_block(flat, (t,), pair)
    listed_physics(a_ref, 0, list_ref, count_ref, w_ref, v_ref)
    for ref, row, t in ((first_ref, OFF, 0), (last_ref, OFF + OWN - HALO, TILES - 1)):
        for b in range(NB):
            ref[HALO * b : HALO * (b + 1), :] = a_ref[b, row : row + HALO, :]
        ref[HALO * NB : HALO * (NB + 1), :] = cx_ref[row : row + HALO, :]
        hit = jnp.int32(0)
        for slot in range(4):
            named = (slot < count_ref[1]) & (list_ref[1, slot] == t)
            hit = jnp.where(named, jnp.int32(1), hit)
        ref[HALO * (NB + 1) :, :] = jnp.broadcast_to(hit.astype(F32), (8, CELLS))
    odd = lax.axis_index("pos") % 2 == 1

    @pl.when(odd)
    def _():
        near_ref[...] = first_ref[...]
        far_ref[...] = last_ref[...]

    @pl.when(jnp.logical_not(odd))
    def _():
        near_ref[...] = last_ref[...]
        far_ref[...] = first_ref[...]


AHEAD = 3


def is_early():
    return lax.axis_index("pos") % (lax.axis_size("pos") // 2) == 0


def ahead_kernel(a_in, far_in, cx_ref, dx_ref, a_ref, far_ref, b_ref):
    @pl.when(is_early())
    def _():
        transport(a_ref, b_ref, cx_ref, dx_ref, OFF, OWN // 8, 64, 0, AHEAD)


def inside_kernel(
    a_in, cx_ref, dx_ref, w_ref, list_hbm, count_hbm,
    a_ref,
    b_ref, v_ref, list_ref, count_ref, sem,
):
    copies = fetch(((list_hbm, list_ref), (count_hbm, count_ref)), sem)
    first = jnp.where(is_early(), AHEAD, 0)
    transport(a_ref, b_ref, cx_ref, dx_ref, OFF, OWN // 8, 64, first)
    for copy in copies:
        copy.wait()
    listed_physics(a_ref, 1, list_ref, count_ref, w_ref, v_ref)


def finish_kernel(
    a_in, cx_in, dx_in, w_ref, first_ref, last_ref, near_ref, far_ref,
    out_ref, a_ref, cx_ref, dx_ref,
    left_ref, right_ref, b_ref, ea_ref, eb_ref, h_ref, v_ref, ec_ref, ed_ref, n_ref, xsem,
):
    odd = lax.axis_index("pos") % 2 == 1

    @pl.when(odd)
    def _():
        left_ref[...] = near_ref[...]
        right_ref[...] = far_ref[...]

    @pl.when(jnp.logical_not(odd))
    def _():
        left_ref[...] = far_ref[...]
        right_ref[...] = near_ref[...]

    parts = (left_ref, first_ref, last_ref, right_ref)
    for i, ref in enumerate(parts):
        rows = slice(8 + HALO * i, 8 + HALO * (i + 1))
        for b in range(NB):
            ea_ref[b, rows, :] = ref[HALO * b : HALO * (b + 1), :]
        c = ref[HALO * NB : HALO * (NB + 1), :]
        ec_ref[rows, :] = c
        ed_ref[rows, :] = 1.0 - c
    for ref, row in ((left_ref, OFF - HALO), (right_ref, OFF + OWN)):
        c = ref[HALO * NB : HALO * (NB + 1), :]
        cx_ref[row : row + HALO, :] = c
        dx_ref[row : row + HALO, :] = 1.0 - c
    flags = [jnp.max(ref[HALO * (NB + 1) :, :]) > 0.5 for ref in parts]
    transport(ea_ref, eb_ref, ec_ref, ed_ref, 8, 4 * HALO // 8, 4 * HALO // 8)
    near = [8 + HALO - 16, 8 + HALO, 8 + 3 * HALO - 16, 8 + 3 * HALO]

    @pl.when(flags[0] | flags[1] | flags[2] | flags[3])
    def _():
        for i, row in enumerate(near):
            h_ref[:, 16 * i : 16 * i + 16] = ea_ref[:, row : row + 16, :]
        physics([(h_ref, 0, 64)], w_ref, v_ref)
        for i, row in enumerate(near):

            @pl.when(flags[i])
            def _():
                ea_ref[:, row : row + 16, :] = h_ref[:, 16 * i : 16 * i + 16]

    sub = iota((8, CELLS), 0)
    for b in range(NB):
        for row in (16, 24, 32):
            a_ref[b, row : row + 8, :] = ea_ref[b, row : row + 8, :]
        a_ref[b, 40:48, :] = jnp.where(sub < 4, ea_ref[b, 40:48, :], a_ref[b, 40:48, :])
        back = OFF + OWN - HALO - (8 + 2 * HALO)
        row = OFF + OWN - 16
        a_ref[b, row : row + 8, :] = jnp.where(
            sub >= 4, ea_ref[b, row - back : row - back + 8, :], a_ref[b, row : row + 8, :]
        )
        for row in (OFF + OWN - 8, OFF + OWN, OFF + OWN + 8):
            a_ref[b, row : row + 8, :] = ea_ref[b, row - back : row - back + 8, :]
    transport(a_ref, b_ref, cx_ref, dx_ref, OFF - 16, OWN // 8 + 4, 66)
    flat = n_ref.reshape(TILES, PLEV * 8, CELLS)
    copies = []
    for group in (range(0, 4), range(4, 7), range(7, 8)):
        for t in group:
            for b, pair in enumerate(BLOCKS):
                block = a_ref[b, pl.ds(OFF + CELLS * t, CELLS), :].T
                for h, f in enumerate(pair):
                    for g in range(PLEV // 8):
                        flat[t, pl.ds(64 * g + f, 8, stride=8), :] = block[
                            HALF * h + 8 * g : HALF * h + 8 * g + 8
                        ]
        for t in group:
            copies += fetch(
                [(n_ref.at[t, pl.ds(0, LEVELS)], out_ref.at[:, pl.ds(8 * t, 8), :])],
                xsem.at[pl.ds(t, 1)],
            )
    for copy in copies:
        copy.wait()


VM = pl.BlockSpec(memory_space=pltpu.VMEM)
HBM = pl.BlockSpec(memory_space=pltpu.HBM)
ANY = pl.BlockSpec(memory_space=pl.ANY)
SMALL = [
    pltpu.VMEM((PLEV * TILES, CELLS), F32),
    pltpu.SMEM((CYCLES, 4), jnp.int32),
    pltpu.SMEM((CYCLES,), jnp.int32),
]
LIMIT = 40 << 20
STATE = (NB, XROWS, CELLS)
COLUMN = (XROWS, CELLS)
ENDS = (HALO * (NB + 1) + 8, CELLS)
BATCH = pltpu.VMEM((NB, 4 * CELLS, CELLS), F32)
NATURAL = pltpu.VMEM((TILES, PLEV, 8, CELLS), F32)


def local(state, courant, level_mix, field_mix, send_list, send_count):
    shape = jax.ShapeDtypeStruct
    hbm = lambda v: pltpu.with_memory_space_constraint(v, pltpu.HBM)
    x = state.reshape(FIELDS, LEVELS, TILES, CELLS).transpose(1, 2, 0, 3)
    x = hbm(x.reshape(LEVELS, TILES * FIELDS, CELLS))
    c = hbm(courant.reshape(LEVELS * TILES, CELLS))
    chosen, count = hbm(send_list.reshape(CYCLES, 4)), hbm(send_count.reshape(CYCLES))
    a, cx, dx, w, first, last, near, far = pl.pallas_call(
        column_kernel,
        name="column",
        out_shape=(
            shape(STATE, F32), shape(COLUMN, F32), shape(COLUMN, F32),
            shape((2 * WIDE, WIDE), BF16), *(shape(ENDS, F32),) * 4,
        ),
        in_specs=[HBM] * 6,
        out_specs=(VM,) * 8,
        scratch_shapes=[
            NATURAL,
            BATCH,
            pltpu.VMEM((CELLS, CELLS), F32),
            SMALL[0],
            pltpu.VMEM((LEVELS, LEVELS), F32),
            pltpu.SMEM((FIELDS, FIELDS), F32),
            *SMALL[1:],
            pltpu.SemaphoreType.DMA((5,)),
            pltpu.SemaphoreType.DMA((TILES,)),
        ],
        compiler_params=pltpu.CompilerParams(vmem_limit_bytes=LIMIT),
    )(x, c, hbm(level_mix), hbm(field_mix), chosen, count)
    n = lax.axis_size("pos")
    near = lax.ppermute(near, "pos", [(i, i ^ 1) for i in range(n)])
    params = pltpu.CompilerParams(vmem_limit_bytes=LIMIT)
    cost = pl.CostEstimate(flops=4_000_000_000, bytes_accessed=8_000_000, transcendentals=0)
    a, far = pl.pallas_call(
        ahead_kernel,
        name="ahead",
        out_shape=(shape(STATE, F32), shape(ENDS, F32)),
        in_specs=[VM] * 4,
        out_specs=(VM, VM),
        input_output_aliases={0: 0, 1: 1},
        scratch_shapes=[pltpu.VMEM(STATE, F32)],
        compiler_params=params,
        cost_estimate=cost,
    )(a, far, cx, dx)
    far = lax.ppermute(far, "pos", [(i, (i + (1 if i % 2 else -1)) % n) for i in range(n)])
    mid = pl.pallas_call(
        inside_kernel,
        name="inside",
        out_shape=shape(STATE, F32),
        in_specs=[VM] * 4 + [HBM] * 2,
        out_specs=VM,
        input_output_aliases={0: 0},
        scratch_shapes=[
            pltpu.VMEM(STATE, F32), BATCH, *SMALL[1:], pltpu.SemaphoreType.DMA((2,))
        ],
        compiler_params=params,
        cost_estimate=cost,
    )(a, cx, dx, w, chosen, count)
    out, *_ = pl.pallas_call(
        finish_kernel,
        name="finish",
        out_shape=(
            shape((LEVELS, TILES * FIELDS, CELLS), F32),
            shape(STATE, F32), shape(COLUMN, F32), shape(COLUMN, F32),
        ),
        in_specs=[VM] * 8,
        out_specs=(ANY, VM, VM, VM),
        input_output_aliases={0: 1, 1: 2, 2: 3},
        scratch_shapes=[
            pltpu.VMEM(ENDS, F32),
            pltpu.VMEM(ENDS, F32),
            pltpu.VMEM(STATE, F32),
            pltpu.VMEM((NB, EROWS, CELLS), F32),
            pltpu.VMEM((NB, EROWS, CELLS), F32),
            pltpu.VMEM((NB, 64, CELLS), F32),
            pltpu.VMEM((NB, 64, CELLS), F32),
            pltpu.VMEM((EROWS, CELLS), F32),
            pltpu.VMEM((EROWS, CELLS), F32),
            NATURAL,
            pltpu.SemaphoreType.DMA((TILES,)),
        ],
        compiler_params=pltpu.CompilerParams(vmem_limit_bytes=LIMIT),
    )(mid, cx, dx, w, first, last, near, far)
    out = out.reshape(LEVELS, TILES, FIELDS, CELLS).transpose(2, 0, 1, 3)
    return out.reshape(1, FIELDS, LEVELS, TILES * CELLS)


def solution(mesh):
    in_specs = (
        P("chan", None, None, "pos"),
        P("chan", None, "pos"),
        P(),
        P(),
        P(None, "chan", "pos", None),
        P(None, "chan", "pos"),
    )
    out_specs = P("chan", None, None, "pos")
    return jax.shard_map(local, mesh=mesh, in_specs=in_specs, out_specs=out_specs, check_vma=False)
```

```python
import jax
import jax.numpy as jnp
from jax import lax
from jax.experimental import pallas as pl
from jax.experimental.pallas import tpu as pltpu
from jax.sharding import PartitionSpec as P


LEVELS = 50
FIELDS = 8
CELLS = 128
SECTIONS = 12
SWEEPS = 4
CYCLES = 2
TILES = 8
BUOYANCY = 0.4
F32 = jnp.float32
BF16 = jnp.bfloat16

BLOCKS = ((2, 0), (1, 3), (4, 6), (5, 7))
HALF = 64
HALO = CYCLES * SECTIONS
OFF = HALO + 8
OWN = TILES * CELLS
XROWS = OFF + OWN + HALO + 8
EROWS = 8 + 4 * HALO + 8
NB = len(BLOCKS)
WIDE = NB * CELLS
PLEV = 56


def iota(shape, dim):
    return lax.broadcasted_iota(jnp.int32, shape, dim)


def fetch(pairs, sem):
    copies = [pltpu.make_async_copy(a, b, sem.at[i]) for i, (a, b) in enumerate(pairs)]
    for copy in copies:
        copy.start()
    return copies


def strips(ref, index, row):
    take = [ref[(*index, pl.ds(64 * g + row, 8, stride=8), slice(None))] for g in range(PLEV // 8)]
    return take + [jnp.zeros((8, CELLS), F32)]


def build_weights(lm_ref, fm_ref, q_ref, w_ref):
    q_ref[...] = jnp.zeros((CELLS, CELLS), F32)
    lm = lm_ref[...]
    q_ref[:LEVELS, :LEVELS] = lm
    q_ref[HALF : HALF + LEVELS, :LEVELS] = lm
    q_ref[...] = q_ref[...].T
    lane = iota((16, CELLS), 1)
    sub = iota((16, CELLS), 0)
    low = lane < HALF
    eyes = [(lane % HALF == sub + r) & (sub + r < LEVELS) for r in range(0, HALF, 16)]
    for kb, pair_k in enumerate(BLOCKS):
        for kh, g in enumerate(pair_k):
            for nb, (fa, fb) in enumerate(BLOCKS):
                mix = jnp.where(low, fm_ref[fa, g], fm_ref[fb, g])
                for i, eye in enumerate(eyes):
                    row = CELLS * kb + HALF * kh + 16 * i
                    w = jnp.where(eye, mix, 0.0)
                    if g in (fa, fb):
                        lt = q_ref[16 * i : 16 * i + 16, :]
                        w = w + (jnp.where(low, lt, 0.0) if g == fa else jnp.where(low, 0.0, lt))
                    hi = w.astype(BF16)
                    cols = slice(CELLS * nb, CELLS * (nb + 1))
                    w_ref[row : row + 16, cols] = hi
                    w_ref[WIDE + row : WIDE + row + 16, cols] = (w - hi.astype(F32)).astype(BF16)


def physics(parts, w_ref, v_ref):
    starts = [sum(rows for _, _, rows in parts[:i]) for i in range(len(parts))]
    total = sum(rows for _, _, rows in parts)
    high = w_ref[:WIDE, :]
    rhs = jnp.concatenate([high, high, w_ref[WIDE:, :]], axis=0)

    def block(sweep_index, b):
        if sweep_index > 0:
            return v_ref[b, :total]
        return jnp.concatenate([ref[b, pl.ds(row, rows), :] for ref, row, rows in parts], axis=0)

    for sweep_index in range(SWEEPS):
        highs, lows = [], []
        for b in range(NB):
            t = jnp.tanh(block(sweep_index, b))
            hi = t.astype(BF16)
            highs.append(hi)
            lows.append((t - hi.astype(F32)).astype(BF16))
        lhs = jnp.concatenate(highs + lows + highs, axis=1)
        acc = jnp.dot(lhs, rhs, preferred_element_type=F32)
        for b in range(NB):
            new = block(sweep_index, b) + acc[:, CELLS * b : CELLS * (b + 1)]
            if sweep_index < SWEEPS - 1:
                v_ref[b, :total] = new
            else:
                for at, (ref, row, rows) in zip(starts, parts):
                    ref[b, pl.ds(row, rows), :] = new[at : at + rows]


def listed_physics(ref, cycle, list_ref, count_ref, w_ref, v_ref):
    for count in range(1, 5):

        @pl.when(count_ref[cycle] == count)
        def _():
            rows = [pl.multiple_of(OFF + CELLS * list_ref[cycle, k], 8) for k in range(count)]
            physics([(ref, row, CELLS) for row in rows], w_ref, v_ref)


def section(src, dst, c_ref, d_ref, kv, base, groups):
    for i in range(groups):
        row = base + 8 * i
        here, before, after = pl.ds(row, 8), pl.ds(row - 1, 8), pl.ds(row + 1, 8)
        d, cm, cp = d_ref[here, :], c_ref[before, :], c_ref[after, :]
        x = []
        for b in range(NB):
            side, coef = (before, cm) if b % 2 == 0 else (after, cp)
            x.append(d * src[b, here, :] + coef * src[b, side, :])
        x[1] = x[1] + kv * x[0]
        x[0] = x[0] - kv * x[1]
        for b in range(NB):
            dst[b, here, :] = x[b]


def transport(a_ref, b_ref, c_ref, d_ref, base, groups, unroll, first=0, last=SECTIONS // 2):
    kv = jnp.where(iota((8, CELLS), 1) < HALF, BUOYANCY, 0.0)

    def sweep(src, dst):
        def body(i, carry):
            row = pl.multiple_of(base + i * (8 * unroll), 8)
            section(src, dst, c_ref, d_ref, kv, row, unroll)
            return carry

        if groups == unroll:
            section(src, dst, c_ref, d_ref, kv, base, groups)
        else:
            lax.fori_loop(0, groups // unroll, body, 0)

    def two(_, carry):
        sweep(a_ref, b_ref)
        sweep(b_ref, a_ref)
        return carry

    lax.fori_loop(first, last, two, 0)


def put_courant(c_ref, d_ref, row, block):
    c = jnp.concatenate(block + block, axis=0).T
    c_ref[pl.ds(row, CELLS), :] = c
    d_ref[pl.ds(row, CELLS), :] = 1.0 - c


def tile_block(ref, index, pair):
    return jnp.concatenate(strips(ref, index, pair[0]) + strips(ref, index, pair[1]), axis=0).T


def column_kernel(
    x_ref, c_hbm, lm_hbm, fm_hbm, list_hbm, count_hbm,
    a_ref, cx_ref, dx_ref, w_ref, first_ref, last_ref, near_ref, far_ref,
    n_ref, v_ref, q_ref, c_ref, lm_ref, fm_ref, list_ref, count_ref, sem, xsem,
):
    lm_copy, fm_copy, c_copy, list_copy, count_copy = fetch(
        (
            (lm_hbm, lm_ref), (fm_hbm, fm_ref), (c_hbm, c_ref.at[pl.ds(0, LEVELS * TILES)]),
            (list_hbm, list_ref), (count_hbm, count_ref),
        ),
        sem,
    )
    tiles = fetch(
        [
            (x_ref.at[:, pl.ds(8 * t, 8), :], n_ref.at[t, pl.ds(0, LEVELS)])
            for t in range(TILES)
        ],
        xsem,
    )
    c_ref[LEVELS * TILES :, :] = jnp.zeros((48, CELLS), F32)
    n_ref[:, LEVELS:] = jnp.zeros((TILES, PLEV - LEVELS, 8, CELLS), F32)
    lm_copy.wait()
    fm_copy.wait()
    build_weights(lm_ref, fm_ref, q_ref, w_ref)
    for copy in (c_copy, list_copy, count_copy, *tiles):
        copy.wait()
    for t in range(TILES):
        put_courant(cx_ref, dx_ref, OFF + CELLS * t, strips(c_ref, (), t))
    flat = n_ref.reshape(TILES, PLEV * 8, CELLS)
    for t in range(TILES):
        for b, pair in enumerate(BLOCKS):
            a_ref[b, pl.ds(OFF + CELLS * t, CELLS), :] = tile_block(flat, (t,), pair)
    listed_physics(a_ref, 0, list_ref, count_ref, w_ref, v_ref)
    for ref, row, t in ((first_ref, OFF, 0), (last_ref, OFF + OWN - HALO, TILES - 1)):
        for b in range(NB):
            ref[HALO * b : HALO * (b + 1), :] = a_ref[b, row : row + HALO, :]
        ref[HALO * NB : HALO * (NB + 1), :] = cx_ref[row : row + HALO, :]
        hit = jnp.int32(0)
        for slot in range(4):
            named = (slot < count_ref[1]) & (list_ref[1, slot] == t)
            hit = jnp.where(named, jnp.int32(1), hit)
        ref[HALO * (NB + 1) :, :] = jnp.broadcast_to(hit.astype(F32), (8, CELLS))
    odd = lax.axis_index("pos") % 2 == 1

    @pl.when(odd)
    def _():
        near_ref[...] = first_ref[...]
        far_ref[...] = last_ref[...]

    @pl.when(jnp.logical_not(odd))
    def _():
        near_ref[...] = last_ref[...]
        far_ref[...] = first_ref[...]


AHEAD = 3


def is_early():
    return lax.axis_index("pos") % (lax.axis_size("pos") // 2) == 0


def ahead_kernel(a_in, far_in, cx_ref, dx_ref, a_ref, far_ref, b_ref):
    @pl.when(is_early())
    def _():
        transport(a_ref, b_ref, cx_ref, dx_ref, OFF, OWN // 8, 64, 0, AHEAD)


def inside_kernel(
    a_in, cx_ref, dx_ref, w_ref, list_hbm, count_hbm,
    a_ref,
    b_ref, v_ref, list_ref, count_ref, sem,
):
    copies = fetch(((list_hbm, list_ref), (count_hbm, count_ref)), sem)
    first = jnp.where(is_early(), AHEAD, 0)
    transport(a_ref, b_ref, cx_ref, dx_ref, OFF, OWN // 8, 64, first)
    for copy in copies:
        copy.wait()
    listed_physics(a_ref, 1, list_ref, count_ref, w_ref, v_ref)


def finish_kernel(
    a_in, cx_in, dx_in, w_ref, first_ref, last_ref, near_ref, far_ref,
    out_ref, a_ref, cx_ref, dx_ref,
    left_ref, right_ref, b_ref, ea_ref, eb_ref, h_ref, v_ref, ec_ref, ed_ref, n_ref, xsem,
):
    odd = lax.axis_index("pos") % 2 == 1

    @pl.when(odd)
    def _():
        left_ref[...] = near_ref[...]
        right_ref[...] = far_ref[...]

    @pl.when(jnp.logical_not(odd))
    def _():
        left_ref[...] = far_ref[...]
        right_ref[...] = near_ref[...]

    parts = (left_ref, first_ref, last_ref, right_ref)
    for i, ref in enumerate(parts):
        rows = slice(8 + HALO * i, 8 + HALO * (i + 1))
        for b in range(NB):
            ea_ref[b, rows, :] = ref[HALO * b : HALO * (b + 1), :]
        c = ref[HALO * NB : HALO * (NB + 1), :]
        ec_ref[rows, :] = c
        ed_ref[rows, :] = 1.0 - c
    for ref, row in ((left_ref, OFF - HALO), (right_ref, OFF + OWN)):
        c = ref[HALO * NB : HALO * (NB + 1), :]
        cx_ref[row : row + HALO, :] = c
        dx_ref[row : row + HALO, :] = 1.0 - c
    flags = [jnp.max(ref[HALO * (NB + 1) :, :]) > 0.5 for ref in parts]
    transport(ea_ref, eb_ref, ec_ref, ed_ref, 8, 4 * HALO // 8, 4 * HALO // 8)
    near = [8 + HALO - 16, 8 + HALO, 8 + 3 * HALO - 16, 8 + 3 * HALO]

    @pl.when(flags[0] | flags[1] | flags[2] | flags[3])
    def _():
        for i, row in enumerate(near):
            h_ref[:, 16 * i : 16 * i + 16] = ea_ref[:, row : row + 16, :]
        physics([(h_ref, 0, 64)], w_ref, v_ref)
        for i, row in enumerate(near):

            @pl.when(flags[i])
            def _():
                ea_ref[:, row : row + 16, :] = h_ref[:, 16 * i : 16 * i + 16]

    sub = iota((8, CELLS), 0)
    for b in range(NB):
        for row in (16, 24, 32):
            a_ref[b, row : row + 8, :] = ea_ref[b, row : row + 8, :]
        a_ref[b, 40:48, :] = jnp.where(sub < 4, ea_ref[b, 40:48, :], a_ref[b, 40:48, :])
        back = OFF + OWN - HALO - (8 + 2 * HALO)
        row = OFF + OWN - 16
        a_ref[b, row : row + 8, :] = jnp.where(
            sub >= 4, ea_ref[b, row - back : row - back + 8, :], a_ref[b, row : row + 8, :]
        )
        for row in (OFF + OWN - 8, OFF + OWN, OFF + OWN + 8):
            a_ref[b, row : row + 8, :] = ea_ref[b, row - back : row - back + 8, :]
    transport(a_ref, b_ref, cx_ref, dx_ref, OFF - 16, OWN // 8 + 4, 66)
    flat = n_ref.reshape(TILES, PLEV * 8, CELLS)
    copies = []
    for group in (range(0, 4), range(4, 7), range(7, 8)):
        for t in group:
            for b, pair in enumerate(BLOCKS):
                block = a_ref[b, pl.ds(OFF + CELLS * t, CELLS), :].T
                for h, f in enumerate(pair):
                    for g in range(PLEV // 8):
                        flat[t, pl.ds(64 * g + f, 8, stride=8), :] = block[
                            HALF * h + 8 * g : HALF * h + 8 * g + 8
                        ]
        for t in group:
            copies += fetch(
                [(n_ref.at[t, pl.ds(0, LEVELS)], out_ref.at[:, pl.ds(8 * t, 8), :])],
                xsem.at[pl.ds(t, 1)],
            )
    for copy in copies:
        copy.wait()


VM = pl.BlockSpec(memory_space=pltpu.VMEM)
HBM = pl.BlockSpec(memory_space=pltpu.HBM)
ANY = pl.BlockSpec(memory_space=pl.ANY)
SMALL = [
    pltpu.VMEM((PLEV * TILES, CELLS), F32),
    pltpu.SMEM((CYCLES, 4), jnp.int32),
    pltpu.SMEM((CYCLES,), jnp.int32),
]
LIMIT = 40 << 20
STATE = (NB, XROWS, CELLS)
COLUMN = (XROWS, CELLS)
ENDS = (HALO * (NB + 1) + 8, CELLS)
BATCH = pltpu.VMEM((NB, 4 * CELLS, CELLS), F32)
NATURAL = pltpu.VMEM((TILES, PLEV, 8, CELLS), F32)


def local(state, courant, level_mix, field_mix, send_list, send_count):
    shape = jax.ShapeDtypeStruct
    hbm = lambda v: pltpu.with_memory_space_constraint(v, pltpu.HBM)
    x = state.reshape(FIELDS, LEVELS, TILES, CELLS).transpose(1, 2, 0, 3)
    x = hbm(x.reshape(LEVELS, TILES * FIELDS, CELLS))
    c = hbm(courant.reshape(LEVELS * TILES, CELLS))
    chosen, count = hbm(send_list.reshape(CYCLES, 4)), hbm(send_count.reshape(CYCLES))
    a, cx, dx, w, first, last, near, far = pl.pallas_call(
        column_kernel,
        name="column",
        out_shape=(
            shape(STATE, F32), shape(COLUMN, F32), shape(COLUMN, F32),
            shape((2 * WIDE, WIDE), BF16), *(shape(ENDS, F32),) * 4,
        ),
        in_specs=[HBM] * 6,
        out_specs=(VM,) * 8,
        scratch_shapes=[
            NATURAL,
            BATCH,
            pltpu.VMEM((CELLS, CELLS), F32),
            SMALL[0],
            pltpu.VMEM((LEVELS, LEVELS), F32),
            pltpu.SMEM((FIELDS, FIELDS), F32),
            *SMALL[1:],
            pltpu.SemaphoreType.DMA((5,)),
            pltpu.SemaphoreType.DMA((TILES,)),
        ],
        compiler_params=pltpu.CompilerParams(vmem_limit_bytes=LIMIT),
    )(x, c, hbm(level_mix), hbm(field_mix), chosen, count)
    n = lax.axis_size("pos")
    near = lax.ppermute(near, "pos", [(i, i ^ 1) for i in range(n)])
    params = pltpu.CompilerParams(vmem_limit_bytes=LIMIT)
    cost = pl.CostEstimate(flops=4_000_000_000, bytes_accessed=8_000_000, transcendentals=0)
    ahead = pl.pallas_call(
        ahead_kernel,
        name="ahead",
        out_shape=(shape(STATE, F32), shape(ENDS, F32)),
        in_specs=[VM] * 4,
        out_specs=(VM, VM),
        input_output_aliases={0: 0, 1: 1},
        scratch_shapes=[pltpu.VMEM(STATE, F32)],
        compiler_params=params,
        cost_estimate=cost,
    )
    a, far = ahead(a, far, cx, dx)
    far = lax.ppermute(far, "pos", [(i, (i + (1 if i % 2 else -1)) % n) for i in range(n)])
    mid = pl.pallas_call(
        inside_kernel,
        name="inside",
        out_shape=shape(STATE, F32),
        in_specs=[VM] * 4 + [HBM] * 2,
        out_specs=VM,
        input_output_aliases={0: 0},
        scratch_shapes=[
            pltpu.VMEM(STATE, F32), BATCH, *SMALL[1:], pltpu.SemaphoreType.DMA((2,))
        ],
        compiler_params=params,
        cost_estimate=cost,
    )(a, cx, dx, w, chosen, count)
    out, *_ = pl.pallas_call(
        finish_kernel,
        name="finish",
        out_shape=(
            shape((LEVELS, TILES * FIELDS, CELLS), F32),
            shape(STATE, F32), shape(COLUMN, F32), shape(COLUMN, F32),
        ),
        in_specs=[VM] * 8,
        out_specs=(ANY, VM, VM, VM),
        input_output_aliases={0: 1, 1: 2, 2: 3},
        scratch_shapes=[
            pltpu.VMEM(ENDS, F32),
            pltpu.VMEM(ENDS, F32),
            pltpu.VMEM(STATE, F32),
            pltpu.VMEM((NB, EROWS, CELLS), F32),
            pltpu.VMEM((NB, EROWS, CELLS), F32),
            pltpu.VMEM((NB, 64, CELLS), F32),
            pltpu.VMEM((NB, 64, CELLS), F32),
            pltpu.VMEM((EROWS, CELLS), F32),
            pltpu.VMEM((EROWS, CELLS), F32),
            NATURAL,
            pltpu.SemaphoreType.DMA((TILES,)),
        ],
        compiler_params=pltpu.CompilerParams(vmem_limit_bytes=LIMIT),
    )(mid, cx, dx, w, first, last, near, far)
    out = out.reshape(LEVELS, TILES, FIELDS, CELLS).transpose(2, 0, 1, 3)
    return out.reshape(1, FIELDS, LEVELS, TILES * CELLS)


def solution(mesh):
    in_specs = (
        P("chan", None, None, "pos"),
        P("chan", None, "pos"),
        P(),
        P(),
        P(None, "chan", "pos", None),
        P(None, "chan", "pos"),
    )
    out_specs = P("chan", None, None, "pos")
    return jax.shard_map(local, mesh=mesh, in_specs=in_specs, out_specs=out_specs, check_vma=False)
```

```python
import jax
import jax.numpy as jnp
from jax import lax
from jax.experimental import pallas as pl
from jax.experimental.pallas import tpu as pltpu
from jax.sharding import PartitionSpec as P


LEVELS = 50
FIELDS = 8
CELLS = 128
SECTIONS = 12
SWEEPS = 4
CYCLES = 2
TILES = 8
BUOYANCY = 0.4
F32 = jnp.float32
BF16 = jnp.bfloat16

BLOCKS = ((2, 0), (1, 3), (4, 6), (5, 7))
HALF = 64
HALO = CYCLES * SECTIONS
OFF = HALO + 8
OWN = TILES * CELLS
XROWS = OFF + OWN + HALO + 8
EROWS = 8 + 4 * HALO + 8
NB = len(BLOCKS)
WIDE = NB * CELLS
PLEV = 56


def iota(shape, dim):
    return lax.broadcasted_iota(jnp.int32, shape, dim)


def fetch(pairs, sem):
    copies = [pltpu.make_async_copy(a, b, sem.at[i]) for i, (a, b) in enumerate(pairs)]
    for copy in copies:
        copy.start()
    return copies


def strips(ref, index, row):
    take = [ref[(*index, pl.ds(64 * g + row, 8, stride=8), slice(None))] for g in range(PLEV // 8)]
    return take + [jnp.zeros((8, CELLS), F32)]


def build_weights(lm_ref, fm_ref, q_ref, w_ref):
    q_ref[...] = jnp.zeros((CELLS, CELLS), F32)
    lm = lm_ref[...]
    q_ref[:LEVELS, :LEVELS] = lm
    q_ref[HALF : HALF + LEVELS, :LEVELS] = lm
    q_ref[...] = q_ref[...].T
    lane = iota((16, CELLS), 1)
    sub = iota((16, CELLS), 0)
    low = lane < HALF
    eyes = [(lane % HALF == sub + r) & (sub + r < LEVELS) for r in range(0, HALF, 16)]
    for kb, pair_k in enumerate(BLOCKS):
        for kh, g in enumerate(pair_k):
            for nb, (fa, fb) in enumerate(BLOCKS):
                mix = jnp.where(low, fm_ref[fa, g], fm_ref[fb, g])
                for i, eye in enumerate(eyes):
                    row = CELLS * kb + HALF * kh + 16 * i
                    w = jnp.where(eye, mix, 0.0)
                    if g in (fa, fb):
                        lt = q_ref[16 * i : 16 * i + 16, :]
                        w = w + (jnp.where(low, lt, 0.0) if g == fa else jnp.where(low, 0.0, lt))
                    hi = w.astype(BF16)
                    cols = slice(CELLS * nb, CELLS * (nb + 1))
                    w_ref[row : row + 16, cols] = hi
                    w_ref[WIDE + row : WIDE + row + 16, cols] = (w - hi.astype(F32)).astype(BF16)


def physics(parts, w_ref, v_ref):
    starts = [sum(rows for _, _, rows in parts[:i]) for i in range(len(parts))]
    total = sum(rows for _, _, rows in parts)
    high = w_ref[:WIDE, :]
    rhs = jnp.concatenate([high, high, w_ref[WIDE:, :]], axis=0)

    def block(sweep_index, b):
        if sweep_index > 0:
            return v_ref[b, :total]
        return jnp.concatenate([ref[b, pl.ds(row, rows), :] for ref, row, rows in parts], axis=0)

    for sweep_index in range(SWEEPS):
        highs, lows = [], []
        for b in range(NB):
            t = jnp.tanh(block(sweep_index, b))
            hi = t.astype(BF16)
            highs.append(hi)
            lows.append((t - hi.astype(F32)).astype(BF16))
        lhs = jnp.concatenate(highs + lows + highs, axis=1)
        acc = jnp.dot(lhs, rhs, preferred_element_type=F32)
        for b in range(NB):
            new = block(sweep_index, b) + acc[:, CELLS * b : CELLS * (b + 1)]
            if sweep_index < SWEEPS - 1:
                v_ref[b, :total] = new
            else:
                for at, (ref, row, rows) in zip(starts, parts):
                    ref[b, pl.ds(row, rows), :] = new[at : at + rows]


def listed_physics(ref, cycle, list_ref, count_ref, w_ref, v_ref):
    for count in range(1, 5):

        @pl.when(count_ref[cycle] == count)
        def _():
            rows = [pl.multiple_of(OFF + CELLS * list_ref[cycle, k], 8) for k in range(count)]
            physics([(ref, row, CELLS) for row in rows], w_ref, v_ref)


def section(src, dst, c_ref, d_ref, kv, base, groups):
    for i in range(groups):
        row = base + 8 * i
        here, before, after = pl.ds(row, 8), pl.ds(row - 1, 8), pl.ds(row + 1, 8)
        d, cm, cp = d_ref[here, :], c_ref[before, :], c_ref[after, :]
        x = []
        for b in range(NB):
            side, coef = (before, cm) if b % 2 == 0 else (after, cp)
            x.append(d * src[b, here, :] + coef * src[b, side, :])
        x[1] = x[1] + kv * x[0]
        x[0] = x[0] - kv * x[1]
        for b in range(NB):
            dst[b, here, :] = x[b]


def transport(a_ref, b_ref, c_ref, d_ref, base, groups, unroll, first=0, last=SECTIONS // 2):
    kv = jnp.where(iota((8, CELLS), 1) < HALF, BUOYANCY, 0.0)

    def sweep(src, dst):
        def body(i, carry):
            row = pl.multiple_of(base + i * (8 * unroll), 8)
            section(src, dst, c_ref, d_ref, kv, row, unroll)
            return carry

        if groups == unroll:
            section(src, dst, c_ref, d_ref, kv, base, groups)
        else:
            lax.fori_loop(0, groups // unroll, body, 0)

    def two(_, carry):
        sweep(a_ref, b_ref)
        sweep(b_ref, a_ref)
        return carry

    lax.fori_loop(first, last, two, 0)


def put_courant(c_ref, d_ref, row, block):
    c = jnp.concatenate(block + block, axis=0).T
    c_ref[pl.ds(row, CELLS), :] = c
    d_ref[pl.ds(row, CELLS), :] = 1.0 - c


def tile_block(ref, index, pair):
    return jnp.concatenate(strips(ref, index, pair[0]) + strips(ref, index, pair[1]), axis=0)


def mxu_flip(x, y):
    eye = (iota((CELLS, 2 * CELLS), 0) == iota((CELLS, 2 * CELLS), 1) % CELLS).astype(F32).astype(BF16)
    both = jnp.concatenate([x, y], axis=0)
    hi = both.astype(BF16)
    lo = (both - hi.astype(F32)).astype(BF16)
    out = lax.dot_general(
        eye,
        jnp.concatenate([hi, lo], axis=1),
        (((1,), (1,)), ((), ())),
        preferred_element_type=F32,
    )
    return out[:, :CELLS], out[:, CELLS:]


def flip_all(blocks):
    return (blocks[0].T, blocks[1].T, *mxu_flip(blocks[2], blocks[3]))


def column_kernel(
    x_ref, c_hbm, lm_hbm, fm_hbm, list_hbm, count_hbm,
    a_ref, cx_ref, dx_ref, w_ref, first_ref, last_ref, near_ref, far_ref,
    n_ref, v_ref, q_ref, c_ref, lm_ref, fm_ref, list_ref, count_ref, sem, xsem,
):
    lm_copy, fm_copy, c_copy, list_copy, count_copy = fetch(
        (
            (lm_hbm, lm_ref), (fm_hbm, fm_ref), (c_hbm, c_ref.at[pl.ds(0, LEVELS * TILES)]),
            (list_hbm, list_ref), (count_hbm, count_ref),
        ),
        sem,
    )
    tiles = fetch(
        [
            (x_ref.at[:, pl.ds(8 * t, 8), :], n_ref.at[t, pl.ds(0, LEVELS)])
            for t in range(TILES)
        ],
        xsem,
    )
    c_ref[LEVELS * TILES :, :] = jnp.zeros((48, CELLS), F32)
    n_ref[:, LEVELS:] = jnp.zeros((TILES, PLEV - LEVELS, 8, CELLS), F32)
    lm_copy.wait()
    fm_copy.wait()
    build_weights(lm_ref, fm_ref, q_ref, w_ref)
    for copy in (c_copy, list_copy, count_copy, *tiles):
        copy.wait()
    for t in range(TILES):
        put_courant(cx_ref, dx_ref, OFF + CELLS * t, strips(c_ref, (), t))
    flat = n_ref.reshape(TILES, PLEV * 8, CELLS)
    for t in range(TILES):
        for b, block in enumerate(flip_all([tile_block(flat, (t,), pair) for pair in BLOCKS])):
            a_ref[b, pl.ds(OFF + CELLS * t, CELLS), :] = block
    listed_physics(a_ref, 0, list_ref, count_ref, w_ref, v_ref)
    for ref, row, t in ((first_ref, OFF, 0), (last_ref, OFF + OWN - HALO, TILES - 1)):
        for b in range(NB):
            ref[HALO * b : HALO * (b + 1), :] = a_ref[b, row : row + HALO, :]
        ref[HALO * NB : HALO * (NB + 1), :] = cx_ref[row : row + HALO, :]
        hit = jnp.int32(0)
        for slot in range(4):
            named = (slot < count_ref[1]) & (list_ref[1, slot] == t)
            hit = jnp.where(named, jnp.int32(1), hit)
        ref[HALO * (NB + 1) :, :] = jnp.broadcast_to(hit.astype(F32), (8, CELLS))
    odd = lax.axis_index("pos") % 2 == 1

    @pl.when(odd)
    def _():
        near_ref[...] = first_ref[...]
        far_ref[...] = last_ref[...]

    @pl.when(jnp.logical_not(odd))
    def _():
        near_ref[...] = last_ref[...]
        far_ref[...] = first_ref[...]


AHEAD = 3


def is_early():
    return lax.axis_index("pos") % (lax.axis_size("pos") // 2) == 0


def ahead_kernel(a_in, far_in, cx_ref, dx_ref, a_ref, far_ref, b_ref):
    @pl.when(is_early())
    def _():
        transport(a_ref, b_ref, cx_ref, dx_ref, OFF, OWN // 8, 64, 0, AHEAD)


def inside_kernel(
    a_in, cx_ref, dx_ref, w_ref, list_hbm, count_hbm,
    a_ref,
    b_ref, v_ref, list_ref, count_ref, sem,
):
    copies = fetch(((list_hbm, list_ref), (count_hbm, count_ref)), sem)
    first = jnp.where(is_early(), AHEAD, 0)
    transport(a_ref, b_ref, cx_ref, dx_ref, OFF, OWN // 8, 64, first)
    for copy in copies:
        copy.wait()
    listed_physics(a_ref, 1, list_ref, count_ref, w_ref, v_ref)


def finish_kernel(
    a_in, cx_in, dx_in, w_ref, first_ref, last_ref, near_ref, far_ref,
    out_ref, a_ref, cx_ref, dx_ref,
    left_ref, right_ref, b_ref, ea_ref, eb_ref, h_ref, v_ref, ec_ref, ed_ref, n_ref, xsem,
):
    odd = lax.axis_index("pos") % 2 == 1

    @pl.when(odd)
    def _():
        left_ref[...] = near_ref[...]
        right_ref[...] = far_ref[...]

    @pl.when(jnp.logical_not(odd))
    def _():
        left_ref[...] = far_ref[...]
        right_ref[...] = near_ref[...]

    parts = (left_ref, first_ref, last_ref, right_ref)
    for i, ref in enumerate(parts):
        rows = slice(8 + HALO * i, 8 + HALO * (i + 1))
        for b in range(NB):
            ea_ref[b, rows, :] = ref[HALO * b : HALO * (b + 1), :]
        c = ref[HALO * NB : HALO * (NB + 1), :]
        ec_ref[rows, :] = c
        ed_ref[rows, :] = 1.0 - c
    for ref, row in ((left_ref, OFF - HALO), (right_ref, OFF + OWN)):
        c = ref[HALO * NB : HALO * (NB + 1), :]
        cx_ref[row : row + HALO, :] = c
        dx_ref[row : row + HALO, :] = 1.0 - c
    flags = [jnp.max(ref[HALO * (NB + 1) :, :]) > 0.5 for ref in parts]
    transport(ea_ref, eb_ref, ec_ref, ed_ref, 8, 4 * HALO // 8, 4 * HALO // 8)
    near = [8 + HALO - 16, 8 + HALO, 8 + 3 * HALO - 16, 8 + 3 * HALO]

    @pl.when(flags[0] | flags[1] | flags[2] | flags[3])
    def _():
        for i, row in enumerate(near):
            h_ref[:, 16 * i : 16 * i + 16] = ea_ref[:, row : row + 16, :]
        physics([(h_ref, 0, 64)], w_ref, v_ref)
        for i, row in enumerate(near):

            @pl.when(flags[i])
            def _():
                ea_ref[:, row : row + 16, :] = h_ref[:, 16 * i : 16 * i + 16]

    sub = iota((8, CELLS), 0)
    for b in range(NB):
        for row in (16, 24, 32):
            a_ref[b, row : row + 8, :] = ea_ref[b, row : row + 8, :]
        a_ref[b, 40:48, :] = jnp.where(sub < 4, ea_ref[b, 40:48, :], a_ref[b, 40:48, :])
        back = OFF + OWN - HALO - (8 + 2 * HALO)
        row = OFF + OWN - 16
        a_ref[b, row : row + 8, :] = jnp.where(
            sub >= 4, ea_ref[b, row - back : row - back + 8, :], a_ref[b, row : row + 8, :]
        )
        for row in (OFF + OWN - 8, OFF + OWN, OFF + OWN + 8):
            a_ref[b, row : row + 8, :] = ea_ref[b, row - back : row - back + 8, :]
    transport(a_ref, b_ref, cx_ref, dx_ref, OFF - 16, OWN // 8 + 4, 66)
    flat = n_ref.reshape(TILES, PLEV * 8, CELLS)
    copies = []
    for group in (range(0, 4), range(4, 7), range(7, 8)):
        for t in group:
            own = pl.ds(OFF + CELLS * t, CELLS)
            for pair, block in zip(BLOCKS, flip_all([a_ref[b, own, :] for b in range(NB)])):
                for h, f in enumerate(pair):
                    for g in range(PLEV // 8):
                        flat[t, pl.ds(64 * g + f, 8, stride=8), :] = block[
                            HALF * h + 8 * g : HALF * h + 8 * g + 8
                        ]
        for t in group:
            copies += fetch(
                [(n_ref.at[t, pl.ds(0, LEVELS)], out_ref.at[:, pl.ds(8 * t, 8), :])],
                xsem.at[pl.ds(t, 1)],
            )
    for copy in copies:
        copy.wait()


VM = pl.BlockSpec(memory_space=pltpu.VMEM)
HBM = pl.BlockSpec(memory_space=pltpu.HBM)
ANY = pl.BlockSpec(memory_space=pl.ANY)
SMALL = [
    pltpu.VMEM((PLEV * TILES, CELLS), F32),
    pltpu.SMEM((CYCLES, 4), jnp.int32),
    pltpu.SMEM((CYCLES,), jnp.int32),
]
LIMIT = 40 << 20
STATE = (NB, XROWS, CELLS)
COLUMN = (XROWS, CELLS)
ENDS = (HALO * (NB + 1) + 8, CELLS)
BATCH = pltpu.VMEM((NB, 4 * CELLS, CELLS), F32)
NATURAL = pltpu.VMEM((TILES, PLEV, 8, CELLS), F32)


def local(state, courant, level_mix, field_mix, send_list, send_count):
    shape = jax.ShapeDtypeStruct
    hbm = lambda v: pltpu.with_memory_space_constraint(v, pltpu.HBM)
    x = state.reshape(FIELDS, LEVELS, TILES, CELLS).transpose(1, 2, 0, 3)
    x = hbm(x.reshape(LEVELS, TILES * FIELDS, CELLS))
    c = hbm(courant.reshape(LEVELS * TILES, CELLS))
    chosen, count = hbm(send_list.reshape(CYCLES, 4)), hbm(send_count.reshape(CYCLES))
    a, cx, dx, w, first, last, near, far = pl.pallas_call(
        column_kernel,
        name="column",
        out_shape=(
            shape(STATE, F32), shape(COLUMN, F32), shape(COLUMN, F32),
            shape((2 * WIDE, WIDE), BF16), *(shape(ENDS, F32),) * 4,
        ),
        in_specs=[HBM] * 6,
        out_specs=(VM,) * 8,
        scratch_shapes=[
            NATURAL,
            BATCH,
            pltpu.VMEM((CELLS, CELLS), F32),
            SMALL[0],
            pltpu.VMEM((LEVELS, LEVELS), F32),
            pltpu.SMEM((FIELDS, FIELDS), F32),
            *SMALL[1:],
            pltpu.SemaphoreType.DMA((5,)),
            pltpu.SemaphoreType.DMA((TILES,)),
        ],
        compiler_params=pltpu.CompilerParams(vmem_limit_bytes=LIMIT),
    )(x, c, hbm(level_mix), hbm(field_mix), chosen, count)
    n = lax.axis_size("pos")
    near = lax.ppermute(near, "pos", [(i, i ^ 1) for i in range(n)])
    params = pltpu.CompilerParams(vmem_limit_bytes=LIMIT)
    cost = pl.CostEstimate(flops=4_000_000_000, bytes_accessed=8_000_000, transcendentals=0)
    ahead = pl.pallas_call(
        ahead_kernel,
        name="ahead",
        out_shape=(shape(STATE, F32), shape(ENDS, F32)),
        in_specs=[VM] * 4,
        out_specs=(VM, VM),
        input_output_aliases={0: 0, 1: 1},
        scratch_shapes=[pltpu.VMEM(STATE, F32)],
        compiler_params=params,
        cost_estimate=cost,
    )
    a, far = ahead(a, far, cx, dx)
    far = lax.ppermute(far, "pos", [(i, (i + (1 if i % 2 else -1)) % n) for i in range(n)])
    mid = pl.pallas_call(
        inside_kernel,
        name="inside",
        out_shape=shape(STATE, F32),
        in_specs=[VM] * 4 + [HBM] * 2,
        out_specs=VM,
        input_output_aliases={0: 0},
        scratch_shapes=[
            pltpu.VMEM(STATE, F32), BATCH, *SMALL[1:], pltpu.SemaphoreType.DMA((2,))
        ],
        compiler_params=params,
        cost_estimate=cost,
    )(a, cx, dx, w, chosen, count)
    out, *_ = pl.pallas_call(
        finish_kernel,
        name="finish",
        out_shape=(
            shape((LEVELS, TILES * FIELDS, CELLS), F32),
            shape(STATE, F32), shape(COLUMN, F32), shape(COLUMN, F32),
        ),
        in_specs=[VM] * 8,
        out_specs=(ANY, VM, VM, VM),
        input_output_aliases={0: 1, 1: 2, 2: 3},
        scratch_shapes=[
            pltpu.VMEM(ENDS, F32),
            pltpu.VMEM(ENDS, F32),
            pltpu.VMEM(STATE, F32),
            pltpu.VMEM((NB, EROWS, CELLS), F32),
            pltpu.VMEM((NB, EROWS, CELLS), F32),
            pltpu.VMEM((NB, 64, CELLS), F32),
            pltpu.VMEM((NB, 64, CELLS), F32),
            pltpu.VMEM((EROWS, CELLS), F32),
            pltpu.VMEM((EROWS, CELLS), F32),
            NATURAL,
            pltpu.SemaphoreType.DMA((TILES,)),
        ],
        compiler_params=pltpu.CompilerParams(vmem_limit_bytes=LIMIT),
    )(mid, cx, dx, w, first, last, near, far)
    out = out.reshape(LEVELS, TILES, FIELDS, CELLS).transpose(2, 0, 1, 3)
    return out.reshape(1, FIELDS, LEVELS, TILES * CELLS)


def solution(mesh):
    in_specs = (
        P("chan", None, None, "pos"),
        P("chan", None, "pos"),
        P(),
        P(),
        P(None, "chan", "pos", None),
        P(None, "chan", "pos"),
    )
    out_specs = P("chan", None, None, "pos")
    return jax.shard_map(local, mesh=mesh, in_specs=in_specs, out_specs=out_specs, check_vma=False)
```

```python
import jax
import jax.numpy as jnp
from jax import lax
from jax.experimental import pallas as pl
from jax.experimental.pallas import tpu as pltpu
from jax.sharding import PartitionSpec as P


LEVELS = 50
FIELDS = 8
CELLS = 128
SECTIONS = 12
SWEEPS = 4
CYCLES = 2
TILES = 8
BUOYANCY = 0.4
F32 = jnp.float32
BF16 = jnp.bfloat16

BLOCKS = ((2, 0), (1, 3), (4, 6), (5, 7))
HALF = 64
HALO = CYCLES * SECTIONS
OFF = HALO + 8
OWN = TILES * CELLS
XROWS = OFF + OWN + HALO + 8
EROWS = 8 + 4 * HALO + 8
NB = len(BLOCKS)
WIDE = NB * CELLS
PLEV = 56


def iota(shape, dim):
    return lax.broadcasted_iota(jnp.int32, shape, dim)


def fetch(pairs, sem):
    copies = [pltpu.make_async_copy(a, b, sem.at[i]) for i, (a, b) in enumerate(pairs)]
    for copy in copies:
        copy.start()
    return copies


def strips(ref, index, row):
    take = [ref[(*index, pl.ds(64 * g + row, 8, stride=8), slice(None))] for g in range(PLEV // 8)]
    return take + [jnp.zeros((8, CELLS), F32)]


def build_weights(lm_ref, fm_ref, q_ref, w_ref):
    q_ref[...] = jnp.zeros((CELLS, CELLS), F32)
    lm = lm_ref[...]
    q_ref[:LEVELS, :LEVELS] = lm
    q_ref[HALF : HALF + LEVELS, :LEVELS] = lm
    q_ref[...] = q_ref[...].T
    lane = iota((16, CELLS), 1)
    sub = iota((16, CELLS), 0)
    low = lane < HALF
    eyes = [(lane % HALF == sub + r) & (sub + r < LEVELS) for r in range(0, HALF, 16)]
    for kb, pair_k in enumerate(BLOCKS):
        for kh, g in enumerate(pair_k):
            for nb, (fa, fb) in enumerate(BLOCKS):
                mix = jnp.where(low, fm_ref[fa, g], fm_ref[fb, g])
                for i, eye in enumerate(eyes):
                    row = CELLS * kb + HALF * kh + 16 * i
                    w = jnp.where(eye, mix, 0.0)
                    if g in (fa, fb):
                        lt = q_ref[16 * i : 16 * i + 16, :]
                        w = w + (jnp.where(low, lt, 0.0) if g == fa else jnp.where(low, 0.0, lt))
                    hi = w.astype(BF16)
                    cols = slice(CELLS * nb, CELLS * (nb + 1))
                    w_ref[row : row + 16, cols] = hi
                    w_ref[WIDE + row : WIDE + row + 16, cols] = (w - hi.astype(F32)).astype(BF16)


def physics(parts, w_ref, v_ref):
    starts = [sum(rows for _, _, rows in parts[:i]) for i in range(len(parts))]
    total = sum(rows for _, _, rows in parts)
    high = w_ref[:WIDE, :]
    rhs = jnp.concatenate([high, high, w_ref[WIDE:, :]], axis=0)

    def block(sweep_index, b):
        if sweep_index > 0:
            return v_ref[b, :total]
        return jnp.concatenate([ref[b, pl.ds(row, rows), :] for ref, row, rows in parts], axis=0)

    for sweep_index in range(SWEEPS):
        highs, lows = [], []
        for b in range(NB):
            t = jnp.tanh(block(sweep_index, b))
            hi = t.astype(BF16)
            highs.append(hi)
            lows.append((t - hi.astype(F32)).astype(BF16))
        lhs = jnp.concatenate(highs + lows + highs, axis=1)
        acc = jnp.dot(lhs, rhs, preferred_element_type=F32)
        for b in range(NB):
            new = block(sweep_index, b) + acc[:, CELLS * b : CELLS * (b + 1)]
            if sweep_index < SWEEPS - 1:
                v_ref[b, :total] = new
            else:
                for at, (ref, row, rows) in zip(starts, parts):
                    ref[b, pl.ds(row, rows), :] = new[at : at + rows]


def listed_physics(ref, cycle, list_ref, count_ref, w_ref, v_ref):
    for count in range(1, 5):

        @pl.when(count_ref[cycle] == count)
        def _():
            rows = [pl.multiple_of(OFF + CELLS * list_ref[cycle, k], 8) for k in range(count)]
            physics([(ref, row, CELLS) for row in rows], w_ref, v_ref)


def section(src, dst, c_ref, d_ref, kv, base, groups):
    for i in range(groups):
        row = base + 8 * i
        here, before, after = pl.ds(row, 8), pl.ds(row - 1, 8), pl.ds(row + 1, 8)
        d, cm, cp = d_ref[here, :], c_ref[before, :], c_ref[after, :]
        x = []
        for b in range(NB):
            side, coef = (before, cm) if b % 2 == 0 else (after, cp)
            x.append(d * src[b, here, :] + coef * src[b, side, :])
        x[1] = x[1] + kv * x[0]
        x[0] = x[0] - kv * x[1]
        for b in range(NB):
            dst[b, here, :] = x[b]


def transport(a_ref, b_ref, c_ref, d_ref, base, groups, unroll, first=0, last=SECTIONS // 2):
    kv = jnp.where(iota((8, CELLS), 1) < HALF, BUOYANCY, 0.0)

    def sweep(src, dst):
        def body(i, carry):
            row = pl.multiple_of(base + i * (8 * unroll), 8)
            section(src, dst, c_ref, d_ref, kv, row, unroll)
            return carry

        if groups == unroll:
            section(src, dst, c_ref, d_ref, kv, base, groups)
        else:
            lax.fori_loop(0, groups // unroll, body, 0)

    def two(_, carry):
        sweep(a_ref, b_ref)
        sweep(b_ref, a_ref)
        return carry

    lax.fori_loop(first, last, two, 0)


def put_courant(c_ref, d_ref, row, block):
    c = jnp.concatenate(block + block, axis=0).T
    c_ref[pl.ds(row, CELLS), :] = c
    d_ref[pl.ds(row, CELLS), :] = 1.0 - c


def tile_block(ref, index, pair):
    return jnp.concatenate(strips(ref, index, pair[0]) + strips(ref, index, pair[1]), axis=0)


def mxu_flip(x, y):
    eye = (iota((CELLS, 2 * CELLS), 0) == iota((CELLS, 2 * CELLS), 1) % CELLS).astype(F32).astype(BF16)
    both = jnp.concatenate([x, y], axis=0)
    hi = both.astype(BF16)
    lo = (both - hi.astype(F32)).astype(BF16)
    out = lax.dot_general(
        eye,
        jnp.concatenate([hi, lo], axis=1),
        (((1,), (1,)), ((), ())),
        preferred_element_type=F32,
    )
    return out[:, :CELLS], out[:, CELLS:]


def flip_all(blocks):
    return (blocks[0].T, blocks[1].T, *mxu_flip(blocks[2], blocks[3]))


def column_kernel(
    x_ref, c_hbm, lm_hbm, fm_hbm, list_hbm, count_hbm,
    a_ref, cx_ref, dx_ref, w_ref, first_ref, last_ref, near_ref, far_ref,
    n_ref, v_ref, q_ref, c_ref, lm_ref, fm_ref, list_ref, count_ref, sem, xsem,
):
    lm_copy, fm_copy, c_copy, list_copy, count_copy = fetch(
        (
            (lm_hbm, lm_ref), (fm_hbm, fm_ref), (c_hbm, c_ref.at[pl.ds(0, LEVELS * TILES)]),
            (list_hbm, list_ref), (count_hbm, count_ref),
        ),
        sem,
    )
    tiles = fetch(
        [
            (x_ref.at[:, pl.ds(8 * t, 8), :], n_ref.at[t, pl.ds(0, LEVELS)])
            for t in range(TILES)
        ],
        xsem,
    )
    c_ref[LEVELS * TILES :, :] = jnp.zeros((48, CELLS), F32)
    n_ref[:, LEVELS:] = jnp.zeros((TILES, PLEV - LEVELS, 8, CELLS), F32)
    lm_copy.wait()
    fm_copy.wait()
    build_weights(lm_ref, fm_ref, q_ref, w_ref)
    for copy in (c_copy, list_copy, count_copy, *tiles):
        copy.wait()
    for t in range(TILES):
        put_courant(cx_ref, dx_ref, OFF + CELLS * t, strips(c_ref, (), t))
    flat = n_ref.reshape(TILES, PLEV * 8, CELLS)
    for t in range(TILES):
        for b, block in enumerate(flip_all([tile_block(flat, (t,), pair) for pair in BLOCKS])):
            a_ref[b, pl.ds(OFF + CELLS * t, CELLS), :] = block
    listed_physics(a_ref, 0, list_ref, count_ref, w_ref, v_ref)
    for ref, row, t in ((first_ref, OFF, 0), (last_ref, OFF + OWN - HALO, TILES - 1)):
        for b in range(NB):
            ref[HALO * b : HALO * (b + 1), :] = a_ref[b, row : row + HALO, :]
        ref[HALO * NB : HALO * (NB + 1), :] = cx_ref[row : row + HALO, :]
        hit = jnp.int32(0)
        for slot in range(4):
            named = (slot < count_ref[1]) & (list_ref[1, slot] == t)
            hit = jnp.where(named, jnp.int32(1), hit)
        ref[HALO * (NB + 1) :, :] = jnp.broadcast_to(hit.astype(F32), (8, CELLS))
    odd = lax.axis_index("pos") % 2 == 1

    @pl.when(odd)
    def _():
        near_ref[...] = first_ref[...]
        far_ref[...] = last_ref[...]

    @pl.when(jnp.logical_not(odd))
    def _():
        near_ref[...] = last_ref[...]
        far_ref[...] = first_ref[...]


AHEAD = 3


def is_early():
    return lax.axis_index("pos") % (lax.axis_size("pos") // 2) == 0


def ahead_kernel(a_in, far_in, cx_ref, dx_ref, a_ref, far_ref, b_ref):
    @pl.when(is_early())
    def _():
        transport(a_ref, b_ref, cx_ref, dx_ref, OFF, OWN // 8, OWN // 8, 0, AHEAD)


def inside_kernel(
    a_in, cx_ref, dx_ref, w_ref, list_hbm, count_hbm,
    a_ref,
    b_ref, v_ref, list_ref, count_ref, sem,
):
    copies = fetch(((list_hbm, list_ref), (count_hbm, count_ref)), sem)
    first = jnp.where(is_early(), AHEAD, 0)
    transport(a_ref, b_ref, cx_ref, dx_ref, OFF, OWN // 8, OWN // 8, first)
    for copy in copies:
        copy.wait()
    listed_physics(a_ref, 1, list_ref, count_ref, w_ref, v_ref)


def finish_kernel(
    a_in, cx_in, dx_in, w_ref, first_ref, last_ref, near_ref, far_ref,
    out_ref, a_ref, cx_ref, dx_ref,
    left_ref, right_ref, b_ref, ea_ref, eb_ref, h_ref, v_ref, ec_ref, ed_ref, n_ref, xsem,
):
    odd = lax.axis_index("pos") % 2 == 1

    @pl.when(odd)
    def _():
        left_ref[...] = near_ref[...]
        right_ref[...] = far_ref[...]

    @pl.when(jnp.logical_not(odd))
    def _():
        left_ref[...] = far_ref[...]
        right_ref[...] = near_ref[...]

    parts = (left_ref, first_ref, last_ref, right_ref)
    for i, ref in enumerate(parts):
        rows = slice(8 + HALO * i, 8 + HALO * (i + 1))
        for b in range(NB):
            ea_ref[b, rows, :] = ref[HALO * b : HALO * (b + 1), :]
        c = ref[HALO * NB : HALO * (NB + 1), :]
        ec_ref[rows, :] = c
        ed_ref[rows, :] = 1.0 - c
    for ref, row in ((left_ref, OFF - HALO), (right_ref, OFF + OWN)):
        c = ref[HALO * NB : HALO * (NB + 1), :]
        cx_ref[row : row + HALO, :] = c
        dx_ref[row : row + HALO, :] = 1.0 - c
    flags = [jnp.max(ref[HALO * (NB + 1) :, :]) > 0.5 for ref in parts]
    transport(ea_ref, eb_ref, ec_ref, ed_ref, 8, 4 * HALO // 8, 4 * HALO // 8)
    near = [8 + HALO - 16, 8 + HALO, 8 + 3 * HALO - 16, 8 + 3 * HALO]

    @pl.when(flags[0] | flags[1] | flags[2] | flags[3])
    def _():
        for i, row in enumerate(near):
            h_ref[:, 16 * i : 16 * i + 16] = ea_ref[:, row : row + 16, :]
        physics([(h_ref, 0, 64)], w_ref, v_ref)
        for i, row in enumerate(near):

            @pl.when(flags[i])
            def _():
                ea_ref[:, row : row + 16, :] = h_ref[:, 16 * i : 16 * i + 16]

    sub = iota((8, CELLS), 0)
    for b in range(NB):
        for row in (16, 24, 32):
            a_ref[b, row : row + 8, :] = ea_ref[b, row : row + 8, :]
        a_ref[b, 40:48, :] = jnp.where(sub < 4, ea_ref[b, 40:48, :], a_ref[b, 40:48, :])
        back = OFF + OWN - HALO - (8 + 2 * HALO)
        row = OFF + OWN - 16
        a_ref[b, row : row + 8, :] = jnp.where(
            sub >= 4, ea_ref[b, row - back : row - back + 8, :], a_ref[b, row : row + 8, :]
        )
        for row in (OFF + OWN - 8, OFF + OWN, OFF + OWN + 8):
            a_ref[b, row : row + 8, :] = ea_ref[b, row - back : row - back + 8, :]
    transport(a_ref, b_ref, cx_ref, dx_ref, OFF - 16, OWN // 8 + 4, OWN // 8 + 4)
    flat = n_ref.reshape(TILES, PLEV * 8, CELLS)
    copies = []
    for group in (range(0, 4), range(4, 7), range(7, 8)):
        for t in group:
            own = pl.ds(OFF + CELLS * t, CELLS)
            for pair, block in zip(BLOCKS, flip_all([a_ref[b, own, :] for b in range(NB)])):
                for h, f in enumerate(pair):
                    for g in range(PLEV // 8):
                        flat[t, pl.ds(64 * g + f, 8, stride=8), :] = block[
                            HALF * h + 8 * g : HALF * h + 8 * g + 8
                        ]
        for t in group:
            copies += fetch(
                [(n_ref.at[t, pl.ds(0, LEVELS)], out_ref.at[:, pl.ds(8 * t, 8), :])],
                xsem.at[pl.ds(t, 1)],
            )
    for copy in copies:
        copy.wait()


VM = pl.BlockSpec(memory_space=pltpu.VMEM)
HBM = pl.BlockSpec(memory_space=pltpu.HBM)
ANY = pl.BlockSpec(memory_space=pl.ANY)
SMALL = [
    pltpu.VMEM((PLEV * TILES, CELLS), F32),
    pltpu.SMEM((CYCLES, 4), jnp.int32),
    pltpu.SMEM((CYCLES,), jnp.int32),
]
LIMIT = 40 << 20
STATE = (NB, XROWS, CELLS)
COLUMN = (XROWS, CELLS)
ENDS = (HALO * (NB + 1) + 8, CELLS)
BATCH = pltpu.VMEM((NB, 4 * CELLS, CELLS), F32)
NATURAL = pltpu.VMEM((TILES, PLEV, 8, CELLS), F32)


def local(state, courant, level_mix, field_mix, send_list, send_count):
    shape = jax.ShapeDtypeStruct
    hbm = lambda v: pltpu.with_memory_space_constraint(v, pltpu.HBM)
    x = state.reshape(FIELDS, LEVELS, TILES, CELLS).transpose(1, 2, 0, 3)
    x = hbm(x.reshape(LEVELS, TILES * FIELDS, CELLS))
    c = hbm(courant.reshape(LEVELS * TILES, CELLS))
    chosen, count = hbm(send_list.reshape(CYCLES, 4)), hbm(send_count.reshape(CYCLES))
    a, cx, dx, w, first, last, near, far = pl.pallas_call(
        column_kernel,
        name="column",
        out_shape=(
            shape(STATE, F32), shape(COLUMN, F32), shape(COLUMN, F32),
            shape((2 * WIDE, WIDE), BF16), *(shape(ENDS, F32),) * 4,
        ),
        in_specs=[HBM] * 6,
        out_specs=(VM,) * 8,
        scratch_shapes=[
            NATURAL,
            BATCH,
            pltpu.VMEM((CELLS, CELLS), F32),
            SMALL[0],
            pltpu.VMEM((LEVELS, LEVELS), F32),
            pltpu.SMEM((FIELDS, FIELDS), F32),
            *SMALL[1:],
            pltpu.SemaphoreType.DMA((5,)),
            pltpu.SemaphoreType.DMA((TILES,)),
        ],
        compiler_params=pltpu.CompilerParams(vmem_limit_bytes=LIMIT),
    )(x, c, hbm(level_mix), hbm(field_mix), chosen, count)
    n = lax.axis_size("pos")
    near = lax.ppermute(near, "pos", [(i, i ^ 1) for i in range(n)])
    params = pltpu.CompilerParams(vmem_limit_bytes=LIMIT)
    cost = pl.CostEstimate(flops=4_000_000_000, bytes_accessed=8_000_000, transcendentals=0)
    ahead = pl.pallas_call(
        ahead_kernel,
        name="ahead",
        out_shape=(shape(STATE, F32), shape(ENDS, F32)),
        in_specs=[VM] * 4,
        out_specs=(VM, VM),
        input_output_aliases={0: 0, 1: 1},
        scratch_shapes=[pltpu.VMEM(STATE, F32)],
        compiler_params=params,
        cost_estimate=cost,
    )
    a, far = ahead(a, far, cx, dx)
    far = lax.ppermute(far, "pos", [(i, (i + (1 if i % 2 else -1)) % n) for i in range(n)])
    mid = pl.pallas_call(
        inside_kernel,
        name="inside",
        out_shape=shape(STATE, F32),
        in_specs=[VM] * 4 + [HBM] * 2,
        out_specs=VM,
        input_output_aliases={0: 0},
        scratch_shapes=[
            pltpu.VMEM(STATE, F32), BATCH, *SMALL[1:], pltpu.SemaphoreType.DMA((2,))
        ],
        compiler_params=params,
        cost_estimate=cost,
    )(a, cx, dx, w, chosen, count)
    out, *_ = pl.pallas_call(
        finish_kernel,
        name="finish",
        out_shape=(
            shape((LEVELS, TILES * FIELDS, CELLS), F32),
            shape(STATE, F32), shape(COLUMN, F32), shape(COLUMN, F32),
        ),
        in_specs=[VM] * 8,
        out_specs=(ANY, VM, VM, VM),
        input_output_aliases={0: 1, 1: 2, 2: 3},
        scratch_shapes=[
            pltpu.VMEM(ENDS, F32),
            pltpu.VMEM(ENDS, F32),
            pltpu.VMEM(STATE, F32),
            pltpu.VMEM((NB, EROWS, CELLS), F32),
            pltpu.VMEM((NB, EROWS, CELLS), F32),
            pltpu.VMEM((NB, 64, CELLS), F32),
            pltpu.VMEM((NB, 64, CELLS), F32),
            pltpu.VMEM((EROWS, CELLS), F32),
            pltpu.VMEM((EROWS, CELLS), F32),
            NATURAL,
            pltpu.SemaphoreType.DMA((TILES,)),
        ],
        compiler_params=pltpu.CompilerParams(vmem_limit_bytes=LIMIT),
    )(mid, cx, dx, w, first, last, near, far)
    out = out.reshape(LEVELS, TILES, FIELDS, CELLS).transpose(2, 0, 1, 3)
    return out.reshape(1, FIELDS, LEVELS, TILES * CELLS)


def solution(mesh):
    in_specs = (
        P("chan", None, None, "pos"),
        P("chan", None, "pos"),
        P(),
        P(),
        P(None, "chan", "pos", None),
        P(None, "chan", "pos"),
    )
    out_specs = P("chan", None, None, "pos")
    return jax.shard_map(local, mesh=mesh, in_specs=in_specs, out_specs=out_specs, check_vma=False)
```

```python
import jax
import jax.numpy as jnp
from jax import lax
from jax.experimental import pallas as pl
from jax.experimental.pallas import tpu as pltpu
from jax.sharding import PartitionSpec as P


LEVELS = 50
FIELDS = 8
CELLS = 128
SECTIONS = 12
SWEEPS = 4
CYCLES = 2
TILES = 8
BUOYANCY = 0.4
F32 = jnp.float32
BF16 = jnp.bfloat16

BLOCKS = ((2, 0), (1, 3), (4, 6), (5, 7))
HALF = 64
HALO = CYCLES * SECTIONS
OFF = HALO + 8
OWN = TILES * CELLS
XROWS = OFF + OWN + HALO + 8
EROWS = 8 + 4 * HALO + 8
NB = len(BLOCKS)
WIDE = NB * CELLS
PLEV = 56


def iota(shape, dim):
    return lax.broadcasted_iota(jnp.int32, shape, dim)


def fetch(pairs, sem):
    copies = [pltpu.make_async_copy(a, b, sem.at[i]) for i, (a, b) in enumerate(pairs)]
    for copy in copies:
        copy.start()
    return copies


def strips(ref, index, row):
    take = [ref[(*index, pl.ds(64 * g + row, 8, stride=8), slice(None))] for g in range(PLEV // 8)]
    return take + [jnp.zeros((8, CELLS), F32)]


def build_weights(lm_ref, fm_ref, q_ref, w_ref, level_ref, mix_ref):
    q_ref[...] = jnp.zeros((CELLS, CELLS), F32)
    lm = lm_ref[...]
    q_ref[:LEVELS, :LEVELS] = lm
    q_ref[HALF : HALF + LEVELS, :LEVELS] = lm
    q_ref[...] = q_ref[...].T
    lane = iota((16, CELLS), 1)
    sub = iota((16, CELLS), 0)
    low = lane < HALF
    eyes = [(lane % HALF == sub + r) & (sub + r < LEVELS) for r in range(0, HALF, 16)]
    for kb, pair_k in enumerate(BLOCKS):
        for kh, g in enumerate(pair_k):
            for nb, (fa, fb) in enumerate(BLOCKS):
                mix = jnp.where(low, fm_ref[fa, g], fm_ref[fb, g])
                for i, eye in enumerate(eyes):
                    row = CELLS * kb + HALF * kh + 16 * i
                    w = jnp.where(eye, mix, 0.0)
                    if g in (fa, fb):
                        lt = q_ref[16 * i : 16 * i + 16, :]
                        w = w + (jnp.where(low, lt, 0.0) if g == fa else jnp.where(low, 0.0, lt))
                    hi = w.astype(BF16)
                    cols = slice(CELLS * nb, CELLS * (nb + 1))
                    w_ref[row : row + 16, cols] = hi
                    w_ref[WIDE + row : WIDE + row + 16, cols] = (w - hi.astype(F32)).astype(BF16)


    for h in range(2):
        for i in range(len(eyes)):
            lt = q_ref[16 * i : 16 * i + 16, :]
            w = jnp.where(low, lt, 0.0) if h == 0 else jnp.where(low, 0.0, lt)
            hi = w.astype(BF16)
            row = HALF * h + 16 * i
            level_ref[row : row + 16, :] = hi
            level_ref[CELLS + row : CELLS + row + 16, :] = hi
            level_ref[2 * CELLS + row : 2 * CELLS + row + 16, :] = (w - hi.astype(F32)).astype(BF16)
    low = iota((8, CELLS), 1) < HALF
    for nb, (fa, fb) in enumerate(BLOCKS):
        for kb, (ga, gb) in enumerate(BLOCKS):
            mix_ref[2 * (NB * nb + kb)] = jnp.where(low, fm_ref[fa, ga], fm_ref[fb, gb])
            mix_ref[2 * (NB * nb + kb) + 1] = jnp.where(low, fm_ref[fa, gb], fm_ref[fb, ga])


def edge_physics(v_ref, level_ref, mix_ref):
    rows = v_ref.shape[1]
    for _ in range(SWEEPS):
        bent, parts = [], []
        for b in range(NB):
            t = jnp.tanh(v_ref[b])
            hi = t.astype(BF16)
            lo = (t - hi.astype(F32)).astype(BF16)
            bent.append((t, pltpu.roll(t, HALF, 1)))
            parts.append(jnp.concatenate([hi, lo, hi], axis=1))
        acc = jnp.dot(
            jnp.concatenate(parts, axis=0), level_ref[...], preferred_element_type=F32
        )
        for nb in range(NB):
            for r in range(0, rows, 8):
                terms = [
                    mix_ref[2 * (NB * nb + kb) + i] * bent[kb][i][r : r + 8]
                    for kb in range(NB)
                    for i in range(2)
                ]
                while len(terms) > 1:
                    terms = [x + y for x, y in zip(terms[::2], terms[1::2])]
                at = rows * nb + r
                v_ref[nb, r : r + 8, :] += terms[0] + acc[at : at + 8]


def physics(parts, w_ref, v_ref):
    starts = [sum(rows for _, _, rows in parts[:i]) for i in range(len(parts))]
    total = sum(rows for _, _, rows in parts)
    high = w_ref[:WIDE, :]
    rhs = jnp.concatenate([high, high, w_ref[WIDE:, :]], axis=0)

    def block(sweep_index, b):
        if sweep_index > 0:
            return v_ref[b, :total]
        return jnp.concatenate([ref[b, pl.ds(row, rows), :] for ref, row, rows in parts], axis=0)

    for sweep_index in range(SWEEPS):
        highs, lows = [], []
        for b in range(NB):
            t = jnp.tanh(block(sweep_index, b))
            hi = t.astype(BF16)
            highs.append(hi)
            lows.append((t - hi.astype(F32)).astype(BF16))
        lhs = jnp.concatenate(highs + lows + highs, axis=1)
        acc = jnp.dot(lhs, rhs, preferred_element_type=F32)
        for b in range(NB):
            new = block(sweep_index, b) + acc[:, CELLS * b : CELLS * (b + 1)]
            if sweep_index < SWEEPS - 1:
                v_ref[b, :total] = new
            else:
                for at, (ref, row, rows) in zip(starts, parts):
                    ref[b, pl.ds(row, rows), :] = new[at : at + rows]


def listed_physics(ref, cycle, list_ref, count_ref, w_ref, v_ref):
    for count in range(1, 5):

        @pl.when(count_ref[cycle] == count)
        def _():
            rows = [pl.multiple_of(OFF + CELLS * list_ref[cycle, k], 8) for k in range(count)]
            physics([(ref, row, CELLS) for row in rows], w_ref, v_ref)


def section(src, dst, c_ref, d_ref, kv, base, groups):
    for i in range(groups):
        row = base + 8 * i
        here, before, after = pl.ds(row, 8), pl.ds(row - 1, 8), pl.ds(row + 1, 8)
        d, cm, cp = d_ref[here, :], c_ref[before, :], c_ref[after, :]
        x = []
        for b in range(NB):
            side, coef = (before, cm) if b % 2 == 0 else (after, cp)
            x.append(d * src[b, here, :] + coef * src[b, side, :])
        x[1] = x[1] + kv * x[0]
        x[0] = x[0] - kv * x[1]
        for b in range(NB):
            dst[b, here, :] = x[b]


def transport(a_ref, b_ref, c_ref, d_ref, base, groups, unroll, first=0, last=SECTIONS // 2):
    kv = jnp.where(iota((8, CELLS), 1) < HALF, BUOYANCY, 0.0)

    def sweep(src, dst):
        def body(i, carry):
            row = pl.multiple_of(base + i * (8 * unroll), 8)
            section(src, dst, c_ref, d_ref, kv, row, unroll)
            return carry

        if groups == unroll:
            section(src, dst, c_ref, d_ref, kv, base, groups)
        else:
            lax.fori_loop(0, groups // unroll, body, 0)

    def two(_, carry):
        sweep(a_ref, b_ref)
        sweep(b_ref, a_ref)
        return carry

    lax.fori_loop(first, last, two, 0)


def put_courant(c_ref, d_ref, row, block):
    c = jnp.concatenate(block + block, axis=0).T
    c_ref[pl.ds(row, CELLS), :] = c
    d_ref[pl.ds(row, CELLS), :] = 1.0 - c


def tile_block(ref, index, pair):
    return jnp.concatenate(strips(ref, index, pair[0]) + strips(ref, index, pair[1]), axis=0)


def mxu_flip(x, y):
    eye = (iota((CELLS, 2 * CELLS), 0) == iota((CELLS, 2 * CELLS), 1) % CELLS).astype(F32).astype(BF16)
    both = jnp.concatenate([x, y], axis=0)
    hi = both.astype(BF16)
    lo = (both - hi.astype(F32)).astype(BF16)
    out = lax.dot_general(
        eye,
        jnp.concatenate([hi, lo], axis=1),
        (((1,), (1,)), ((), ())),
        preferred_element_type=F32,
    )
    return out[:, :CELLS], out[:, CELLS:]


def flip_all(blocks):
    return (blocks[0].T, blocks[1].T, *mxu_flip(blocks[2], blocks[3]))


def column_kernel(
    x_ref, c_hbm, lm_hbm, fm_hbm, list_hbm, count_hbm,
    a_ref, cx_ref, dx_ref, w_ref, first_ref, last_ref, near_ref, far_ref, level_ref, mix_ref,
    n_ref, v_ref, q_ref, c_ref, lm_ref, fm_ref, list_ref, count_ref, sem, xsem,
):
    lm_copy, fm_copy, c_copy, list_copy, count_copy = fetch(
        (
            (lm_hbm, lm_ref), (fm_hbm, fm_ref), (c_hbm, c_ref.at[pl.ds(0, LEVELS * TILES)]),
            (list_hbm, list_ref), (count_hbm, count_ref),
        ),
        sem,
    )
    tiles = fetch(
        [
            (x_ref.at[:, pl.ds(8 * t, 8), :], n_ref.at[t, pl.ds(0, LEVELS)])
            for t in range(TILES)
        ],
        xsem,
    )
    c_ref[LEVELS * TILES :, :] = jnp.zeros((48, CELLS), F32)
    n_ref[:, LEVELS:] = jnp.zeros((TILES, PLEV - LEVELS, 8, CELLS), F32)
    lm_copy.wait()
    fm_copy.wait()
    build_weights(lm_ref, fm_ref, q_ref, w_ref, level_ref, mix_ref)
    for copy in (c_copy, list_copy, count_copy, *tiles):
        copy.wait()
    for t in range(TILES):
        put_courant(cx_ref, dx_ref, OFF + CELLS * t, strips(c_ref, (), t))
    flat = n_ref.reshape(TILES, PLEV * 8, CELLS)
    for t in range(TILES):
        for b, block in enumerate(flip_all([tile_block(flat, (t,), pair) for pair in BLOCKS])):
            a_ref[b, pl.ds(OFF + CELLS * t, CELLS), :] = block
    listed_physics(a_ref, 0, list_ref, count_ref, w_ref, v_ref)
    for ref, row, t in ((first_ref, OFF, 0), (last_ref, OFF + OWN - HALO, TILES - 1)):
        for b in range(NB):
            ref[HALO * b : HALO * (b + 1), :] = a_ref[b, row : row + HALO, :]
        ref[HALO * NB : HALO * (NB + 1), :] = cx_ref[row : row + HALO, :]
        hit = jnp.int32(0)
        for slot in range(4):
            named = (slot < count_ref[1]) & (list_ref[1, slot] == t)
            hit = jnp.where(named, jnp.int32(1), hit)
        ref[HALO * (NB + 1) :, :] = jnp.broadcast_to(hit.astype(F32), (8, CELLS))
    odd = lax.axis_index("pos") % 2 == 1

    @pl.when(odd)
    def _():
        near_ref[...] = first_ref[...]
        far_ref[...] = last_ref[...]

    @pl.when(jnp.logical_not(odd))
    def _():
        near_ref[...] = last_ref[...]
        far_ref[...] = first_ref[...]


AHEAD = 3


def is_early():
    return lax.axis_index("pos") % (lax.axis_size("pos") // 2) == 0


def ahead_kernel(a_in, far_in, cx_ref, dx_ref, a_ref, far_ref, b_ref):
    @pl.when(is_early())
    def _():
        transport(a_ref, b_ref, cx_ref, dx_ref, OFF, OWN // 8, OWN // 8, 0, AHEAD)


def inside_kernel(
    a_in, cx_ref, dx_ref, w_ref, list_hbm, count_hbm,
    a_ref,
    b_ref, v_ref, list_ref, count_ref, sem,
):
    copies = fetch(((list_hbm, list_ref), (count_hbm, count_ref)), sem)
    first = jnp.where(is_early(), AHEAD, 0)
    transport(a_ref, b_ref, cx_ref, dx_ref, OFF, OWN // 8, OWN // 8, first)
    for copy in copies:
        copy.wait()
    listed_physics(a_ref, 1, list_ref, count_ref, w_ref, v_ref)


def finish_kernel(
    a_in, cx_in, dx_in, level_ref, mix_ref, first_ref, last_ref, near_ref, far_ref,
    out_ref, a_ref, cx_ref, dx_ref,
    left_ref, right_ref, b_ref, ea_ref, eb_ref, h_ref, ec_ref, ed_ref, n_ref, xsem,
):
    odd = lax.axis_index("pos") % 2 == 1

    @pl.when(odd)
    def _():
        left_ref[...] = near_ref[...]
        right_ref[...] = far_ref[...]

    @pl.when(jnp.logical_not(odd))
    def _():
        left_ref[...] = far_ref[...]
        right_ref[...] = near_ref[...]

    parts = (left_ref, first_ref, last_ref, right_ref)
    for i, ref in enumerate(parts):
        rows = slice(8 + HALO * i, 8 + HALO * (i + 1))
        for b in range(NB):
            ea_ref[b, rows, :] = ref[HALO * b : HALO * (b + 1), :]
        c = ref[HALO * NB : HALO * (NB + 1), :]
        ec_ref[rows, :] = c
        ed_ref[rows, :] = 1.0 - c
    for ref, row in ((left_ref, OFF - HALO), (right_ref, OFF + OWN)):
        c = ref[HALO * NB : HALO * (NB + 1), :]
        cx_ref[row : row + HALO, :] = c
        dx_ref[row : row + HALO, :] = 1.0 - c
    flags = [jnp.max(ref[HALO * (NB + 1) :, :]) > 0.5 for ref in parts]
    transport(ea_ref, eb_ref, ec_ref, ed_ref, 8, 4 * HALO // 8, 4 * HALO // 8)
    near = [8 + HALO - 16, 8 + HALO, 8 + 3 * HALO - 16, 8 + 3 * HALO]

    @pl.when(flags[0] | flags[1] | flags[2] | flags[3])
    def _():
        for i, row in enumerate(near):
            h_ref[:, 16 * i : 16 * i + 16] = ea_ref[:, row : row + 16, :]
        edge_physics(h_ref, level_ref, mix_ref)
        for i, row in enumerate(near):

            @pl.when(flags[i])
            def _():
                ea_ref[:, row : row + 16, :] = h_ref[:, 16 * i : 16 * i + 16]

    sub = iota((8, CELLS), 0)
    for b in range(NB):
        for row in (16, 24, 32):
            a_ref[b, row : row + 8, :] = ea_ref[b, row : row + 8, :]
        a_ref[b, 40:48, :] = jnp.where(sub < 4, ea_ref[b, 40:48, :], a_ref[b, 40:48, :])
        back = OFF + OWN - HALO - (8 + 2 * HALO)
        row = OFF + OWN - 16
        a_ref[b, row : row + 8, :] = jnp.where(
            sub >= 4, ea_ref[b, row - back : row - back + 8, :], a_ref[b, row : row + 8, :]
        )
        for row in (OFF + OWN - 8, OFF + OWN, OFF + OWN + 8):
            a_ref[b, row : row + 8, :] = ea_ref[b, row - back : row - back + 8, :]
    transport(a_ref, b_ref, cx_ref, dx_ref, OFF - 16, OWN // 8 + 4, OWN // 8 + 4)
    flat = n_ref.reshape(TILES, PLEV * 8, CELLS)
    copies = []
    for group in (range(0, 4), range(4, 7), range(7, 8)):
        for t in group:
            own = pl.ds(OFF + CELLS * t, CELLS)
            for pair, block in zip(BLOCKS, flip_all([a_ref[b, own, :] for b in range(NB)])):
                for h, f in enumerate(pair):
                    for g in range(PLEV // 8):
                        flat[t, pl.ds(64 * g + f, 8, stride=8), :] = block[
                            HALF * h + 8 * g : HALF * h + 8 * g + 8
                        ]
        for t in group:
            copies += fetch(
                [(n_ref.at[t, pl.ds(0, LEVELS)], out_ref.at[:, pl.ds(8 * t, 8), :])],
                xsem.at[pl.ds(t, 1)],
            )
    for copy in copies:
        copy.wait()


VM = pl.BlockSpec(memory_space=pltpu.VMEM)
HBM = pl.BlockSpec(memory_space=pltpu.HBM)
ANY = pl.BlockSpec(memory_space=pl.ANY)
SMALL = [
    pltpu.VMEM((PLEV * TILES, CELLS), F32),
    pltpu.SMEM((CYCLES, 4), jnp.int32),
    pltpu.SMEM((CYCLES,), jnp.int32),
]
LIMIT = 40 << 20
STATE = (NB, XROWS, CELLS)
COLUMN = (XROWS, CELLS)
ENDS = (HALO * (NB + 1) + 8, CELLS)
BATCH = pltpu.VMEM((NB, 4 * CELLS, CELLS), F32)
NATURAL = pltpu.VMEM((TILES, PLEV, 8, CELLS), F32)


def local(state, courant, level_mix, field_mix, send_list, send_count):
    shape = jax.ShapeDtypeStruct
    hbm = lambda v: pltpu.with_memory_space_constraint(v, pltpu.HBM)
    x = state.reshape(FIELDS, LEVELS, TILES, CELLS).transpose(1, 2, 0, 3)
    x = hbm(x.reshape(LEVELS, TILES * FIELDS, CELLS))
    c = hbm(courant.reshape(LEVELS * TILES, CELLS))
    chosen, count = hbm(send_list.reshape(CYCLES, 4)), hbm(send_count.reshape(CYCLES))
    a, cx, dx, w, first, last, near, far, level, mix = pl.pallas_call(
        column_kernel,
        name="column",
        out_shape=(
            shape(STATE, F32), shape(COLUMN, F32), shape(COLUMN, F32),
            shape((2 * WIDE, WIDE), BF16), *(shape(ENDS, F32),) * 4,
            shape((3 * CELLS, CELLS), BF16), shape((2 * NB * NB, 8, CELLS), F32),
        ),
        in_specs=[HBM] * 6,
        out_specs=(VM,) * 10,
        scratch_shapes=[
            NATURAL,
            BATCH,
            pltpu.VMEM((CELLS, CELLS), F32),
            SMALL[0],
            pltpu.VMEM((LEVELS, LEVELS), F32),
            pltpu.SMEM((FIELDS, FIELDS), F32),
            *SMALL[1:],
            pltpu.SemaphoreType.DMA((5,)),
            pltpu.SemaphoreType.DMA((TILES,)),
        ],
        compiler_params=pltpu.CompilerParams(vmem_limit_bytes=LIMIT),
    )(x, c, hbm(level_mix), hbm(field_mix), chosen, count)
    n = lax.axis_size("pos")
    near = lax.ppermute(near, "pos", [(i, i ^ 1) for i in range(n)])
    params = pltpu.CompilerParams(vmem_limit_bytes=LIMIT)
    cost = pl.CostEstimate(flops=4_000_000_000, bytes_accessed=8_000_000, transcendentals=0)
    ahead = pl.pallas_call(
        ahead_kernel,
        name="ahead",
        out_shape=(shape(STATE, F32), shape(ENDS, F32)),
        in_specs=[VM] * 4,
        out_specs=(VM, VM),
        input_output_aliases={0: 0, 1: 1},
        scratch_shapes=[pltpu.VMEM(STATE, F32)],
        compiler_params=params,
        cost_estimate=cost,
    )
    a, far = ahead(a, far, cx, dx)
    far = lax.ppermute(far, "pos", [(i, (i + (1 if i % 2 else -1)) % n) for i in range(n)])
    mid = pl.pallas_call(
        inside_kernel,
        name="inside",
        out_shape=shape(STATE, F32),
        in_specs=[VM] * 4 + [HBM] * 2,
        out_specs=VM,
        input_output_aliases={0: 0},
        scratch_shapes=[
            pltpu.VMEM(STATE, F32), BATCH, *SMALL[1:], pltpu.SemaphoreType.DMA((2,))
        ],
        compiler_params=params,
        cost_estimate=cost,
    )(a, cx, dx, w, chosen, count)
    out, *_ = pl.pallas_call(
        finish_kernel,
        name="finish",
        out_shape=(
            shape((LEVELS, TILES * FIELDS, CELLS), F32),
            shape(STATE, F32), shape(COLUMN, F32), shape(COLUMN, F32),
        ),
        in_specs=[VM] * 9,
        out_specs=(ANY, VM, VM, VM),
        input_output_aliases={0: 1, 1: 2, 2: 3},
        scratch_shapes=[
            pltpu.VMEM(ENDS, F32),
            pltpu.VMEM(ENDS, F32),
            pltpu.VMEM(STATE, F32),
            pltpu.VMEM((NB, EROWS, CELLS), F32),
            pltpu.VMEM((NB, EROWS, CELLS), F32),
            pltpu.VMEM((NB, 64, CELLS), F32),
            pltpu.VMEM((EROWS, CELLS), F32),
            pltpu.VMEM((EROWS, CELLS), F32),
            NATURAL,
            pltpu.SemaphoreType.DMA((TILES,)),
        ],
        compiler_params=pltpu.CompilerParams(vmem_limit_bytes=LIMIT),
    )(mid, cx, dx, level, mix, first, last, near, far)
    out = out.reshape(LEVELS, TILES, FIELDS, CELLS).transpose(2, 0, 1, 3)
    return out.reshape(1, FIELDS, LEVELS, TILES * CELLS)


def solution(mesh):
    in_specs = (
        P("chan", None, None, "pos"),
        P("chan", None, "pos"),
        P(),
        P(),
        P(None, "chan", "pos", None),
        P(None, "chan", "pos"),
    )
    out_specs = P("chan", None, None, "pos")
    return jax.shard_map(local, mesh=mesh, in_specs=in_specs, out_specs=out_specs, check_vma=False)
```

```python
import jax
import jax.numpy as jnp
from jax import lax
from jax.experimental import pallas as pl
from jax.experimental.pallas import tpu as pltpu
from jax.sharding import PartitionSpec as P


LEVELS = 50
FIELDS = 8
CELLS = 128
SECTIONS = 12
SWEEPS = 4
CYCLES = 2
TILES = 8
BUOYANCY = 0.4
F32 = jnp.float32
BF16 = jnp.bfloat16

BLOCKS = ((2, 0), (1, 3), (4, 6), (5, 7))
HALF = 64
HALO = CYCLES * SECTIONS
OFF = HALO + 8
OWN = TILES * CELLS
XROWS = OFF + OWN + HALO + 8
EROWS = 8 + 4 * HALO + 8
NB = len(BLOCKS)
WIDE = NB * CELLS
PLEV = 56


def iota(shape, dim):
    return lax.broadcasted_iota(jnp.int32, shape, dim)


def fetch(pairs, sem):
    copies = [pltpu.make_async_copy(a, b, sem.at[i]) for i, (a, b) in enumerate(pairs)]
    for copy in copies:
        copy.start()
    return copies


def strips(ref, index, row):
    take = [ref[(*index, pl.ds(64 * g + row, 8, stride=8), slice(None))] for g in range(PLEV // 8)]
    return take + [jnp.zeros((8, CELLS), F32)]


def build_weights(lm_ref, fm_ref, q_ref, w_ref, level_ref, mix_ref):
    q_ref[...] = jnp.zeros((CELLS, CELLS), F32)
    lm = lm_ref[...]
    q_ref[:LEVELS, :LEVELS] = lm
    q_ref[HALF : HALF + LEVELS, :LEVELS] = lm
    q_ref[...] = q_ref[...].T
    lane = iota((16, CELLS), 1)
    sub = iota((16, CELLS), 0)
    low = lane < HALF
    eyes = [(lane % HALF == sub + r) & (sub + r < LEVELS) for r in range(0, HALF, 16)]
    for kb, pair_k in enumerate(BLOCKS):
        for kh, g in enumerate(pair_k):
            for nb, (fa, fb) in enumerate(BLOCKS):
                mix = jnp.where(low, fm_ref[fa, g], fm_ref[fb, g])
                for i, eye in enumerate(eyes):
                    row = CELLS * kb + HALF * kh + 16 * i
                    w = jnp.where(eye, mix, 0.0)
                    if g in (fa, fb):
                        lt = q_ref[16 * i : 16 * i + 16, :]
                        w = w + (jnp.where(low, lt, 0.0) if g == fa else jnp.where(low, 0.0, lt))
                    hi = w.astype(BF16)
                    cols = slice(CELLS * nb, CELLS * (nb + 1))
                    w_ref[row : row + 16, cols] = hi
                    w_ref[WIDE + row : WIDE + row + 16, cols] = (w - hi.astype(F32)).astype(BF16)


    for h in range(2):
        for i in range(len(eyes)):
            lt = q_ref[16 * i : 16 * i + 16, :]
            w = jnp.where(low, lt, 0.0) if h == 0 else jnp.where(low, 0.0, lt)
            hi = w.astype(BF16)
            row = HALF * h + 16 * i
            level_ref[row : row + 16, :] = hi
            level_ref[CELLS + row : CELLS + row + 16, :] = hi
            level_ref[2 * CELLS + row : 2 * CELLS + row + 16, :] = (w - hi.astype(F32)).astype(BF16)
    low = iota((8, CELLS), 1) < HALF
    for nb, (fa, fb) in enumerate(BLOCKS):
        for kb, (ga, gb) in enumerate(BLOCKS):
            mix_ref[2 * (NB * nb + kb)] = jnp.where(low, fm_ref[fa, ga], fm_ref[fb, gb])
            mix_ref[2 * (NB * nb + kb) + 1] = jnp.where(low, fm_ref[fa, gb], fm_ref[fb, ga])


def edge_physics(v_ref, level_ref, mix_ref):
    rows = v_ref.shape[1]
    for _ in range(SWEEPS):
        bent, parts = [], []
        for b in range(NB):
            t = jnp.tanh(v_ref[b])
            hi = t.astype(BF16)
            lo = (t - hi.astype(F32)).astype(BF16)
            bent.append((t, pltpu.roll(t, HALF, 1)))
            parts.append(jnp.concatenate([hi, lo, hi], axis=1))
        acc = jnp.dot(
            jnp.concatenate(parts, axis=0), level_ref[...], preferred_element_type=F32
        )
        for nb in range(NB):
            for r in range(0, rows, 8):
                terms = [
                    mix_ref[2 * (NB * nb + kb) + i] * bent[kb][i][r : r + 8]
                    for kb in range(NB)
                    for i in range(2)
                ]
                while len(terms) > 1:
                    terms = [x + y for x, y in zip(terms[::2], terms[1::2])]
                at = rows * nb + r
                v_ref[nb, r : r + 8, :] += terms[0] + acc[at : at + 8]


def physics(parts, w_ref, v_ref):
    starts = [sum(rows for _, _, rows in parts[:i]) for i in range(len(parts))]
    total = sum(rows for _, _, rows in parts)
    high = w_ref[:WIDE, :]
    rhs = jnp.concatenate([high, high, w_ref[WIDE:, :]], axis=0)

    def block(sweep_index, b):
        if sweep_index > 0:
            return v_ref[b, :total]
        return jnp.concatenate([ref[b, pl.ds(row, rows), :] for ref, row, rows in parts], axis=0)

    for sweep_index in range(SWEEPS):
        highs, lows = [], []
        for b in range(NB):
            t = jnp.tanh(block(sweep_index, b))
            hi = t.astype(BF16)
            highs.append(hi)
            lows.append((t - hi.astype(F32)).astype(BF16))
        lhs = jnp.concatenate(highs + lows + highs, axis=1)
        acc = jnp.dot(lhs, rhs, preferred_element_type=F32)
        for b in range(NB):
            new = block(sweep_index, b) + acc[:, CELLS * b : CELLS * (b + 1)]
            if sweep_index < SWEEPS - 1:
                v_ref[b, :total] = new
            else:
                for at, (ref, row, rows) in zip(starts, parts):
                    ref[b, pl.ds(row, rows), :] = new[at : at + rows]


def listed_physics(ref, cycle, list_ref, count_ref, w_ref, v_ref, counts=(1, 2, 3, 4)):
    for count in counts:

        @pl.when(count_ref[cycle] == count)
        def _():
            rows = [pl.multiple_of(OFF + CELLS * list_ref[cycle, k], 8) for k in range(count)]
            physics([(ref, row, CELLS) for row in rows], w_ref, v_ref)


def section(src, dst, c_ref, d_ref, kv, base, groups):
    for i in range(groups):
        row = base + 8 * i
        here, before, after = pl.ds(row, 8), pl.ds(row - 1, 8), pl.ds(row + 1, 8)
        d, cm, cp = d_ref[here, :], c_ref[before, :], c_ref[after, :]
        x = []
        for b in range(NB):
            side, coef = (before, cm) if b % 2 == 0 else (after, cp)
            x.append(d * src[b, here, :] + coef * src[b, side, :])
        x[1] = x[1] + kv * x[0]
        x[0] = x[0] - kv * x[1]
        for b in range(NB):
            dst[b, here, :] = x[b]


def transport(a_ref, b_ref, c_ref, d_ref, base, groups, unroll, first=0, last=SECTIONS // 2):
    kv = jnp.where(iota((8, CELLS), 1) < HALF, BUOYANCY, 0.0)

    def sweep(src, dst):
        def body(i, carry):
            row = pl.multiple_of(base + i * (8 * unroll), 8)
            section(src, dst, c_ref, d_ref, kv, row, unroll)
            return carry

        if groups == unroll:
            section(src, dst, c_ref, d_ref, kv, base, groups)
        else:
            lax.fori_loop(0, groups // unroll, body, 0)

    def two(_, carry):
        sweep(a_ref, b_ref)
        sweep(b_ref, a_ref)
        return carry

    lax.fori_loop(first, last, two, 0)


def put_courant(c_ref, d_ref, row, block):
    c = jnp.concatenate(block + block, axis=0).T
    c_ref[pl.ds(row, CELLS), :] = c
    d_ref[pl.ds(row, CELLS), :] = 1.0 - c


def tile_block(ref, index, pair):
    return jnp.concatenate(strips(ref, index, pair[0]) + strips(ref, index, pair[1]), axis=0)


def mxu_flip(x, y):
    eye = (iota((CELLS, 2 * CELLS), 0) == iota((CELLS, 2 * CELLS), 1) % CELLS).astype(F32).astype(BF16)
    both = jnp.concatenate([x, y], axis=0)
    hi = both.astype(BF16)
    lo = (both - hi.astype(F32)).astype(BF16)
    out = lax.dot_general(
        eye,
        jnp.concatenate([hi, lo], axis=1),
        (((1,), (1,)), ((), ())),
        preferred_element_type=F32,
    )
    return out[:, :CELLS], out[:, CELLS:]


def flip_all(blocks):
    return (blocks[0].T, blocks[1].T, *mxu_flip(blocks[2], blocks[3]))


def column_kernel(
    x_ref, c_hbm, lm_hbm, fm_hbm, list_hbm, count_hbm,
    a_ref, cx_ref, dx_ref, w_ref, first_ref, last_ref, near_ref, far_ref, level_ref, mix_ref,
    n_ref, v_ref, q_ref, c_ref, lm_ref, fm_ref, list_ref, count_ref, sem, xsem,
):
    lm_copy, fm_copy, c_copy, list_copy, count_copy = fetch(
        (
            (lm_hbm, lm_ref), (fm_hbm, fm_ref), (c_hbm, c_ref.at[pl.ds(0, LEVELS * TILES)]),
            (list_hbm, list_ref), (count_hbm, count_ref),
        ),
        sem,
    )
    tiles = fetch(
        [
            (x_ref.at[:, pl.ds(8 * t, 8), :], n_ref.at[t, pl.ds(0, LEVELS)])
            for t in range(TILES)
        ],
        xsem,
    )
    c_ref[LEVELS * TILES :, :] = jnp.zeros((48, CELLS), F32)
    n_ref[:, LEVELS:] = jnp.zeros((TILES, PLEV - LEVELS, 8, CELLS), F32)
    lm_copy.wait()
    fm_copy.wait()
    build_weights(lm_ref, fm_ref, q_ref, w_ref, level_ref, mix_ref)
    for copy in (c_copy, list_copy, count_copy, *tiles):
        copy.wait()
    for t in range(TILES):
        put_courant(cx_ref, dx_ref, OFF + CELLS * t, strips(c_ref, (), t))
    flat = n_ref.reshape(TILES, PLEV * 8, CELLS)
    for t in range(TILES):
        for b, block in enumerate(flip_all([tile_block(flat, (t,), pair) for pair in BLOCKS])):
            a_ref[b, pl.ds(OFF + CELLS * t, CELLS), :] = block
    listed_physics(a_ref, 0, list_ref, count_ref, w_ref, v_ref)
    for ref, row, t in ((first_ref, OFF, 0), (last_ref, OFF + OWN - HALO, TILES - 1)):
        for b in range(NB):
            ref[HALO * b : HALO * (b + 1), :] = a_ref[b, row : row + HALO, :]
        ref[HALO * NB : HALO * (NB + 1), :] = cx_ref[row : row + HALO, :]
        hit = jnp.int32(0)
        for slot in range(4):
            named = (slot < count_ref[1]) & (list_ref[1, slot] == t)
            hit = jnp.where(named, jnp.int32(1), hit)
        ref[HALO * (NB + 1) :, :] = jnp.broadcast_to(hit.astype(F32), (8, CELLS))
    odd = lax.axis_index("pos") % 2 == 1

    @pl.when(odd)
    def _():
        near_ref[...] = first_ref[...]
        far_ref[...] = last_ref[...]

    @pl.when(jnp.logical_not(odd))
    def _():
        near_ref[...] = last_ref[...]
        far_ref[...] = first_ref[...]


AHEAD = 3


def is_early():
    return lax.axis_index("pos") % (lax.axis_size("pos") // 2) == 0


def ahead_kernel(a_in, far_in, cx_ref, dx_ref, a_ref, far_ref, b_ref):
    @pl.when(is_early())
    def _():
        transport(a_ref, b_ref, cx_ref, dx_ref, OFF, OWN // 8, OWN // 8, 0, AHEAD)


def inside_kernel(
    a_in, cx_ref, dx_ref, w_ref, list_hbm, count_hbm,
    a_ref, info_ref,
    b_ref, v_ref, list_ref, count_ref, sem,
):
    copies = fetch(((list_hbm, list_ref), (count_hbm, count_ref)), sem)
    first = jnp.where(is_early(), AHEAD, 0)
    transport(a_ref, b_ref, cx_ref, dx_ref, OFF, OWN // 8, OWN // 8, first)
    for copy in copies:
        copy.wait()
    listed_physics(a_ref, 1, list_ref, count_ref, w_ref, v_ref, (1, 2, 3))
    for k in range(4):
        row = (OFF + CELLS * list_ref[1, k]).astype(F32)
        info_ref[k : k + 1, :] = jnp.broadcast_to(row, (1, CELLS))
    info_ref[4:5, :] = jnp.broadcast_to(count_ref[1].astype(F32), (1, CELLS))


def four_kernel(a_in, w_ref, info_ref, a_ref, v_ref):
    @pl.when(jnp.max(info_ref[4:5, :]) > 3.5)
    def _():
        rows = [
            pl.multiple_of(jnp.max(info_ref[k : k + 1, :]).astype(jnp.int32), 8) for k in range(4)
        ]
        physics([(a_ref, row, CELLS) for row in rows], w_ref, v_ref)


def finish_kernel(
    a_in, cx_in, dx_in, level_ref, mix_ref, first_ref, last_ref, near_ref, far_ref,
    out_ref, a_ref, cx_ref, dx_ref,
    left_ref, right_ref, b_ref, ea_ref, eb_ref, h_ref, ec_ref, ed_ref, n_ref, xsem,
):
    odd = lax.axis_index("pos") % 2 == 1

    @pl.when(odd)
    def _():
        left_ref[...] = near_ref[...]
        right_ref[...] = far_ref[...]

    @pl.when(jnp.logical_not(odd))
    def _():
        left_ref[...] = far_ref[...]
        right_ref[...] = near_ref[...]

    parts = (left_ref, first_ref, last_ref, right_ref)
    for i, ref in enumerate(parts):
        rows = slice(8 + HALO * i, 8 + HALO * (i + 1))
        for b in range(NB):
            ea_ref[b, rows, :] = ref[HALO * b : HALO * (b + 1), :]
        c = ref[HALO * NB : HALO * (NB + 1), :]
        ec_ref[rows, :] = c
        ed_ref[rows, :] = 1.0 - c
    for ref, row in ((left_ref, OFF - HALO), (right_ref, OFF + OWN)):
        c = ref[HALO * NB : HALO * (NB + 1), :]
        cx_ref[row : row + HALO, :] = c
        dx_ref[row : row + HALO, :] = 1.0 - c
    flags = [jnp.max(ref[HALO * (NB + 1) :, :]) > 0.5 for ref in parts]
    transport(ea_ref, eb_ref, ec_ref, ed_ref, 8, 4 * HALO // 8, 4 * HALO // 8)
    near = [8 + HALO - 16, 8 + HALO, 8 + 3 * HALO - 16, 8 + 3 * HALO]

    @pl.when(flags[0] | flags[1] | flags[2] | flags[3])
    def _():
        for i, row in enumerate(near):
            h_ref[:, 16 * i : 16 * i + 16] = ea_ref[:, row : row + 16, :]
        edge_physics(h_ref, level_ref, mix_ref)
        for i, row in enumerate(near):

            @pl.when(flags[i])
            def _():
                ea_ref[:, row : row + 16, :] = h_ref[:, 16 * i : 16 * i + 16]

    sub = iota((8, CELLS), 0)
    for b in range(NB):
        for row in (16, 24, 32):
            a_ref[b, row : row + 8, :] = ea_ref[b, row : row + 8, :]
        a_ref[b, 40:48, :] = jnp.where(sub < 4, ea_ref[b, 40:48, :], a_ref[b, 40:48, :])
        back = OFF + OWN - HALO - (8 + 2 * HALO)
        row = OFF + OWN - 16
        a_ref[b, row : row + 8, :] = jnp.where(
            sub >= 4, ea_ref[b, row - back : row - back + 8, :], a_ref[b, row : row + 8, :]
        )
        for row in (OFF + OWN - 8, OFF + OWN, OFF + OWN + 8):
            a_ref[b, row : row + 8, :] = ea_ref[b, row - back : row - back + 8, :]
    transport(a_ref, b_ref, cx_ref, dx_ref, OFF - 16, OWN // 8 + 4, OWN // 8 + 4)
    flat = n_ref.reshape(TILES, PLEV * 8, CELLS)
    copies = []
    for group in (range(0, 4), range(4, 7), range(7, 8)):
        for t in group:
            own = pl.ds(OFF + CELLS * t, CELLS)
            for pair, block in zip(BLOCKS, flip_all([a_ref[b, own, :] for b in range(NB)])):
                for h, f in enumerate(pair):
                    for g in range(PLEV // 8):
                        flat[t, pl.ds(64 * g + f, 8, stride=8), :] = block[
                            HALF * h + 8 * g : HALF * h + 8 * g + 8
                        ]
        for t in group:
            copies += fetch(
                [(n_ref.at[t, pl.ds(0, LEVELS)], out_ref.at[:, pl.ds(8 * t, 8), :])],
                xsem.at[pl.ds(t, 1)],
            )
    for copy in copies:
        copy.wait()


VM = pl.BlockSpec(memory_space=pltpu.VMEM)
HBM = pl.BlockSpec(memory_space=pltpu.HBM)
ANY = pl.BlockSpec(memory_space=pl.ANY)
SMALL = [
    pltpu.VMEM((PLEV * TILES, CELLS), F32),
    pltpu.SMEM((CYCLES, 4), jnp.int32),
    pltpu.SMEM((CYCLES,), jnp.int32),
]
LIMIT = 40 << 20
STATE = (NB, XROWS, CELLS)
COLUMN = (XROWS, CELLS)
ENDS = (HALO * (NB + 1) + 8, CELLS)
BATCH = pltpu.VMEM((NB, 4 * CELLS, CELLS), F32)
NATURAL = pltpu.VMEM((TILES, PLEV, 8, CELLS), F32)


def local(state, courant, level_mix, field_mix, send_list, send_count):
    shape = jax.ShapeDtypeStruct
    hbm = lambda v: pltpu.with_memory_space_constraint(v, pltpu.HBM)
    x = state.reshape(FIELDS, LEVELS, TILES, CELLS).transpose(1, 2, 0, 3)
    x = hbm(x.reshape(LEVELS, TILES * FIELDS, CELLS))
    c = hbm(courant.reshape(LEVELS * TILES, CELLS))
    chosen, count = hbm(send_list.reshape(CYCLES, 4)), hbm(send_count.reshape(CYCLES))
    a, cx, dx, w, first, last, near, far, level, mix = pl.pallas_call(
        column_kernel,
        name="column",
        out_shape=(
            shape(STATE, F32), shape(COLUMN, F32), shape(COLUMN, F32),
            shape((2 * WIDE, WIDE), BF16), *(shape(ENDS, F32),) * 4,
            shape((3 * CELLS, CELLS), BF16), shape((2 * NB * NB, 8, CELLS), F32),
        ),
        in_specs=[HBM] * 6,
        out_specs=(VM,) * 10,
        scratch_shapes=[
            NATURAL,
            BATCH,
            pltpu.VMEM((CELLS, CELLS), F32),
            SMALL[0],
            pltpu.VMEM((LEVELS, LEVELS), F32),
            pltpu.SMEM((FIELDS, FIELDS), F32),
            *SMALL[1:],
            pltpu.SemaphoreType.DMA((5,)),
            pltpu.SemaphoreType.DMA((TILES,)),
        ],
        compiler_params=pltpu.CompilerParams(vmem_limit_bytes=LIMIT),
    )(x, c, hbm(level_mix), hbm(field_mix), chosen, count)
    n = lax.axis_size("pos")
    near = lax.ppermute(near, "pos", [(i, i ^ 1) for i in range(n)])
    params = pltpu.CompilerParams(vmem_limit_bytes=LIMIT)
    cost = pl.CostEstimate(flops=4_000_000_000, bytes_accessed=8_000_000, transcendentals=0)
    ahead = pl.pallas_call(
        ahead_kernel,
        name="ahead",
        out_shape=(shape(STATE, F32), shape(ENDS, F32)),
        in_specs=[VM] * 4,
        out_specs=(VM, VM),
        input_output_aliases={0: 0, 1: 1},
        scratch_shapes=[pltpu.VMEM(STATE, F32)],
        compiler_params=params,
        cost_estimate=cost,
    )
    a, far = ahead(a, far, cx, dx)
    far = lax.ppermute(far, "pos", [(i, (i + (1 if i % 2 else -1)) % n) for i in range(n)])
    mid, info = pl.pallas_call(
        inside_kernel,
        name="inside",
        out_shape=(shape(STATE, F32), shape((8, CELLS), F32)),
        in_specs=[VM] * 4 + [HBM] * 2,
        out_specs=(VM, VM),
        input_output_aliases={0: 0},
        scratch_shapes=[
            pltpu.VMEM(STATE, F32), BATCH, *SMALL[1:], pltpu.SemaphoreType.DMA((2,))
        ],
        compiler_params=params,
        cost_estimate=cost,
    )(a, cx, dx, w, chosen, count)
    mid = pl.pallas_call(
        four_kernel,
        name="four",
        out_shape=shape(STATE, F32),
        in_specs=[VM] * 3,
        out_specs=VM,
        input_output_aliases={0: 0},
        scratch_shapes=[BATCH],
        compiler_params=pltpu.CompilerParams(vmem_limit_bytes=LIMIT),
        cost_estimate=cost,
    )(mid, w, info)
    out, *_ = pl.pallas_call(
        finish_kernel,
        name="finish",
        out_shape=(
            shape((LEVELS, TILES * FIELDS, CELLS), F32),
            shape(STATE, F32), shape(COLUMN, F32), shape(COLUMN, F32),
        ),
        in_specs=[VM] * 9,
        out_specs=(ANY, VM, VM, VM),
        input_output_aliases={0: 1, 1: 2, 2: 3},
        scratch_shapes=[
            pltpu.VMEM(ENDS, F32),
            pltpu.VMEM(ENDS, F32),
            pltpu.VMEM(STATE, F32),
            pltpu.VMEM((NB, EROWS, CELLS), F32),
            pltpu.VMEM((NB, EROWS, CELLS), F32),
            pltpu.VMEM((NB, 64, CELLS), F32),
            pltpu.VMEM((EROWS, CELLS), F32),
            pltpu.VMEM((EROWS, CELLS), F32),
            NATURAL,
            pltpu.SemaphoreType.DMA((TILES,)),
        ],
        compiler_params=pltpu.CompilerParams(vmem_limit_bytes=LIMIT),
    )(mid, cx, dx, level, mix, first, last, near, far)
    out = out.reshape(LEVELS, TILES, FIELDS, CELLS).transpose(2, 0, 1, 3)
    return out.reshape(1, FIELDS, LEVELS, TILES * CELLS)


def solution(mesh):
    in_specs = (
        P("chan", None, None, "pos"),
        P("chan", None, "pos"),
        P(),
        P(),
        P(None, "chan", "pos", None),
        P(None, "chan", "pos"),
    )
    out_specs = P("chan", None, None, "pos")
    return jax.shard_map(local, mesh=mesh, in_specs=in_specs, out_specs=out_specs, check_vma=False)
```
